512 devices in a mesh: test: 8 (over z_lo, core), bx: 4 (over y), by: 16 (over z_hi, x).
Axes of the slice: x: 4, y: 4, z: 16 (z_hi: 4, z_lo: 4; z = z_hi * 4 + z_lo), core: 2. Of those that a mesh axis runs over, the one named last changes fastest.
Arguments:
- log_conductivity: float32 [32, 128, 256], P('bx', 'by'), may hold values from -3 to 3
- storage: float32 [32, 128, 256], P('bx', 'by'), may hold values from 0.5 to 2
- recharge: float32 [32, 128, 256], P('bx', 'by'), may hold values from -6 to 6
- pump_rate: float32 [32], P('test'), may hold values from 4 to 16
- pump_well: int32 [32], P('test'), may hold values from 0 to 2047
- observed: float32 [32, 2048], P('test'), may hold values from -9 to 9
- owner: int32 [2048], replicated, may hold values from 0 to 63, as said below
- screen_column: int32 [2048], replicated, may hold values from 0 to 63
- screen_top: int32 [2048], replicated, may hold values from 0 to 248
Outputs:
- gradient: float32 [32, 128, 256], P('bx', 'by', 'test')
The draws below stay inside these ranges and needn't reach their ends.
Inputs may be any that keep to these rules, and one draw needn't show every extreme that they name: `owner`: each brick owns exactly 32 wells.
All inputs are finite; a program needn't handle non-finite values.
Results may differ from the reference program's by a relative error of at most 0.0001.
Values sent between devices are 32-bit elements; how exact they have to be, the bound alone decides.
A program may use at most 64 MiB of HBM per device.

```python
import math
import jax
import jax.numpy as jnp
from jax import lax

CX = 8
CY = 8
NZ = 256
SWEEPS = 3
SCREEN = 8
NX = 32
NY = 128
TESTS = 32
BRICKS = 64
WELLS = 2048
N_BY = 16


def owner_table(key):
    return (jax.random.permutation(jax.random.fold_in(key, 3), WELLS) % BRICKS).astype(jnp.int32)


def draw_owner(key, part):
    return owner_table(key)


def draw_observed(key, part):
    ramp = 1.0 + 2.0 * owner_table(key).astype(jnp.float32) / max(BRICKS - 1, 1)
    noise_key = jax.random.fold_in(key, 11)
    values = jnp.clip(jax.random.normal(noise_key, (TESTS, WELLS), jnp.float32), -3.0, 3.0)
    return values * ramp[None, :]


def set_ends(values, key, least, high):
    longest = values.shape.index(max(values.shape))
    spots = []
    for shift in (0, 1):
        where = [jax.random.randint(jax.random.fold_in(key, axis), (), 0, length) for axis, length in enumerate(values.shape)]
        where[longest] = (where[longest] + shift) % values.shape[longest]
        spots.append(tuple(where))
    return values.at[spots[0]].set(least).at[spots[1]].set(high)


def block_levels(rng, dims, cuts, smallest, largest):
    level = 1.0
    for dim, shards_of in cuts:
        steps = jax.random.uniform(jax.random.fold_in(jax.random.fold_in(rng, 6), dim), (shards_of,), jnp.float32, smallest / len(cuts), largest / len(cuts))
        level = level * jnp.repeat(jnp.exp(steps), dims[dim] // shards_of).reshape((-1,) + (1,) * (len(dims) - 1 - dim))
    return level


def noise(stream_key, shape, deviation, bound, cuts=(), held_as=jnp.bfloat16):
    result = jax.random.normal(stream_key, shape, jnp.float32) * deviation
    if len(cuts) > 0:
        result = block_levels(stream_key, shape, cuts, -0.22, 0.18) * result
    return jnp.clip(result, min=-bound, max=bound).astype(held_as)


def setup_inputs(seed: int = 0) -> dict:
    seeds = jax.random.split(jax.random.key(seed), 10)
    return {
        "log_conductivity": noise(seeds[0], (NX, NY, NZ), 0.7, 3.0, ((0, 4), (1, 16)), jnp.float32),
        "storage": jnp.clip(jnp.exp(math.log(2.0) - 1.3862944 * jax.random.uniform(seeds[1], (NX, NY, NZ), jnp.float32) ** block_levels(seeds[1], (NX, NY, NZ), ((0, 4), (1, 16)), -0.2, 0.2)), 0.5, 2.0),
        "recharge": noise(seeds[2], (NX, NY, NZ), 1.0, 6.0, ((0, 4), (1, 16)), jnp.float32),
        "pump_rate": jnp.clip(jnp.exp(math.log(16.0) - 1.3862944 * jax.random.uniform(seeds[3], (TESTS,), jnp.float32) ** block_levels(seeds[3], (TESTS,), ((0, 8),), -0.2, 0.2)), 4.0, 16.0),
        "pump_well": set_ends(jax.random.randint(seeds[4], (TESTS,), 0, WELLS), jax.random.fold_in(seeds[4], 1), 0, WELLS - 1).astype(jnp.int32),
        "observed": draw_observed(jax.random.fold_in(seeds[9], 71), 0),
        "owner": draw_owner(jax.random.fold_in(seeds[9], 71), 0),
        "screen_column": set_ends(jax.random.randint(seeds[7], (WELLS,), 0, CX * CY), jax.random.fold_in(seeds[7], 1), 0, (CX * CY) - 1).astype(jnp.int32),
        "screen_top": set_ends(jax.random.randint(seeds[8], (WELLS,), 0, NZ - SCREEN + 1), jax.random.fold_in(seeds[8], 1), 0, NZ - SCREEN).astype(jnp.int32),
    }


epsilon = 1e-6


def pad_depth(values):
    return jnp.pad(values, [(0, 0)] * (values.ndim - 1) + [(1, 1)])


def neighbours(padded, centre):
    z_padded = pad_depth(centre)
    return [padded[..., 2:, 1:-1, :], padded[..., :-2, 1:-1, :],
            padded[..., 1:-1, 2:, :], padded[..., 1:-1, :-2, :],
            z_padded[..., 2:], z_padded[..., :-2]]


def weighted(conductance, others):
    accumulated = conductance[0] * others[0]
    for position in range(1, 6):
        accumulated = accumulated + conductance[position] * others[position]
    return accumulated


def sensitivity(conductance, heads_field, heads_padded, adjoint_field, adjoint_padded):
    near_heads = neighbours(heads_padded, heads_field)
    near_adjoint = neighbours(adjoint_padded, adjoint_field)
    accumulated = jnp.zeros_like(heads_field)
    for position in range(6):
        accumulated = accumulated + conductance[position] * (heads_field - near_heads[position]) * (adjoint_field - near_adjoint[position])
    return -0.5 * accumulated


def pad_plane(values):
    return jnp.pad(values, ((1, 1), (1, 1), (0, 0)))


def reference(log_conductivity, storage, recharge, pump_rate, pump_well, observed, owner, screen_column, screen_top):
    conductance = [jnp.exp(0.5 * (log_conductivity + other)) for other in neighbours(pad_plane(log_conductivity), log_conductivity)]
    diagonal = storage + weighted(conductance, [1.0] * 6)
    offsets = jnp.arange(SCREEN, dtype=jnp.int32)
    cell_z = screen_top[:, None] + offsets[None, :]
    cell_x = jnp.broadcast_to(((owner // N_BY) * CX + screen_column // CY)[:, None], cell_z.shape).astype(jnp.int32)
    cell_y = jnp.broadcast_to(((owner % N_BY) * CY + screen_column % CY)[:, None], cell_z.shape).astype(jnp.int32)

    def relax_field(source):
        iterate = source / diagonal
        for sweep_index in range(SWEEPS - 1):
            iterate = (source + weighted(conductance, neighbours(pad_plane(iterate), iterate))) / diagonal
        return iterate

    def one_test(running_sum, inputs):
        pump_value, well_index, observed_row = inputs
        source = recharge.at[cell_x[well_index], cell_y[well_index], cell_z[well_index]].add(-pump_value)
        heads_field = relax_field(source)
        well_heads = jnp.mean(heads_field[cell_x, cell_y, cell_z], axis=1)
        residual = well_heads - observed_row
        misfit = jnp.sum(residual * residual) / residual.shape[0] + epsilon
        values = jnp.broadcast_to((residual / misfit)[:, None], cell_z.shape)
        adjoint_source = jnp.zeros_like(heads_field).at[cell_x, cell_y, cell_z].add(values)
        adjoint_field = relax_field(adjoint_source)
        terms = sensitivity(conductance, heads_field, pad_plane(heads_field), adjoint_field, pad_plane(adjoint_field))
        return running_sum + terms, None

    running_sum, unused = lax.scan(one_test, jnp.zeros(log_conductivity.shape, jnp.float32), (pump_rate, pump_well, observed))
    return running_sum / TESTS
```

```python
import functools

import jax
import jax.numpy as jnp
from jax import lax
from jax.experimental import pallas as pl
from jax.experimental.pallas import tpu as pltpu
from jax.sharding import PartitionSpec as P

F32 = jnp.float32
MESH = pl.DeviceIdType.MESH
VMEM = pltpu.VMEM
SMEM = pltpu.SMEM
HIGHEST = lax.Precision.HIGHEST
EPSILON = 1e-06
SCREEN = 8
SIDE = 8
HALO = 4
EXT = SIDE + 2 * HALO
NX_BRICKS, NY_BRICKS = 4, 16
ROUND = 4
TESTS_AXIS = 8
WELLS = 2048
OWN = 32
DIRECTIONS = [(dx, dy) for dx in (-1, 0, 1) for dy in (-1, 0, 1)]
NEIGHBOURS = [(k, d) for k, d in enumerate(DIRECTIONS) if d != (0, 0)]


def iota(shape, dim):
    return lax.broadcasted_iota(jnp.int32, shape, dim)


def z_neighbours(values, fill):
    sub, lane = iota(values.shape, 1), iota(values.shape, 2)
    low = pltpu.roll(values, 1, 2)
    low = jnp.where(lane == 0, jnp.where(sub < 4, fill, pltpu.roll(low, 4, 1)), low)
    high = pltpu.roll(values, 127, 2)
    high = jnp.where(lane == 127, jnp.where(sub < 4, pltpu.roll(high, 4, 1), fill), high)
    return low, high


def around(ref, x, lo, hi, fill):
    low, high = z_neighbours(ref[x, lo:hi], fill)
    return (
        (ref[x - 1, lo:hi] + ref[x + 1, lo:hi])
        + (ref[x, lo - 1 : hi - 1] + ref[x, lo + 1 : hi + 1])
        + (low + high)
    )


def rows(lo, hi, body):
    def step(x, carry):
        body(x)
        return carry

    lax.fori_loop(lo, hi, step, 0)


def halves(ref, x, lo, hi, field):
    first = ref[x, lo:hi, 2 * field : 2 * field + 1, :]
    second = ref[x, lo:hi, 2 * field + 1 : 2 * field + 2, :]
    shape = (hi - lo, 8, 128)
    return jnp.where(
        iota(shape, 1) < 4, jnp.broadcast_to(first, shape), jnp.broadcast_to(second, shape)
    )


def inside(x, lo, hi):
    shape = (hi - lo, 8, 128)
    gx = lax.axis_index("bx") * SIDE + x - HALO + jnp.zeros(shape, jnp.int32)
    gy = lax.axis_index("by") * SIDE + lo - HALO + iota(shape, 0)
    return (gx >= 0) & (gx < NX_BRICKS * SIDE) & (gy >= 0) & (gy < NY_BRICKS * SIDE)


def neighbour(dx, dy):
    bx, by = lax.axis_index("bx"), lax.axis_index("by")
    return {
        "bx": lax.rem(bx + dx + NX_BRICKS, NX_BRICKS),
        "by": lax.rem(by + dy + NY_BRICKS, NY_BRICKS),
    }


def span(step, width):
    if step == 0:
        return 0, HALO, SIDE
    if step > 0:
        return SIDE - width, HALO - width, width
    return 0, HALO + SIDE, width


def greet(peers):
    barrier = pltpu.get_barrier_semaphore()
    for peer in peers:
        pl.semaphore_signal(barrier, inc=1, device_id=peer, device_id_type=MESH)
    pl.semaphore_wait(barrier, len(peers))


def exchange_kernel(packed, ext, send_sems, recv_sems):
    for cx in (0, HALO + SIDE):
        for cy in (0, HALO + SIDE):
            ext[cx : cx + HALO, cy : cy + HALO] = jnp.zeros((HALO, HALO, 8, 128), F32)
    greet([neighbour(dx, dy) for k, (dx, dy) in NEIGHBOURS])
    copies = []
    for k, (dx, dy) in NEIGHBOURS:
        width = HALO if dx == 0 or dy == 0 else HALO - 1
        from_x, to_x, count_x = span(dx, width)
        from_y, to_y, count_y = span(dy, width)
        copies.append(
            pltpu.make_async_remote_copy(
                src_ref=packed.at[pl.ds(from_x, count_x), pl.ds(from_y, count_y)],
                dst_ref=ext.at[pl.ds(to_x, count_x), pl.ds(to_y, count_y)],
                send_sem=send_sems.at[k],
                recv_sem=recv_sems.at[k],
                device_id=neighbour(dx, dy),
                device_id_type=MESH,
            )
        )
        copies[-1].start()
    ext[HALO : HALO + SIDE, HALO : HALO + SIDE] = packed[...]
    for copy in copies:
        copy.wait()


def coefficients(ext, e_ref, r_ref, alpha_ref, beta_ref, pump_cell, pump_tile):
    def roots(x):
        e_ref[x] = jnp.where(inside(x, 0, EXT), jnp.exp(0.5 * halves(ext, x, 0, EXT, 0)), 1.0)

    rows(0, EXT, roots)
    lo, hi = 1, EXT - 1

    def terms(x):
        e = e_ref[x, lo:hi]
        diagonal = halves(ext, x, lo, hi, 1) + e * around(e_ref, x, lo, hi, 1.0)
        r = jnp.where(inside(x, lo, hi), 1.0 / diagonal, 0.0)
        cell = x * EXT + lo + iota(e.shape, 0)
        source = halves(ext, x, lo, hi, 2) + jnp.where(pump_cell[None] == cell, pump_tile[None], 0.0)
        er = e * r
        r_ref[x, lo:hi] = r
        alpha_ref[x, lo:hi] = e * er
        beta_ref[x, lo:hi] = er * source

    rows(lo, hi, terms)


def sweeps(e_ref, alpha_ref, beta_ref, u_ref, out_ref):
    def second(x):
        u_ref[x, 2 : EXT - 2] = beta_ref[x, 2 : EXT - 2] + alpha_ref[x, 2 : EXT - 2] * around(
            beta_ref, x, 2, EXT - 2, 0.0
        )

    rows(2, EXT - 2, second)

    def third(x):
        u = beta_ref[x, 3 : EXT - 3] + alpha_ref[x, 3 : EXT - 3] * around(u_ref, x, 3, EXT - 3, 0.0)
        out_ref[x, 3 : EXT - 3] = u / e_ref[x, 3 : EXT - 3]

    rows(3, EXT - 3, third)


def pumping(pump_rate, pump_well, owner, column, top):
    sub, lane = iota((8, 128), 0), iota((8, 128), 1)
    z = lane + jnp.where(sub < 4, 0, 128)
    cell = jnp.zeros((8, 128), jnp.int32)
    tile = jnp.zeros((8, 128), F32)
    first_x = lax.axis_index("bx") * SIDE - HALO
    first_y = lax.axis_index("by") * SIDE - HALO
    for t in range(4):
        well = pump_well[t]
        brick, place, start = owner[well], column[well], top[well]
        x = (brick >> 4) * SIDE + (place >> 3) - first_x
        y = (brick & 15) * SIDE + (place & 7) - first_y
        ok = (x >= 0) & (x < EXT) & (y >= 0) & (y < EXT)
        mine = (sub & 3) == t
        cell = jnp.where(mine, jnp.where(ok, x * EXT + y, -1), cell)
        hit = mine & (z >= start) & (z < start + SCREEN)
        tile = jnp.where(hit, -pump_rate[t], tile)
    return cell, tile


def own_wells(owner, column, top, observed):
    brick = lax.axis_index("bx") * NY_BRICKS + lax.axis_index("by")
    mine = jnp.where(owner[...] == brick, 1.0, 0.0)
    upto = jnp.where(iota((128, 128), 0) <= iota((128, 128), 1), 1.0, 0.0)
    inner = jnp.dot(mine, upto, precision=HIGHEST, preferred_element_type=F32)
    count = jnp.broadcast_to(jnp.sum(mine, axis=1, keepdims=True), (16, 128))
    before = jnp.where(iota((16, 16), 1) < iota((16, 16), 0), 1.0, 0.0)
    rank = inner + jnp.dot(before, count, precision=HIGHEST, preferred_element_type=F32) - 1.0
    rank = jnp.where(mine > 0.0, rank, -1.0)
    place = iota((OWN, 128), 0).astype(F32)
    sums = [jnp.zeros((OWN, 128), F32) for field in range(6)]
    for k in range(16):
        hit = jnp.broadcast_to(rank[k : k + 1, :], (OWN, 128)) == place
        values = [column[k : k + 1, :].astype(F32), top[k : k + 1, :].astype(F32)]
        values += [observed[t : t + 1, k * 128 : (k + 1) * 128] for t in range(4)]
        for field in range(6):
            sums[field] = sums[field] + jnp.where(
                hit, jnp.broadcast_to(values[field], (OWN, 128)), 0.0
            )
    return [jnp.sum(s, axis=1, keepdims=True) for s in sums]


def residuals(heads_ref, wells, message, squares):
    column, top, observed = wells[0], wells[1], wells[2:]
    column2 = jnp.concatenate([column, column], axis=0)
    top2 = jnp.concatenate([top, top], axis=0)
    half = iota((2 * OWN, 128), 0) // OWN
    z = (iota((2 * OWN, 128), 1) + 128 * half).astype(F32)
    screen = jnp.where((z >= top2) & (z < top2 + SCREEN), 1.0, 0.0)
    heads = heads_ref[HALO : HALO + SIDE, HALO : HALO + SIDE].reshape(512, 128)
    sums = lax.dot_general(
        screen, heads, (((1,), (1,)), ((), ())), precision=HIGHEST, preferred_element_type=F32
    )
    at = iota((2 * OWN, 512), 1)
    keep = ((at >> 3).astype(F32) == column2) & (
        ((at >> 2) & 1) == iota((2 * OWN, 512), 0) // OWN
    )
    sums = jnp.where(keep, sums, 0.0)
    pick = jnp.where((iota((512, 128), 0) & 3) == iota((512, 128), 1), 1.0, 0.0)
    sums = jnp.dot(sums, pick, precision=HIGHEST, preferred_element_type=F32)
    sums = (sums[:OWN] + sums[OWN:]) * (1.0 / SCREEN)
    lane = iota((OWN, 128), 1)
    for t in range(4):
        sums = jnp.where(lane == t, sums - observed[t], sums)
    sums = jnp.where(lane == 4, column, sums)
    sums = jnp.where(lane == 5, top, sums)
    eye = jnp.where(iota((8, 128), 0) == iota((8, 128), 1), 1.0, 0.0)
    turned = lax.dot_general(
        eye, sums, (((1,), (1,)), ((), ())), precision=HIGHEST, preferred_element_type=F32
    )
    message[...] = jnp.concatenate([turned, jnp.zeros((8, 128 - OWN), F32)], axis=1)
    total = jnp.broadcast_to(jnp.sum(turned * turned, axis=1, keepdims=True), (8, 128))
    squares[...] = jnp.where(iota((8, 128), 0) < 4, total, pltpu.roll(total, 4, 0))


def heads_kernel(
    ext, owner, column, top, observed, owner_s, column_s, top_s, pump_rate, pump_well,
    e_ref, r_ref, alpha_ref, heads_ref, message, squares, beta_ref, u_ref,
):
    pump_cell, pump_tile = pumping(pump_rate, pump_well, owner_s, column_s, top_s)
    coefficients(ext, e_ref, r_ref, alpha_ref, beta_ref, pump_cell, pump_tile)
    sweeps(e_ref, alpha_ref, beta_ref, u_ref, heads_ref)
    residuals(heads_ref, own_wells(owner, column, top, observed), message, squares)


def residual_exchange_kernel(
    message, squares, messages, total, near, partial, far, msg_send, msg_recv, near_send, near_recv,
    far_send, far_recv,
):
    bx, by = lax.axis_index("bx"), lax.axis_index("by")
    turn, place = by // ROUND, lax.rem(by, ROUND)
    near_peers = [
        {
            "bx": lax.rem(bx + a, NX_BRICKS),
            "by": turn * ROUND + lax.rem(place + b, ROUND),
        }
        for a in range(NX_BRICKS) for b in range(ROUND) if a + b > 0
    ]
    far_count = NY_BRICKS // ROUND
    far_peers = [{"by": lax.rem(by + c * ROUND, NY_BRICKS)} for c in range(1, far_count)]
    greet([neighbour(dx, dy) for k, (dx, dy) in NEIGHBOURS] + near_peers + far_peers)
    copies = []

    def send(source, target, send_sem, recv_sem, peer):
        copy = pltpu.make_async_remote_copy(
            src_ref=source, dst_ref=target, send_sem=send_sem, recv_sem=recv_sem,
            device_id=peer, device_id_type=MESH,
        )
        copy.start()
        return copy

    near_copies = [
        send(squares, near.at[i], near_send.at[i], near_recv.at[i], peer)
        for i, peer in enumerate(near_peers)
    ]
    copies = [
        send(message, messages.at[8 - k], msg_send.at[k], msg_recv.at[k], neighbour(dx, dy))
        for k, (dx, dy) in NEIGHBOURS
    ]
    messages[4] = message[...]
    for copy in near_copies:
        copy.wait()
    here = squares[...]
    for i in range(len(near_peers)):
        here = here + near[i]
    partial[...] = here
    far_copies = [
        send(partial, far.at[i], far_send.at[i], far_recv.at[i], peer)
        for i, peer in enumerate(far_peers)
    ]
    for copy in far_copies + copies:
        copy.wait()
    for i in range(len(far_peers)):
        here = here + far[i]
    total[...] = here


def adjoint_source(messages, e_ref, r_ref, beta_ref, lhs):
    sub, lane = iota((8, 128), 0), iota((8, 128), 1)
    values = [jnp.zeros((8, 128), F32) for g in range(3)]
    cells = [jnp.zeros((8, 128), F32) for g in range(3)]
    tops = [jnp.zeros((8, 128), F32) for g in range(3)]
    for k, (dx, dy) in enumerate(DIRECTIONS):
        tile = messages[k]
        value = jnp.where(sub < 4, tile, pltpu.roll(tile, 4, 0))
        column = jnp.broadcast_to(tile[4:5], (8, 128))
        along = jnp.floor(column * (1.0 / SIDE))
        x = along + (HALO + SIDE * dx)
        y = column - along * SIDE + (HALO + SIDE * dy)
        ok = (x >= 1) & (x < EXT - 1) & (y >= 1) & (y < EXT - 1) & (lane < OWN)
        cell = jnp.where(ok, x * EXT + y, 0.0)
        top = jnp.where(lane < OWN, jnp.broadcast_to(tile[5:6], (8, 128)), 0.0)
        g, shift = k // 4, OWN * (k % 4)
        if shift:
            value, cell, top = [pltpu.roll(v, shift, 1) for v in (value, cell, top)]
        values[g], cells[g], tops[g] = values[g] + value, cells[g] + cell, tops[g] + top
    z = iota((256, 128), 0).astype(F32)
    screens = []
    for g in range(3):
        top = jnp.broadcast_to(tops[g][0:1], (256, 128))
        screens.append(jnp.where((z >= top) & (z < top + SCREEN), 1.0, 0.0))
    screen = jnp.concatenate(screens, axis=1)
    wide = EXT - 2
    shape = (wide, 8, 128)
    lo, hi = 1, EXT - 1

    def left(x):
        cell = (x * EXT + 1 + iota(shape, 0)).astype(F32)
        for g in range(3):
            lhs[x - 1, :, g * 128 : (g + 1) * 128] = jnp.where(
                cells[g][None] == cell, values[g][None], 0.0
            ).reshape(wide * 8, 128)

    rows(lo, hi, left)
    group = 7
    for first in range(0, wide, group):
        block = lhs[first : first + group].reshape(group * wide * 8, 384)
        both = lax.dot_general(
            block, screen, (((1,), (1,)), ((), ())), precision=HIGHEST, preferred_element_type=F32
        )
        pair = both.reshape(group, wide, 8, 256)
        for i in range(group):
            source = jnp.where(iota(shape, 1) < 4, pair[i, :, :, :128], pair[i, :, :, 128:])
            x = first + i + 1
            beta_ref[x, lo:hi] = e_ref[x, lo:hi] * r_ref[x, lo:hi] * source


def sensitivity(e_ref, heads_ref, adjoint_ref, scale, out_ref):
    lo, hi = HALO, HALO + SIDE

    def cell_terms(x):
        h, a = heads_ref[x, lo:hi], adjoint_ref[x, lo:hi]
        e = e_ref[x, lo:hi]
        total = jnp.zeros_like(h)
        for step_x, step_y in ((1, 0), (-1, 0), (0, 1), (0, -1)):
            at = (x + step_x, slice(lo + step_y, hi + step_y))
            total = total + e_ref[at] * (h - heads_ref[at]) * (a - adjoint_ref[at])
        for e_n, h_n, a_n in zip(
            z_neighbours(e, 1.0), z_neighbours(h, 0.0), z_neighbours(a, 0.0)
        ):
            total = total + e_n * (h - h_n) * (a - a_n)
        total = total * e * scale[None]
        total = total + pltpu.roll(total, 7, 1)
        out_ref[x - HALO] = total + pltpu.roll(total, 6, 1)

    rows(lo, hi, cell_terms)


def slabs(sum_ref, out):
    lane = iota((8, 128), 1)
    for half in range(2):
        planes = sum_ref[:, :, 4 * half, :]
        for q in range(4):
            for xq in range(2):
                packed = jnp.zeros((8, 128), F32)
                for xx in range(4):
                    plane = planes[4 * xq + xx]
                    shift = (32 * (xx - q)) % 128
                    if shift:
                        plane = pltpu.roll(plane, shift, 1)
                    packed = jnp.where((lane >> 5) == xx, plane, packed)
                out[4 * half + q, xq] = packed


def adjoint_kernel(
    e_ref, r_ref, alpha_ref, heads_ref, messages, total, out, beta_ref, u_ref, adjoint_ref, sum_ref, lhs
):
    adjoint_source(messages, e_ref, r_ref, beta_ref, lhs)
    sweeps(e_ref, alpha_ref, beta_ref, u_ref, adjoint_ref)
    scale = (-0.5 / (4 * TESTS_AXIS)) / (total[...] / WELLS + EPSILON)
    sensitivity(e_ref, heads_ref, adjoint_ref, scale, sum_ref)
    slabs(sum_ref, out)


def reduce_kernel(parts, out, slots, send_sems, recv_sems):
    me = lax.axis_index("test")
    peers = [lax.rem(me + d, TESTS_AXIS) for d in range(1, TESTS_AXIS)]
    greet([{"test": peer} for peer in peers])
    copies = []
    for i, peer in enumerate(peers):
        copies.append(
            pltpu.make_async_remote_copy(
                src_ref=parts.at[peer],
                dst_ref=slots.at[i],
                send_sem=send_sems.at[i],
                recv_sem=recv_sems.at[i],
                device_id={"test": peer},
                device_id_type=MESH,
            )
        )
        copies[-1].start()
    for copy in copies:
        copy.wait()
    total = parts[me]
    for i in range(TESTS_AXIS - 1):
        total = total + slots[i]
    for xq in range(2):
        for xx in range(4):
            plane = total[xq]
            if xx:
                plane = pltpu.roll(plane, 128 - 32 * xx, 1)
            out[4 * xq + xx] = plane[:, :32]


def call(kernel, inputs, outputs, scratch, *args, collective_id=None):
    remote = {} if collective_id is None else dict(collective_id=collective_id, has_side_effects=True)
    specs = [pl.BlockSpec(memory_space=space) for space in inputs]
    shapes = [jax.ShapeDtypeStruct(shape, F32) for shape in outputs]
    out_specs = [pl.BlockSpec(memory_space=VMEM) for shape in outputs]
    return pl.pallas_call(
        kernel,
        out_shape=shapes,
        in_specs=specs,
        out_specs=out_specs,
        scratch_shapes=scratch,
        compiler_params=pltpu.CompilerParams(vmem_limit_bytes=48 * 1024 * 1024, **remote),
    )(*args)


def local(
    log_conductivity, storage, recharge, pump_rate, pump_well, observed, owner, screen_column, screen_top
):
    dma = pltpu.SemaphoreType.DMA
    field = (EXT, EXT, 8, 128)
    tile = (8, 128)
    shape = (SIDE, SIDE, 2, 128)
    packed = jnp.concatenate(
        [log_conductivity.reshape(shape), storage.reshape(shape), recharge.reshape(shape),
         jnp.zeros(shape, F32)],
        axis=2,
    )
    (ext,) = call(
        exchange_kernel, [VMEM], [field], [dma((9,)), dma((9,))], packed, collective_id=0
    )
    table = [a.reshape(16, 128) for a in (owner, screen_column, screen_top)]
    e, r, alpha, heads, message, squares = call(
        heads_kernel, [VMEM] * 5 + [SMEM] * 5, [field] * 4 + [tile] * 2,
        [VMEM(field, F32), VMEM(field, F32)],
        ext, *table, observed, owner, screen_column, screen_top, pump_rate, pump_well,
    )
    near, far = NX_BRICKS * ROUND - 1, NY_BRICKS // ROUND - 1
    messages, total = call(
        residual_exchange_kernel, [VMEM] * 2, [(9,) + tile, tile],
        [VMEM((near,) + tile, F32), VMEM(tile, F32), VMEM((far,) + tile, F32),
         dma((9,)), dma((9,)), dma((near,)), dma((near,)), dma((far,)), dma((far,))],
        message, squares, collective_id=1,
    )
    (parts,) = call(
        adjoint_kernel, [VMEM] * 6, [(TESTS_AXIS, 2) + tile],
        [VMEM(field, F32), VMEM(field, F32), VMEM(field, F32), VMEM((SIDE, SIDE) + tile, F32),
         VMEM((EXT - 2, (EXT - 2) * 8, 384), F32)],
        e, r, alpha, heads, messages, total,
    )
    (gradient,) = call(
        reduce_kernel, [VMEM], [(SIDE, SIDE, 32)],
        [VMEM((TESTS_AXIS - 1, 2) + tile, F32), dma((TESTS_AXIS - 1,)), dma((TESTS_AXIS - 1,))],
        parts, collective_id=2,
    )
    return gradient


def solution(mesh):
    placed = (
        P("bx", "by", None), P("bx", "by", None), P("bx", "by", None), P("test"), P("test"),
        P("test", None), P(), P(), P(),
    )
    return jax.shard_map(
        local, mesh=mesh, in_specs=placed, out_specs=P("bx", "by", "test"), check_vma=False
    )
```

```python
import jax
import jax.numpy as jnp
from jax import lax
from jax.experimental import pallas as pl
from jax.experimental.pallas import tpu as pltpu
from jax.sharding import PartitionSpec as P

F32 = jnp.float32
MESH = pl.DeviceIdType.MESH
VMEM = pltpu.VMEM
SMEM = pltpu.SMEM
HIGHEST = lax.Precision.HIGHEST
EPSILON = 1e-06
SCREEN = 8
SIDE = 8
HALO = 4
EXT = SIDE + 2 * HALO
NX_BRICKS, NY_BRICKS = 4, 16
ROUND = 4
TESTS_AXIS = 8
WELLS = 2048
OWN = 32
DIRECTIONS = [(dx, dy) for dx in (-1, 0, 1) for dy in (-1, 0, 1)]
NEIGHBOURS = [(k, d) for k, d in enumerate(DIRECTIONS) if d != (0, 0)]


def iota(shape, dim):
    return lax.broadcasted_iota(jnp.int32, shape, dim)


def z_neighbours(values, fill):
    sub, lane = iota(values.shape, 1), iota(values.shape, 2)
    low = pltpu.roll(values, 1, 2)
    low = jnp.where(lane == 0, jnp.where(sub < 4, fill, pltpu.roll(low, 4, 1)), low)
    high = pltpu.roll(values, 127, 2)
    high = jnp.where(lane == 127, jnp.where(sub < 4, pltpu.roll(high, 4, 1), fill), high)
    return low, high


def around(ref, x, lo, hi, fill):
    low, high = z_neighbours(ref[x, lo:hi], fill)
    return (
        (ref[x - 1, lo:hi] + ref[x + 1, lo:hi])
        + (ref[x, lo - 1 : hi - 1] + ref[x, lo + 1 : hi + 1])
        + (low + high)
    )


def rows(lo, hi, body):
    def step(x, carry):
        body(x)
        return carry

    lax.fori_loop(lo, hi, step, 0)


def halves(ref, x, lo, hi, field):
    first = ref[x, lo:hi, 2 * field : 2 * field + 1, :]
    second = ref[x, lo:hi, 2 * field + 1 : 2 * field + 2, :]
    shape = (hi - lo, 8, 128)
    return jnp.where(
        iota(shape, 1) < 4, jnp.broadcast_to(first, shape), jnp.broadcast_to(second, shape)
    )


def inside(x, lo, hi):
    shape = (hi - lo, 8, 128)
    gx = lax.axis_index("bx") * SIDE + x - HALO + jnp.zeros(shape, jnp.int32)
    gy = lax.axis_index("by") * SIDE + lo - HALO + iota(shape, 0)
    return (gx >= 0) & (gx < NX_BRICKS * SIDE) & (gy >= 0) & (gy < NY_BRICKS * SIDE)


def neighbour(dx, dy):
    bx, by = lax.axis_index("bx"), lax.axis_index("by")
    return {
        "bx": lax.rem(bx + dx + NX_BRICKS, NX_BRICKS),
        "by": lax.rem(by + dy + NY_BRICKS, NY_BRICKS),
    }


def span(step, width):
    if step == 0:
        return 0, HALO, SIDE
    if step > 0:
        return SIDE - width, HALO - width, width
    return 0, HALO + SIDE, width


def remote(source, target, send_sem, recv_sem, peer):
    copy = pltpu.make_async_remote_copy(
        src_ref=source, dst_ref=target, send_sem=send_sem, recv_sem=recv_sem,
        device_id=peer, device_id_type=MESH,
    )
    copy.start()
    return copy


def start_halos(packed, ext, send_sems, recv_sems):
    copies = []
    for k, (dx, dy) in NEIGHBOURS:
        width = HALO if dx == 0 or dy == 0 else HALO - 1
        from_x, to_x, count_x = span(dx, width)
        from_y, to_y, count_y = span(dy, width)
        copies.append(
            remote(
                packed.at[pl.ds(from_x, count_x), pl.ds(from_y, count_y)],
                ext.at[pl.ds(to_x, count_x), pl.ds(to_y, count_y)],
                send_sems.at[k], recv_sems.at[k], neighbour(dx, dy),
            )
        )
    return copies


def coefficients(ext, e_ref, r_ref, alpha_ref, beta_ref, pump_cell, pump_tile):
    def roots(x):
        e_ref[x] = jnp.where(inside(x, 0, EXT), jnp.exp(0.5 * halves(ext, x, 0, EXT, 0)), 1.0)

    rows(0, EXT, roots)
    lo, hi = 1, EXT - 1

    def terms(x):
        e = e_ref[x, lo:hi]
        diagonal = halves(ext, x, lo, hi, 1) + e * around(e_ref, x, lo, hi, 1.0)
        r = jnp.where(inside(x, lo, hi), 1.0 / diagonal, 0.0)
        cell = x * EXT + lo + iota(e.shape, 0)
        source = halves(ext, x, lo, hi, 2) + jnp.where(pump_cell[None] == cell, pump_tile[None], 0.0)
        er = e * r
        r_ref[x, lo:hi] = r
        alpha_ref[x, lo:hi] = e * er
        beta_ref[x, lo:hi] = er * source

    rows(lo, hi, terms)


def sweeps(e_ref, alpha_ref, beta_ref, u_ref, out_ref):
    def second(x):
        u_ref[x, 2 : EXT - 2] = beta_ref[x, 2 : EXT - 2] + alpha_ref[x, 2 : EXT - 2] * around(
            beta_ref, x, 2, EXT - 2, 0.0
        )

    rows(2, EXT - 2, second)

    def third(x):
        u = beta_ref[x, 3 : EXT - 3] + alpha_ref[x, 3 : EXT - 3] * around(u_ref, x, 3, EXT - 3, 0.0)
        out_ref[x, 3 : EXT - 3] = u / e_ref[x, 3 : EXT - 3]

    rows(3, EXT - 3, third)


def pumping(pump_rate, pump_well, owner, column, top):
    sub, lane = iota((8, 128), 0), iota((8, 128), 1)
    z = lane + jnp.where(sub < 4, 0, 128)
    cell = jnp.zeros((8, 128), jnp.int32)
    tile = jnp.zeros((8, 128), F32)
    first_x = lax.axis_index("bx") * SIDE - HALO
    first_y = lax.axis_index("by") * SIDE - HALO
    for t in range(4):
        well = pump_well[t]
        brick, place, start = owner[well], column[well], top[well]
        x = (brick >> 4) * SIDE + (place >> 3) - first_x
        y = (brick & 15) * SIDE + (place & 7) - first_y
        ok = (x >= 0) & (x < EXT) & (y >= 0) & (y < EXT)
        mine = (sub & 3) == t
        cell = jnp.where(mine, jnp.where(ok, x * EXT + y, -1), cell)
        hit = mine & (z >= start) & (z < start + SCREEN)
        tile = jnp.where(hit, -pump_rate[t], tile)
    return cell, tile


def own_wells(owner, column, top, observed):
    brick = lax.axis_index("bx") * NY_BRICKS + lax.axis_index("by")
    mine = jnp.where(owner[...] == brick, 1.0, 0.0)
    upto = jnp.where(iota((128, 128), 0) <= iota((128, 128), 1), 1.0, 0.0)
    inner = jnp.dot(mine, upto, precision=HIGHEST, preferred_element_type=F32)
    count = jnp.broadcast_to(jnp.sum(mine, axis=1, keepdims=True), (16, 128))
    before = jnp.where(iota((16, 16), 1) < iota((16, 16), 0), 1.0, 0.0)
    rank = inner + jnp.dot(before, count, precision=HIGHEST, preferred_element_type=F32) - 1.0
    rank = jnp.where(mine > 0.0, rank, -1.0)
    place = iota((OWN, 128), 0).astype(F32)
    sums = [jnp.zeros((OWN, 128), F32) for field in range(6)]
    for k in range(16):
        hit = jnp.broadcast_to(rank[k : k + 1, :], (OWN, 128)) == place
        values = [column[k : k + 1, :].astype(F32), top[k : k + 1, :].astype(F32)]
        values += [observed[t : t + 1, k * 128 : (k + 1) * 128] for t in range(4)]
        for field in range(6):
            sums[field] = sums[field] + jnp.where(
                hit, jnp.broadcast_to(values[field], (OWN, 128)), 0.0
            )
    return [jnp.sum(s, axis=1, keepdims=True) for s in sums]


def residuals(heads_ref, wells, message, squares):
    column, top, observed = wells[0], wells[1], wells[2:]
    column2 = jnp.concatenate([column, column], axis=0)
    top2 = jnp.concatenate([top, top], axis=0)
    half = iota((2 * OWN, 128), 0) // OWN
    z = (iota((2 * OWN, 128), 1) + 128 * half).astype(F32)
    screen = jnp.where((z >= top2) & (z < top2 + SCREEN), 1.0, 0.0)
    heads = heads_ref[HALO : HALO + SIDE, HALO : HALO + SIDE].reshape(512, 128)
    sums = lax.dot_general(
        screen, heads, (((1,), (1,)), ((), ())), precision=HIGHEST, preferred_element_type=F32
    )
    at = iota((2 * OWN, 512), 1)
    keep = ((at >> 3).astype(F32) == column2) & (
        ((at >> 2) & 1) == iota((2 * OWN, 512), 0) // OWN
    )
    sums = jnp.where(keep, sums, 0.0)
    pick = jnp.where((iota((512, 128), 0) & 3) == iota((512, 128), 1), 1.0, 0.0)
    sums = jnp.dot(sums, pick, precision=HIGHEST, preferred_element_type=F32)
    sums = (sums[:OWN] + sums[OWN:]) * (1.0 / SCREEN)
    lane = iota((OWN, 128), 1)
    for t in range(4):
        sums = jnp.where(lane == t, sums - observed[t], sums)
    sums = jnp.where(lane == 4, column, sums)
    sums = jnp.where(lane == 5, top, sums)
    eye = jnp.where(iota((8, 128), 0) == iota((8, 128), 1), 1.0, 0.0)
    turned = lax.dot_general(
        eye, sums, (((1,), (1,)), ((), ())), precision=HIGHEST, preferred_element_type=F32
    )
    message[...] = jnp.concatenate([turned, jnp.zeros((8, 128 - OWN), F32)], axis=1)
    total = jnp.broadcast_to(jnp.sum(turned * turned, axis=1, keepdims=True), (8, 128))
    squares[...] = jnp.where(iota((8, 128), 0) < 4, total, pltpu.roll(total, 4, 0))


def adjoint_source(messages, e_ref, r_ref, beta_ref, lhs):
    sub, lane = iota((8, 128), 0), iota((8, 128), 1)
    values = [jnp.zeros((8, 128), F32) for g in range(3)]
    cells = [jnp.zeros((8, 128), F32) for g in range(3)]
    tops = [jnp.zeros((8, 128), F32) for g in range(3)]
    for k, (dx, dy) in enumerate(DIRECTIONS):
        tile = messages[k]
        value = jnp.where(sub < 4, tile, pltpu.roll(tile, 4, 0))
        column = jnp.broadcast_to(tile[4:5], (8, 128))
        along = jnp.floor(column * (1.0 / SIDE))
        x = along + (HALO + SIDE * dx)
        y = column - along * SIDE + (HALO + SIDE * dy)
        ok = (x >= 1) & (x < EXT - 1) & (y >= 1) & (y < EXT - 1) & (lane < OWN)
        cell = jnp.where(ok, x * EXT + y, 0.0)
        top = jnp.where(lane < OWN, jnp.broadcast_to(tile[5:6], (8, 128)), 0.0)
        g, shift = k // 4, OWN * (k % 4)
        if shift:
            value, cell, top = [pltpu.roll(v, shift, 1) for v in (value, cell, top)]
        values[g], cells[g], tops[g] = values[g] + value, cells[g] + cell, tops[g] + top
    z = iota((256, 128), 0).astype(F32)
    screens = []
    for g in range(3):
        top = jnp.broadcast_to(tops[g][0:1], (256, 128))
        screens.append(jnp.where((z >= top) & (z < top + SCREEN), 1.0, 0.0))
    screen = jnp.concatenate(screens, axis=1)
    wide = EXT - 2
    shape = (wide, 8, 128)
    lo, hi = 1, EXT - 1

    def left(x):
        cell = (x * EXT + 1 + iota(shape, 0)).astype(F32)
        for g in range(3):
            lhs[x - 1, :, g * 128 : (g + 1) * 128] = jnp.where(
                cells[g][None] == cell, values[g][None], 0.0
            ).reshape(wide * 8, 128)

    rows(lo, hi, left)
    group = 7
    for first in range(0, wide, group):
        block = lhs[first : first + group].reshape(group * wide * 8, 384)
        both = lax.dot_general(
            block, screen, (((1,), (1,)), ((), ())), precision=HIGHEST, preferred_element_type=F32
        )
        pair = both.reshape(group, wide, 8, 256)
        for i in range(group):
            source = jnp.where(iota(shape, 1) < 4, pair[i, :, :, :128], pair[i, :, :, 128:])
            x = first + i + 1
            beta_ref[x, lo:hi] = e_ref[x, lo:hi] * r_ref[x, lo:hi] * source


def sensitivity(e_ref, heads_ref, adjoint_ref, scale, out_ref):
    lo, hi = HALO, HALO + SIDE

    def cell_terms(x):
        h, a = heads_ref[x, lo:hi], adjoint_ref[x, lo:hi]
        e = e_ref[x, lo:hi]
        total = jnp.zeros_like(h)
        for step_x, step_y in ((1, 0), (-1, 0), (0, 1), (0, -1)):
            at = (x + step_x, slice(lo + step_y, hi + step_y))
            total = total + e_ref[at] * (h - heads_ref[at]) * (a - adjoint_ref[at])
        for e_n, h_n, a_n in zip(
            z_neighbours(e, 1.0), z_neighbours(h, 0.0), z_neighbours(a, 0.0)
        ):
            total = total + e_n * (h - h_n) * (a - a_n)
        total = total * e * scale[None]
        total = total + pltpu.roll(total, 7, 1)
        out_ref[x - HALO] = total + pltpu.roll(total, 6, 1)

    rows(lo, hi, cell_terms)


def slabs(sum_ref, out):
    lane = iota((8, 128), 1)
    for half in range(2):
        planes = sum_ref[:, :, 4 * half, :]
        for q in range(4):
            for xq in range(2):
                packed = jnp.zeros((8, 128), F32)
                for xx in range(4):
                    plane = planes[4 * xq + xx]
                    shift = (32 * (xx - q)) % 128
                    if shift:
                        plane = pltpu.roll(plane, shift, 1)
                    packed = jnp.where((lane >> 5) == xx, plane, packed)
                out[4 * half + q, xq] = packed


def kernel(
    packed, owner, column, top, observed, owner_s, column_s, top_s, pump_rate, pump_well, out,
    ext, e_ref, r_ref, alpha_ref, heads_ref, beta_ref, u_ref, adjoint_ref, sum_ref, lhs,
    message, squares, messages, near, partial, far, parts, slots,
    halo_send, halo_recv, msg_send, msg_recv, near_send, near_recv, far_send, far_recv,
    part_send, part_recv,
):
    me, bx, by = lax.axis_index("test"), lax.axis_index("bx"), lax.axis_index("by")
    turn, place = by // ROUND, lax.rem(by, ROUND)
    neighbours = [neighbour(dx, dy) for k, (dx, dy) in NEIGHBOURS]
    near_peers = [
        {
            "bx": lax.rem(bx + a, NX_BRICKS),
            "by": turn * ROUND + lax.rem(place + b, ROUND),
        }
        for a in range(NX_BRICKS) for b in range(ROUND) if a + b > 0
    ]
    far_peers = [
        {"by": lax.rem(by + c * ROUND, NY_BRICKS)} for c in range(1, NY_BRICKS // ROUND)
    ]
    test_peers = [lax.rem(me + d, TESTS_AXIS) for d in range(1, TESTS_AXIS)]
    for cx in (0, HALO + SIDE):
        for cy in (0, HALO + SIDE):
            ext[cx : cx + HALO, cy : cy + HALO] = jnp.zeros((HALO, HALO, 8, 128), F32)
    everyone = far_peers + neighbours + near_peers + [{"test": peer} for peer in test_peers]
    barrier = pltpu.get_barrier_semaphore()
    for peer in everyone:
        pl.semaphore_signal(barrier, inc=1, device_id=peer, device_id_type=MESH)
    pl.semaphore_wait(barrier, len(everyone))
    halo_copies = start_halos(packed, ext, halo_send, halo_recv)
    ext[HALO : HALO + SIDE, HALO : HALO + SIDE] = packed[...]
    pump_cell, pump_tile = pumping(pump_rate, pump_well, owner_s, column_s, top_s)
    wells = own_wells(owner, column, top, observed)
    for copy in halo_copies:
        copy.wait()
    coefficients(ext, e_ref, r_ref, alpha_ref, beta_ref, pump_cell, pump_tile)
    sweeps(e_ref, alpha_ref, beta_ref, u_ref, heads_ref)
    residuals(heads_ref, wells, message, squares)
    near_copies = [
        remote(squares, near.at[i], near_send.at[i], near_recv.at[i], peer)
        for i, peer in enumerate(near_peers)
    ]
    copies = [
        remote(message, messages.at[8 - k], msg_send.at[k], msg_recv.at[k], neighbour(dx, dy))
        for k, (dx, dy) in NEIGHBOURS
    ]
    messages[4] = message[...]
    for copy in near_copies:
        copy.wait()
    here = squares[...]
    for i in range(len(near_peers)):
        here = here + near[i]
    partial[...] = here
    far_copies = [
        remote(partial, far.at[i], far_send.at[i], far_recv.at[i], peer)
        for i, peer in enumerate(far_peers)
    ]
    for copy in copies:
        copy.wait()
    adjoint_source(messages, e_ref, r_ref, beta_ref, lhs)
    sweeps(e_ref, alpha_ref, beta_ref, u_ref, adjoint_ref)
    for copy in far_copies:
        copy.wait()
    total = partial[...]
    for i in range(len(far_peers)):
        total = total + far[i]
    scale = (-0.5 / (4 * TESTS_AXIS)) / (total / WELLS + EPSILON)
    sensitivity(e_ref, heads_ref, adjoint_ref, scale, sum_ref)
    slabs(sum_ref, parts)
    part_copies = [
        remote(parts.at[peer], slots.at[i], part_send.at[i], part_recv.at[i], {"test": peer})
        for i, peer in enumerate(test_peers)
    ]
    for copy in part_copies:
        copy.wait()
    total = parts[me]
    for i in range(TESTS_AXIS - 1):
        total = total + slots[i]
    for xq in range(2):
        for xx in range(4):
            plane = total[xq]
            if xx:
                plane = pltpu.roll(plane, 128 - 32 * xx, 1)
            out[4 * xq + xx] = plane[:, :32]


def local(
    log_conductivity, storage, recharge, pump_rate, pump_well, observed, owner, screen_column, screen_top
):
    dma = pltpu.SemaphoreType.DMA
    field = (EXT, EXT, 8, 128)
    tile = (8, 128)
    shape = (SIDE, SIDE, 2, 128)
    packed = jnp.concatenate(
        [log_conductivity.reshape(shape), storage.reshape(shape), recharge.reshape(shape),
         jnp.zeros(shape, F32)],
        axis=2,
    )
    table = [a.reshape(16, 128) for a in (owner, screen_column, screen_top)]
    near, far = NX_BRICKS * ROUND - 1, NY_BRICKS // ROUND - 1
    scratch = [field] * 8 + [
        (SIDE, SIDE) + tile, (EXT - 2, (EXT - 2) * 8, 384), tile, tile, (9,) + tile,
        (near,) + tile, tile, (far,) + tile, (TESTS_AXIS, 2) + tile, (TESTS_AXIS - 1, 2) + tile,
    ]
    counts = (9, 9, 9, 9, near, near, far, far, TESTS_AXIS - 1, TESTS_AXIS - 1)
    return pl.pallas_call(
        kernel,
        out_shape=jax.ShapeDtypeStruct((SIDE, SIDE, 32), F32),
        in_specs=[pl.BlockSpec(memory_space=VMEM)] * 5 + [pl.BlockSpec(memory_space=SMEM)] * 5,
        out_specs=pl.BlockSpec(memory_space=VMEM),
        scratch_shapes=[VMEM(s, F32) for s in scratch] + [dma((n,)) for n in counts],
        compiler_params=pltpu.CompilerParams(
            vmem_limit_bytes=48 * 1024 * 1024, collective_id=0, has_side_effects=True
        ),
    )(packed, *table, observed, owner, screen_column, screen_top, pump_rate, pump_well)


def solution(mesh):
    placed = (
        P("bx", "by", None), P("bx", "by", None), P("bx", "by", None), P("test"), P("test"),
        P("test", None), P(), P(), P(),
    )
    return jax.shard_map(
        local, mesh=mesh, in_specs=placed, out_specs=P("bx", "by", "test"), check_vma=False
    )
```

```python
import jax
import jax.numpy as jnp
from jax import lax
from jax.experimental import pallas as pl
from jax.experimental.pallas import tpu as pltpu
from jax.sharding import PartitionSpec as P

F32 = jnp.float32
MESH = pl.DeviceIdType.MESH
VMEM = pltpu.VMEM
SMEM = pltpu.SMEM
HIGHEST = lax.Precision.HIGHEST
EPSILON = 1e-06
SCREEN = 8
SIDE = 8
HALO = 4
EXT = SIDE + 2 * HALO
NX_BRICKS, NY_BRICKS = 4, 16
ROUND = 4
TESTS_AXIS = 8
WELLS = 2048
OWN = 32
DIRECTIONS = [(dx, dy) for dx in (-1, 0, 1) for dy in (-1, 0, 1)]
NEIGHBOURS = [(k, d) for k, d in enumerate(DIRECTIONS) if d != (0, 0)]


def iota(shape, dim):
    return lax.broadcasted_iota(jnp.int32, shape, dim)


def z_neighbours(values, fill):
    sub, lane = iota(values.shape, 1), iota(values.shape, 2)
    low = pltpu.roll(values, 1, 2)
    low = jnp.where(lane == 0, jnp.where(sub < 4, fill, pltpu.roll(low, 4, 1)), low)
    high = pltpu.roll(values, 127, 2)
    high = jnp.where(lane == 127, jnp.where(sub < 4, pltpu.roll(high, 4, 1), fill), high)
    return low, high


def around(ref, x, lo, hi, fill):
    low, high = z_neighbours(ref[x, lo:hi], fill)
    return (
        (ref[x - 1, lo:hi] + ref[x + 1, lo:hi])
        + (ref[x, lo - 1 : hi - 1] + ref[x, lo + 1 : hi + 1])
        + (low + high)
    )


def rows(lo, hi, body):
    def step(x, carry):
        body(x)
        return carry

    lax.fori_loop(lo, hi, step, 0)


def halves(ref, x, lo, hi, field):
    first = ref[x, lo:hi, 2 * field : 2 * field + 1, :]
    second = ref[x, lo:hi, 2 * field + 1 : 2 * field + 2, :]
    shape = (hi - lo, 8, 128)
    return jnp.where(
        iota(shape, 1) < 4, jnp.broadcast_to(first, shape), jnp.broadcast_to(second, shape)
    )


def inside(x, lo, hi):
    shape = (hi - lo, 8, 128)
    gx = lax.axis_index("bx") * SIDE + x - HALO + jnp.zeros(shape, jnp.int32)
    gy = lax.axis_index("by") * SIDE + lo - HALO + iota(shape, 0)
    return (gx >= 0) & (gx < NX_BRICKS * SIDE) & (gy >= 0) & (gy < NY_BRICKS * SIDE)


def neighbour(dx, dy):
    bx, by = lax.axis_index("bx"), lax.axis_index("by")
    return {
        "bx": lax.rem(bx + dx + NX_BRICKS, NX_BRICKS),
        "by": lax.rem(by + dy + NY_BRICKS, NY_BRICKS),
    }


def remote(source, target, send_sem, recv_sem, peer):
    copy = pltpu.make_async_remote_copy(
        src_ref=source, dst_ref=target, send_sem=send_sem, recv_sem=recv_sem,
        device_id=peer, device_id_type=MESH,
    )
    copy.start()
    return copy


def halo_copies(packed, ext, send_sems, recv_sems):
    me = lax.axis_index("test")
    core = lax.rem(me, 2)
    partner = {"test": me + 1 - 2 * core}
    deep = HALO - 1
    first, second = [], []
    half = pl.ds(SIDE // 2 * core, SIDE // 2)
    half_there = pl.ds(HALO + SIDE // 2 * core, SIDE // 2)
    corner = pl.ds((SIDE - deep) * core, deep)
    corner_there = pl.ds((HALO + SIDE) * (1 - core) + core, deep)
    for dy, from_y, to_y, skip in ((1, SIDE - deep, 1, 1), (-1, 0, HALO + SIDE, 0)):
        first.append(
            (half, pl.ds(from_y, deep), half_there, pl.ds(to_y, deep), neighbour(0, dy))
        )
        first.append(
            (corner, pl.ds(from_y + skip, deep - 1), corner_there, pl.ds(to_y + skip, deep - 1),
             neighbour(2 * core - 1, dy))
        )
    first = [first[0], first[2], first[1], first[3]]
    for dx, from_x, to_x in ((1, SIDE - HALO, 0), (-1, 0, HALO + SIDE)):
        second.append(
            (pl.ds(from_x, HALO), pl.ds(0, SIDE), pl.ds(to_x, HALO), pl.ds(HALO, SIDE),
             neighbour(dx, 0))
        )
    started = [
        remote(packed.at[x, y], ext.at[to_x, to_y], send_sems.at[k], recv_sems.at[k], peer)
        for k, (x, y, to_x, to_y, peer) in enumerate(first + second)
    ]

    def finish():
        passed = []
        for k, (x, y, to_x, to_y, peer) in enumerate(first):
            started[k].wait_recv()
            block = ext.at[to_x, to_y]
            passed.append(remote(block, block, send_sems.at[6 + k], recv_sems.at[6 + k], partner))
        for copy in started[: len(first)]:
            copy.wait_send()
        for copy in started[len(first) :] + passed:
            copy.wait()

    return finish


def coefficients(ext, e_ref, r_ref, alpha_ref, beta_ref, pump_cell, pump_tile):
    def roots(x):
        e_ref[x] = jnp.where(inside(x, 0, EXT), jnp.exp(0.5 * halves(ext, x, 0, EXT, 0)), 1.0)

    rows(0, EXT, roots)
    lo, hi = 1, EXT - 1

    def edge(xs, y, source_y):
        count = xs.stop - xs.start
        shape = (count, 8, 128)
        first = ext[xs, source_y, 6:7, :]
        second = ext[xs, source_y, 7:8, :]
        logs = jnp.where(
            iota(shape, 1) < 4, jnp.broadcast_to(first, shape), jnp.broadcast_to(second, shape)
        )
        gx = lax.axis_index("bx") * SIDE + xs.start - HALO + iota(shape, 0)
        gy = lax.axis_index("by") * SIDE + y - HALO + jnp.zeros(shape, jnp.int32)
        ok = (gx >= 0) & (gx < NX_BRICKS * SIDE) & (gy >= 0) & (gy < NY_BRICKS * SIDE)
        e_ref[xs, y] = jnp.where(ok, jnp.exp(0.5 * logs), 1.0)

    middle = slice(HALO, HALO + SIDE)
    edge(middle, 0, 1)
    edge(middle, EXT - 1, EXT - 2)
    for x in (HALO - 1, HALO + SIDE):
        edge(slice(x, x + 1), 1, 2)
        edge(slice(x, x + 1), EXT - 2, EXT - 3)

    def terms(x):
        e = e_ref[x, lo:hi]
        diagonal = halves(ext, x, lo, hi, 1) + e * around(e_ref, x, lo, hi, 1.0)
        r = jnp.where(inside(x, lo, hi), 1.0 / diagonal, 0.0)
        cell = x * EXT + lo + iota(e.shape, 0)
        source = halves(ext, x, lo, hi, 2) + jnp.where(pump_cell[None] == cell, pump_tile[None], 0.0)
        er = e * r
        r_ref[x, lo:hi] = r
        alpha_ref[x, lo:hi] = e * er
        beta_ref[x, lo:hi] = er * source

    rows(lo, hi, terms)


def sweeps(e_ref, alpha_ref, beta_ref, u_ref, out_ref):
    def second(x):
        u_ref[x, 2 : EXT - 2] = beta_ref[x, 2 : EXT - 2] + alpha_ref[x, 2 : EXT - 2] * around(
            beta_ref, x, 2, EXT - 2, 0.0
        )

    rows(2, EXT - 2, second)

    def third(x):
        u = beta_ref[x, 3 : EXT - 3] + alpha_ref[x, 3 : EXT - 3] * around(u_ref, x, 3, EXT - 3, 0.0)
        out_ref[x, 3 : EXT - 3] = u / e_ref[x, 3 : EXT - 3]

    rows(3, EXT - 3, third)


def pumping(pump_rate, pump_well, owner, column, top):
    sub, lane = iota((8, 128), 0), iota((8, 128), 1)
    z = lane + jnp.where(sub < 4, 0, 128)
    cell = jnp.zeros((8, 128), jnp.int32)
    tile = jnp.zeros((8, 128), F32)
    first_x = lax.axis_index("bx") * SIDE - HALO
    first_y = lax.axis_index("by") * SIDE - HALO
    for t in range(4):
        well = pump_well[t]
        brick, place, start = owner[well], column[well], top[well]
        x = (brick >> 4) * SIDE + (place >> 3) - first_x
        y = (brick & 15) * SIDE + (place & 7) - first_y
        ok = (x >= 0) & (x < EXT) & (y >= 0) & (y < EXT)
        mine = (sub & 3) == t
        cell = jnp.where(mine, jnp.where(ok, x * EXT + y, -1), cell)
        hit = mine & (z >= start) & (z < start + SCREEN)
        tile = jnp.where(hit, -pump_rate[t], tile)
    return cell, tile


def own_wells(owner, column, top, observed):
    brick = lax.axis_index("bx") * NY_BRICKS + lax.axis_index("by")
    mine = jnp.where(owner[...] == brick, 1.0, 0.0)
    upto = jnp.where(iota((128, 128), 0) <= iota((128, 128), 1), 1.0, 0.0)
    inner = jnp.dot(mine, upto, precision=HIGHEST, preferred_element_type=F32)
    count = jnp.broadcast_to(jnp.sum(mine, axis=1, keepdims=True), (16, 128))
    before = jnp.where(iota((16, 16), 1) < iota((16, 16), 0), 1.0, 0.0)
    rank = inner + jnp.dot(before, count, precision=HIGHEST, preferred_element_type=F32) - 1.0
    rank = jnp.where(mine > 0.0, rank, -1.0)
    place = iota((OWN, 128), 0).astype(F32)
    sums = [jnp.zeros((OWN, 128), F32) for field in range(6)]
    for k in range(16):
        hit = jnp.broadcast_to(rank[k : k + 1, :], (OWN, 128)) == place
        values = [column[k : k + 1, :].astype(F32), top[k : k + 1, :].astype(F32)]
        values += [observed[t : t + 1, k * 128 : (k + 1) * 128] for t in range(4)]
        for field in range(6):
            sums[field] = sums[field] + jnp.where(
                hit, jnp.broadcast_to(values[field], (OWN, 128)), 0.0
            )
    return [jnp.sum(s, axis=1, keepdims=True) for s in sums]


def residuals(heads_ref, wells, message, squares):
    column, top, observed = wells[0], wells[1], wells[2:]
    column2 = jnp.concatenate([column, column], axis=0)
    top2 = jnp.concatenate([top, top], axis=0)
    half = iota((2 * OWN, 128), 0) // OWN
    z = (iota((2 * OWN, 128), 1) + 128 * half).astype(F32)
    screen = jnp.where((z >= top2) & (z < top2 + SCREEN), 1.0, 0.0)
    heads = heads_ref[HALO : HALO + SIDE, HALO : HALO + SIDE].reshape(512, 128)
    sums = lax.dot_general(
        screen, heads, (((1,), (1,)), ((), ())), precision=HIGHEST, preferred_element_type=F32
    )
    at = iota((2 * OWN, 512), 1)
    keep = ((at >> 3).astype(F32) == column2) & (
        ((at >> 2) & 1) == iota((2 * OWN, 512), 0) // OWN
    )
    sums = jnp.where(keep, sums, 0.0)
    pick = jnp.where((iota((512, 128), 0) & 3) == iota((512, 128), 1), 1.0, 0.0)
    sums = jnp.dot(sums, pick, precision=HIGHEST, preferred_element_type=F32)
    sums = (sums[:OWN] + sums[OWN:]) * (1.0 / SCREEN)
    lane = iota((OWN, 128), 1)
    for t in range(4):
        sums = jnp.where(lane == t, sums - observed[t], sums)
    sums = jnp.where(lane == 4, column, sums)
    sums = jnp.where(lane == 5, top, sums)
    eye = jnp.where(iota((8, 128), 0) == iota((8, 128), 1), 1.0, 0.0)
    turned = lax.dot_general(
        eye, sums, (((1,), (1,)), ((), ())), precision=HIGHEST, preferred_element_type=F32
    )
    message[...] = jnp.concatenate([turned, jnp.zeros((8, 128 - OWN), F32)], axis=1)
    total = jnp.broadcast_to(jnp.sum(turned * turned, axis=1, keepdims=True), (8, 128))
    squares[...] = jnp.where(iota((8, 128), 0) < 4, total, pltpu.roll(total, 4, 0))


def adjoint_source(messages, e_ref, r_ref, beta_ref, lhs):
    sub, lane = iota((8, 128), 0), iota((8, 128), 1)
    values = [jnp.zeros((8, 128), F32) for g in range(3)]
    cells = [jnp.zeros((8, 128), F32) for g in range(3)]
    tops = [jnp.zeros((8, 128), F32) for g in range(3)]
    for k, (dx, dy) in enumerate(DIRECTIONS):
        tile = messages[k]
        value = jnp.where(sub < 4, tile, pltpu.roll(tile, 4, 0))
        column = jnp.broadcast_to(tile[4:5], (8, 128))
        along = jnp.floor(column * (1.0 / SIDE))
        x = along + (HALO + SIDE * dx)
        y = column - along * SIDE + (HALO + SIDE * dy)
        ok = (x >= 1) & (x < EXT - 1) & (y >= 1) & (y < EXT - 1) & (lane < OWN)
        cell = jnp.where(ok, x * EXT + y, 0.0)
        top = jnp.where(lane < OWN, jnp.broadcast_to(tile[5:6], (8, 128)), 0.0)
        g, shift = k // 4, OWN * (k % 4)
        if shift:
            value, cell, top = [pltpu.roll(v, shift, 1) for v in (value, cell, top)]
        values[g], cells[g], tops[g] = values[g] + value, cells[g] + cell, tops[g] + top
    z = iota((256, 128), 0).astype(F32)
    screens = []
    for g in range(3):
        top = jnp.broadcast_to(tops[g][0:1], (256, 128))
        screens.append(jnp.where((z >= top) & (z < top + SCREEN), 1.0, 0.0))
    screen = jnp.concatenate(screens, axis=1)
    wide = EXT - 2
    shape = (wide, 8, 128)
    lo, hi = 1, EXT - 1

    def left(x):
        cell = (x * EXT + 1 + iota(shape, 0)).astype(F32)
        for g in range(3):
            lhs[x - 1, :, g * 128 : (g + 1) * 128] = jnp.where(
                cells[g][None] == cell, values[g][None], 0.0
            ).reshape(wide * 8, 128)

    rows(lo, hi, left)
    group = 7
    for first in range(0, wide, group):
        block = lhs[first : first + group].reshape(group * wide * 8, 384)
        both = lax.dot_general(
            block, screen, (((1,), (1,)), ((), ())), precision=HIGHEST, preferred_element_type=F32
        )
        pair = both.reshape(group, wide, 8, 256)
        for i in range(group):
            source = jnp.where(iota(shape, 1) < 4, pair[i, :, :, :128], pair[i, :, :, 128:])
            x = first + i + 1
            beta_ref[x, lo:hi] = e_ref[x, lo:hi] * r_ref[x, lo:hi] * source


def sensitivity(e_ref, heads_ref, adjoint_ref, scale, out_ref):
    lo, hi = HALO, HALO + SIDE

    def cell_terms(x):
        h, a = heads_ref[x, lo:hi], adjoint_ref[x, lo:hi]
        e = e_ref[x, lo:hi]
        total = jnp.zeros_like(h)
        for step_x, step_y in ((1, 0), (-1, 0), (0, 1), (0, -1)):
            at = (x + step_x, slice(lo + step_y, hi + step_y))
            total = total + e_ref[at] * (h - heads_ref[at]) * (a - adjoint_ref[at])
        for e_n, h_n, a_n in zip(
            z_neighbours(e, 1.0), z_neighbours(h, 0.0), z_neighbours(a, 0.0)
        ):
            total = total + e_n * (h - h_n) * (a - a_n)
        total = total * e * scale[None]
        total = total + pltpu.roll(total, 7, 1)
        out_ref[x - HALO] = total + pltpu.roll(total, 6, 1)

    rows(lo, hi, cell_terms)


def slabs(sum_ref, out):
    lane = iota((8, 128), 1)
    for half in range(2):
        planes = sum_ref[:, :, 4 * half, :]
        for q in range(4):
            for xq in range(2):
                packed = jnp.zeros((8, 128), F32)
                for xx in range(4):
                    plane = planes[4 * xq + xx]
                    shift = (32 * (xx - q)) % 128
                    if shift:
                        plane = pltpu.roll(plane, shift, 1)
                    packed = jnp.where((lane >> 5) == xx, plane, packed)
                out[4 * half + q, xq] = packed


def kernel(
    packed, owner, column, top, observed, owner_s, column_s, top_s, pump_rate, pump_well, out,
    ext, e_ref, r_ref, alpha_ref, heads_ref, beta_ref, u_ref, adjoint_ref, sum_ref, lhs,
    message, squares, messages, near, partial, far, parts, slots,
    halo_send, halo_recv, msg_send, msg_recv, near_send, near_recv, far_send, far_recv,
    part_send, part_recv,
):
    me, bx, by = lax.axis_index("test"), lax.axis_index("bx"), lax.axis_index("by")
    turn, place = by // ROUND, lax.rem(by, ROUND)
    neighbours = [neighbour(dx, dy) for k, (dx, dy) in NEIGHBOURS]
    near_peers = [
        {
            "bx": lax.rem(bx + a, NX_BRICKS),
            "by": turn * ROUND + lax.rem(place + b, ROUND),
        }
        for a in range(NX_BRICKS) for b in range(ROUND) if a + b > 0
    ]
    far_peers = [
        {"by": lax.rem(by + c * ROUND, NY_BRICKS)} for c in range(1, NY_BRICKS // ROUND)
    ]
    test_peers = [lax.rem(me + d, TESTS_AXIS) for d in range(1, TESTS_AXIS)]
    for cx in (0, HALO + SIDE):
        for cy in (0, HALO + SIDE):
            ext[cx : cx + HALO, cy : cy + HALO] = jnp.zeros((HALO, HALO, 8, 128), F32)
    everyone = far_peers + neighbours + near_peers + [{"test": peer} for peer in test_peers]
    barrier = pltpu.get_barrier_semaphore()
    for peer in everyone:
        pl.semaphore_signal(barrier, inc=1, device_id=peer, device_id_type=MESH)
    pl.semaphore_wait(barrier, len(everyone))
    finish_halo = halo_copies(packed, ext, halo_send, halo_recv)
    ext[HALO : HALO + SIDE, HALO : HALO + SIDE] = packed[...]
    pump_cell, pump_tile = pumping(pump_rate, pump_well, owner_s, column_s, top_s)
    wells = own_wells(owner, column, top, observed)
    finish_halo()
    coefficients(ext, e_ref, r_ref, alpha_ref, beta_ref, pump_cell, pump_tile)
    sweeps(e_ref, alpha_ref, beta_ref, u_ref, heads_ref)
    residuals(heads_ref, wells, message, squares)
    near_copies = [
        remote(squares, near.at[i], near_send.at[i], near_recv.at[i], peer)
        for i, peer in enumerate(near_peers)
    ]
    copies = [
        remote(message, messages.at[8 - k], msg_send.at[k], msg_recv.at[k], neighbour(dx, dy))
        for k, (dx, dy) in NEIGHBOURS
    ]
    messages[4] = message[...]
    for copy in near_copies:
        copy.wait()
    here = squares[...]
    for i in range(len(near_peers)):
        here = here + near[i]
    partial[...] = here
    far_copies = [
        remote(partial, far.at[i], far_send.at[i], far_recv.at[i], peer)
        for i, peer in enumerate(far_peers)
    ]
    for copy in copies:
        copy.wait()
    adjoint_source(messages, e_ref, r_ref, beta_ref, lhs)
    sweeps(e_ref, alpha_ref, beta_ref, u_ref, adjoint_ref)
    for copy in far_copies:
        copy.wait()
    total = partial[...]
    for i in range(len(far_peers)):
        total = total + far[i]
    scale = (-0.5 / (4 * TESTS_AXIS)) / (total / WELLS + EPSILON)
    sensitivity(e_ref, heads_ref, adjoint_ref, scale, sum_ref)
    slabs(sum_ref, parts)
    part_copies = [
        remote(parts.at[peer], slots.at[i], part_send.at[i], part_recv.at[i], {"test": peer})
        for i, peer in enumerate(test_peers)
    ]
    for copy in part_copies:
        copy.wait()
    total = parts[me]
    for i in range(TESTS_AXIS - 1):
        total = total + slots[i]
    for xq in range(2):
        for xx in range(4):
            plane = total[xq]
            if xx:
                plane = pltpu.roll(plane, 128 - 32 * xx, 1)
            out[4 * xq + xx] = plane[:, :32]


def local(
    log_conductivity, storage, recharge, pump_rate, pump_well, observed, owner, screen_column, screen_top
):
    dma = pltpu.SemaphoreType.DMA
    field = (EXT, EXT, 8, 128)
    tile = (8, 128)
    shape = (SIDE, SIDE, 2, 128)
    further = jnp.concatenate([log_conductivity[:, 1:5], log_conductivity[:, 3:7]], axis=1)
    packed = jnp.concatenate(
        [a.reshape(shape) for a in (log_conductivity, storage, recharge, further)], axis=2
    )
    table = [a.reshape(16, 128) for a in (owner, screen_column, screen_top)]
    near, far = NX_BRICKS * ROUND - 1, NY_BRICKS // ROUND - 1
    scratch = [field] * 8 + [
        (SIDE, SIDE) + tile, (EXT - 2, (EXT - 2) * 8, 384), tile, tile, (9,) + tile,
        (near,) + tile, tile, (far,) + tile, (TESTS_AXIS, 2) + tile, (TESTS_AXIS - 1, 2) + tile,
    ]
    counts = (10, 10, 9, 9, near, near, far, far, TESTS_AXIS - 1, TESTS_AXIS - 1)
    return pl.pallas_call(
        kernel,
        out_shape=jax.ShapeDtypeStruct((SIDE, SIDE, 32), F32),
        in_specs=[pl.BlockSpec(memory_space=VMEM)] * 5 + [pl.BlockSpec(memory_space=SMEM)] * 5,
        out_specs=pl.BlockSpec(memory_space=VMEM),
        scratch_shapes=[VMEM(s, F32) for s in scratch] + [dma((n,)) for n in counts],
        compiler_params=pltpu.CompilerParams(
            vmem_limit_bytes=48 * 1024 * 1024, collective_id=0, has_side_effects=True
        ),
    )(packed, *table, observed, owner, screen_column, screen_top, pump_rate, pump_well)


def solution(mesh):
    placed = (
        P("bx", "by", None), P("bx", "by", None), P("bx", "by", None), P("test"), P("test"),
        P("test", None), P(), P(), P(),
    )
    return jax.shard_map(
        local, mesh=mesh, in_specs=placed, out_specs=P("bx", "by", "test"), check_vma=False
    )
```

```python
import jax
import jax.numpy as jnp
from jax import lax
from jax.experimental import pallas as pl
from jax.experimental.pallas import tpu as pltpu
from jax.sharding import PartitionSpec as P

F32 = jnp.float32
MESH = pl.DeviceIdType.MESH
VMEM = pltpu.VMEM
HIGHEST = lax.Precision.HIGHEST
EPSILON = 1e-06
SCREEN = 8
SIDE = 8
HALO = 4
EXT = SIDE + 2 * HALO
NX_BRICKS, NY_BRICKS = 4, 16
ROUND = 4
TESTS_AXIS = 8
WELLS = 2048
OWN = 32
GROUPS = 7
DIRECTIONS = [(dx, dy) for dx in (-1, 0, 1) for dy in (-1, 0, 1)]
FACES = [(1, 0), (-1, 0), (0, 1), (0, -1)]
NEIGHBOURS = [(k, d) for k, d in enumerate(DIRECTIONS) if d != (0, 0)]


def iota(shape, dim):
    return lax.broadcasted_iota(jnp.int32, shape, dim)


def z_neighbours(values, fill):
    sub, lane = iota(values.shape, 1), iota(values.shape, 2)
    low = pltpu.roll(values, 1, 2)
    low = jnp.where(lane == 0, jnp.where(sub < 4, fill, pltpu.roll(low, 4, 1)), low)
    high = pltpu.roll(values, 127, 2)
    high = jnp.where(lane == 127, jnp.where(sub < 4, pltpu.roll(high, 4, 1), fill), high)
    return low, high


def around(ref, x, lo, hi, fill):
    low, high = z_neighbours(ref[x, lo:hi], fill)
    return (
        (ref[x - 1, lo:hi] + ref[x + 1, lo:hi])
        + (ref[x, lo - 1 : hi - 1] + ref[x, lo + 1 : hi + 1])
        + (low + high)
    )


def rows(lo, hi, body, group):
    def step(i, carry):
        for j in range(group):
            body(lo + i * group + j)
        return carry

    lax.fori_loop(0, (hi - lo) // group, step, 0)


def thirds(values):
    parts, rest = [], values
    for i in range(3):
        parts.append(rest.astype(jnp.bfloat16))
        rest = rest - parts[-1].astype(F32)
    return parts


def halves(ref, x, lo, hi, field):
    first = ref[x, lo:hi, 2 * field : 2 * field + 1, :]
    second = ref[x, lo:hi, 2 * field + 1 : 2 * field + 2, :]
    shape = (hi - lo, 8, 128)
    return jnp.where(
        iota(shape, 1) < 4, jnp.broadcast_to(first, shape), jnp.broadcast_to(second, shape)
    )


def inside(x, lo, hi):
    shape = (hi - lo, 8, 128)
    gx = lax.axis_index("bx") * SIDE + x - HALO + jnp.zeros(shape, jnp.int32)
    gy = lax.axis_index("by") * SIDE + lo - HALO + iota(shape, 0)
    return (gx >= 0) & (gx < NX_BRICKS * SIDE) & (gy >= 0) & (gy < NY_BRICKS * SIDE)


def neighbour(dx, dy):
    bx, by = lax.axis_index("bx"), lax.axis_index("by")
    return {
        "bx": lax.rem(bx + dx + NX_BRICKS, NX_BRICKS),
        "by": lax.rem(by + dy + NY_BRICKS, NY_BRICKS),
    }


def remote(source, target, send_sem, recv_sem, peer):
    copy = pltpu.make_async_remote_copy(
        src_ref=source, dst_ref=target, send_sem=send_sem, recv_sem=recv_sem,
        device_id=peer, device_id_type=MESH,
    )
    copy.start()
    return copy


def halo_copies(packed, ext, send_sems, recv_sems):
    me = lax.axis_index("test")
    core = lax.rem(me, 2)
    partner = {"test": me + 1 - 2 * core}
    deep = HALO - 1
    first, second = [], []
    half = pl.ds(SIDE // 2 * core, SIDE // 2)
    half_there = pl.ds(HALO + SIDE // 2 * core, SIDE // 2)
    corner = pl.ds((SIDE - deep) * core, deep)
    corner_there = pl.ds((HALO + SIDE) * (1 - core) + core, deep)
    for dy, from_y, to_y, skip in ((1, SIDE - deep, 1, 1), (-1, 0, HALO + SIDE, 0)):
        first.append(
            (half, pl.ds(from_y, deep), half_there, pl.ds(to_y, deep), neighbour(0, dy))
        )
        first.append(
            (corner, pl.ds(from_y + skip, deep - 1), corner_there, pl.ds(to_y + skip, deep - 1),
             neighbour(2 * core - 1, dy))
        )
    first = [first[0], first[2], first[1], first[3]]
    for dx, from_x, to_x in ((1, SIDE - HALO, 0), (-1, 0, HALO + SIDE)):
        second.append(
            (pl.ds(from_x, HALO), pl.ds(0, SIDE), pl.ds(to_x, HALO), pl.ds(HALO, SIDE),
             neighbour(dx, 0))
        )
    started = [
        remote(packed.at[x, y], ext.at[to_x, to_y], send_sems.at[k], recv_sems.at[k], peer)
        for k, (x, y, to_x, to_y, peer) in enumerate(first + second)
    ]

    def finish():
        passed = []
        for k, (x, y, to_x, to_y, peer) in enumerate(first):
            started[k].wait_recv()
            block = ext.at[to_x, to_y]
            passed.append(remote(block, block, send_sems.at[6 + k], recv_sems.at[6 + k], partner))
        for copy in started[: len(first)]:
            copy.wait_send()
        for copy in started[len(first) :] + passed:
            copy.wait()

    return finish


def coefficients(ext, e_ref, r_ref, alpha_ref, beta_ref, pump_cell, pump_tile):
    def roots(x):
        e_ref[x] = jnp.where(inside(x, 0, EXT), jnp.exp(0.5 * halves(ext, x, 0, EXT, 0)), 1.0)

    rows(0, EXT, roots, 4)
    lo, hi = 1, EXT - 1

    def edge(xs, y, source_y):
        count = xs.stop - xs.start
        shape = (count, 8, 128)
        first = ext[xs, source_y, 6:7, :]
        second = ext[xs, source_y, 7:8, :]
        logs = jnp.where(
            iota(shape, 1) < 4, jnp.broadcast_to(first, shape), jnp.broadcast_to(second, shape)
        )
        gx = lax.axis_index("bx") * SIDE + xs.start - HALO + iota(shape, 0)
        gy = lax.axis_index("by") * SIDE + y - HALO + jnp.zeros(shape, jnp.int32)
        ok = (gx >= 0) & (gx < NX_BRICKS * SIDE) & (gy >= 0) & (gy < NY_BRICKS * SIDE)
        e_ref[xs, y] = jnp.where(ok, jnp.exp(0.5 * logs), 1.0)

    middle = slice(HALO, HALO + SIDE)
    edge(middle, 0, 1)
    edge(middle, EXT - 1, EXT - 2)
    for x in (HALO - 1, HALO + SIDE):
        edge(slice(x, x + 1), 1, 2)
        edge(slice(x, x + 1), EXT - 2, EXT - 3)

    def terms(x):
        e = e_ref[x, lo:hi]
        diagonal = halves(ext, x, lo, hi, 1) + e * around(e_ref, x, lo, hi, 1.0)
        r = jnp.where(inside(x, lo, hi), 1.0 / diagonal, 0.0)
        cell = x * EXT + lo + iota(e.shape, 0)
        source = halves(ext, x, lo, hi, 2) + jnp.where(pump_cell[None] == cell, pump_tile[None], 0.0)
        er = e * r
        r_ref[x, lo:hi] = r
        alpha_ref[x, lo:hi] = e * er
        beta_ref[x, lo:hi] = er * source

    rows(lo, hi, terms, 2)


def sweeps(e_ref, alpha_ref, beta_ref, u_ref, out_ref):
    def second(x):
        u_ref[x, 2 : EXT - 2] = beta_ref[x, 2 : EXT - 2] + alpha_ref[x, 2 : EXT - 2] * around(
            beta_ref, x, 2, EXT - 2, 0.0
        )

    rows(2, EXT - 2, second, 4)

    def third(x):
        u = beta_ref[x, 3 : EXT - 3] + alpha_ref[x, 3 : EXT - 3] * around(u_ref, x, 3, EXT - 3, 0.0)
        out_ref[x, 3 : EXT - 3] = u / e_ref[x, 3 : EXT - 3]

    rows(3, EXT - 3, third, 5)


def pumping(pump_rate, pump_well, owner, column, top):
    sub, lane = iota((8, 128), 0), iota((8, 128), 1)
    z = lane + jnp.where(sub < 4, 0, 128)
    cell = jnp.zeros((8, 128), jnp.int32)
    tile = jnp.zeros((8, 128), F32)
    first_x = lax.axis_index("bx") * SIDE - HALO
    first_y = lax.axis_index("by") * SIDE - HALO
    code = (owner[...] * 64 + column[...]) * 256 + top[...]
    code = code.astype(F32)
    index = iota((16, 128), 0) * 128 + iota((16, 128), 1)
    for t in range(4):
        well = jnp.broadcast_to(pump_well[0:1, t : t + 1], (16, 128))
        found = jnp.sum(jnp.where(index == well, code, 0.0), axis=0, keepdims=True)
        found = jnp.broadcast_to(jnp.sum(found, axis=1, keepdims=True), (8, 128)).astype(jnp.int32)
        brick, place, start = found >> 14, (found >> 8) & 63, found & 255
        x = (brick >> 4) * SIDE + (place >> 3) - first_x
        y = (brick & 15) * SIDE + (place & 7) - first_y
        ok = (x >= 0) & (x < EXT) & (y >= 0) & (y < EXT)
        mine = (sub & 3) == t
        cell = jnp.where(mine, jnp.where(ok, x * EXT + y, -1), cell)
        hit = mine & (z >= start) & (z < start + SCREEN)
        tile = jnp.where(hit, -jnp.broadcast_to(pump_rate[0:1, t : t + 1], (8, 128)), tile)
    return cell, tile


def pack(log_conductivity, storage, recharge, packed):
    def row(x):
        logs = log_conductivity[x]
        further = jnp.where(
            iota((SIDE, 256), 0) < 4, pltpu.roll(logs, SIDE - 1, 0), pltpu.roll(logs, 1, 0)
        )
        for field, values in enumerate((logs, storage[x], recharge[x], further)):
            packed[x, :, 2 * field, :] = values[:, :128]
            packed[x, :, 2 * field + 1, :] = values[:, 128:]

    rows(0, SIDE, row, 2)


def own_wells(owner, column, top, observed):
    brick = lax.axis_index("bx") * NY_BRICKS + lax.axis_index("by")
    mine = jnp.where(owner[...] == brick, 1.0, 0.0)
    upto = jnp.where(iota((128, 128), 0) <= iota((128, 128), 1), 1.0, 0.0)
    inner = jnp.dot(mine, upto, precision=HIGHEST, preferred_element_type=F32)
    count = jnp.broadcast_to(jnp.sum(mine, axis=1, keepdims=True), (16, 128))
    before = jnp.where(iota((16, 16), 1) < iota((16, 16), 0), 1.0, 0.0)
    rank = inner + jnp.dot(before, count, precision=HIGHEST, preferred_element_type=F32) - 1.0
    rank = jnp.where(mine > 0.0, rank, -1.0)
    place = iota((OWN, 128), 0).astype(F32)
    sums = [jnp.zeros((OWN, 128), F32) for field in range(6)]
    for k in range(16):
        hit = jnp.broadcast_to(rank[k : k + 1, :], (OWN, 128)) == place
        values = [column[k : k + 1, :].astype(F32), top[k : k + 1, :].astype(F32)]
        values += [observed[t : t + 1, k * 128 : (k + 1) * 128] for t in range(4)]
        for field in range(6):
            sums[field] = sums[field] + jnp.where(
                hit, jnp.broadcast_to(values[field], (OWN, 128)), 0.0
            )
    return [jnp.sum(s, axis=1, keepdims=True) for s in sums]


def residuals(heads_ref, wells, message, squares):
    column, top, observed = wells[0], wells[1], wells[2:]
    column2 = jnp.concatenate([column, column], axis=0)
    top2 = jnp.concatenate([top, top], axis=0)
    half = iota((2 * OWN, 128), 0) // OWN
    z = (iota((2 * OWN, 128), 1) + 128 * half).astype(F32)
    screen = jnp.where((z >= top2) & (z < top2 + SCREEN), 1.0, 0.0)
    heads = heads_ref[HALO : HALO + SIDE, HALO : HALO + SIDE].reshape(512, 128)
    screen = screen.astype(jnp.bfloat16)
    sums = lax.dot_general(
        jnp.concatenate([screen] * 3, axis=1), jnp.concatenate(thirds(heads), axis=1),
        (((1,), (1,)), ((), ())), preferred_element_type=F32,
    )
    at = iota((2 * OWN, 512), 1)
    keep = ((at >> 3).astype(F32) == column2) & (
        ((at >> 2) & 1) == iota((2 * OWN, 512), 0) // OWN
    )
    sums = jnp.where(keep, sums, 0.0)
    pick = jnp.where((iota((512, 128), 0) & 3) == iota((512, 128), 1), 1.0, 0.0)
    pick = pick.astype(jnp.bfloat16)
    sums = sum(jnp.dot(part, pick, preferred_element_type=F32) for part in thirds(sums))
    sums = (sums[:OWN] + sums[OWN:]) * (1.0 / SCREEN)
    lane = iota((OWN, 128), 1)
    for t in range(4):
        sums = jnp.where(lane == t, sums - observed[t], sums)
    sums = jnp.where(lane == 4, column, sums)
    sums = jnp.where(lane == 5, top, sums)
    eye = jnp.where(iota((8, 128), 0) == iota((8, 128), 1), 1.0, 0.0)
    turned = lax.dot_general(
        eye, sums, (((1,), (1,)), ((), ())), precision=HIGHEST, preferred_element_type=F32
    )
    message[...] = jnp.concatenate([turned, jnp.zeros((8, 128 - OWN), F32)], axis=1)
    total = jnp.broadcast_to(jnp.sum(turned * turned, axis=1, keepdims=True), (8, 128))
    squares[...] = jnp.where(iota((8, 128), 0) < 4, total, pltpu.roll(total, 4, 0))


def adjoint_source(messages, e_ref, r_ref, beta_ref, lhs):
    sub, lane = iota((8, 128), 0), iota((8, 128), 1)
    values = [jnp.zeros((8, 128), F32) for g in range(GROUPS)]
    cells = [jnp.zeros((8, 128), F32) for g in range(GROUPS)]
    tops = [jnp.zeros((8, 128), F32) for g in range(GROUPS)]
    for k, (dx, dy) in enumerate(DIRECTIONS):
        tile = messages[k]
        value = jnp.where(sub < 4, tile, pltpu.roll(tile, 4, 0))
        column = jnp.broadcast_to(tile[4:5], (8, 128))
        along = jnp.floor(column * (1.0 / SIDE))
        x = along + (HALO + SIDE * dx)
        y = column - along * SIDE + (HALO + SIDE * dy)
        ok = (x >= 1) & (x < EXT - 1) & (y >= 1) & (y < EXT - 1) & (lane < OWN)
        cell = jnp.where(ok, x * EXT + y, 0.0)
        top = jnp.where(lane < OWN, jnp.broadcast_to(tile[5:6], (8, 128)), 0.0)
        for p, part in enumerate(thirds(value)):
            g, shift = (3 * k + p) // 4, OWN * ((3 * k + p) % 4)
            moved = [part.astype(F32), cell, top]
            if shift:
                moved = [pltpu.roll(v, shift, 1) for v in moved]
            values[g], cells[g], tops[g] = values[g] + moved[0], cells[g] + moved[1], tops[g] + moved[2]
    z = iota((256, 128), 0).astype(F32)
    screens = []
    for g in range(GROUPS):
        top = jnp.broadcast_to(tops[g][0:1], (256, 128))
        screens.append(jnp.where((z >= top) & (z < top + SCREEN), 1.0, 0.0).astype(jnp.bfloat16))
    screen = jnp.concatenate(screens, axis=1)
    wide = EXT - 2
    shape = (wide, 8, 128)
    lo, hi = 1, EXT - 1

    def left(x):
        cell = (x * EXT + 1 + iota(shape, 0)).astype(F32)
        for g in range(GROUPS):
            lhs[x - 1, :, g * 128 : (g + 1) * 128] = (
                jnp.where(cells[g][None] == cell, values[g][None], 0.0)
                .reshape(wide * 8, 128)
                .astype(jnp.bfloat16)
            )

    rows(lo, hi, left, 2)
    group = 7
    for first in range(0, wide, group):
        block = lhs[first : first + group].reshape(group * wide * 8, GROUPS * 128)
        both = lax.dot_general(
            block, screen, (((1,), (1,)), ((), ())), preferred_element_type=F32
        )
        pair = both.reshape(group, wide, 8, 256)
        for i in range(group):
            source = jnp.where(iota(shape, 1) < 4, pair[i, :, :, :128], pair[i, :, :, 128:])
            x = first + i + 1
            beta_ref[x, lo:hi] = e_ref[x, lo:hi] * r_ref[x, lo:hi] * source


def head_steps(e_ref, heads_ref, steps_ref):
    lo, hi = HALO, HALO + SIDE

    def row(x):
        h, e = heads_ref[x, lo:hi], e_ref[x, lo:hi]
        for f, (step_x, step_y) in enumerate(FACES):
            at = (x + step_x, slice(lo + step_y, hi + step_y))
            steps_ref[f, x - HALO] = e * e_ref[at] * (h - heads_ref[at])
        for f, (e_n, h_n) in enumerate(zip(z_neighbours(e, 1.0), z_neighbours(h, 0.0))):
            steps_ref[4 + f, x - HALO] = e * e_n * (h - h_n)

    rows(lo, hi, row, 2)


def sensitivity(steps_ref, adjoint_ref, scale, out_ref):
    lo, hi = HALO, HALO + SIDE

    def row(x):
        a = adjoint_ref[x, lo:hi]
        total = jnp.zeros_like(a)
        for f, (step_x, step_y) in enumerate(FACES):
            total = total + steps_ref[f, x - HALO] * (
                a - adjoint_ref[x + step_x, lo + step_y : hi + step_y]
            )
        for f, a_n in enumerate(z_neighbours(a, 0.0)):
            total = total + steps_ref[4 + f, x - HALO] * (a - a_n)
        total = total * scale[None]
        total = total + pltpu.roll(total, 7, 1)
        out_ref[x - HALO] = total + pltpu.roll(total, 6, 1)

    rows(lo, hi, row, 4)


def slabs(sum_ref, out):
    lane = iota((8, 128), 1)
    for half in range(2):
        planes = sum_ref[:, :, 4 * half, :]
        for q in range(4):
            for xq in range(2):
                packed = jnp.zeros((8, 128), F32)
                for xx in range(4):
                    plane = planes[4 * xq + xx]
                    shift = (32 * (xx - q)) % 128
                    if shift:
                        plane = pltpu.roll(plane, shift, 1)
                    packed = jnp.where((lane >> 5) == xx, plane, packed)
                out[4 * half + q, xq] = packed


def kernel(
    log_conductivity, storage, recharge, owner, column, top, observed, pump_rate, pump_well, out,
    packed, steps_ref, lhs, ext, e_ref, r_ref, alpha_ref, heads_ref, beta_ref, u_ref, adjoint_ref, sum_ref,
    message, squares, messages, near, partial, far, parts, slots,
    halo_send, halo_recv, msg_send, msg_recv, near_send, near_recv, far_send, far_recv,
    part_send, part_recv,
):
    me, bx, by = lax.axis_index("test"), lax.axis_index("bx"), lax.axis_index("by")
    turn, place = by // ROUND, lax.rem(by, ROUND)
    neighbours = [neighbour(dx, dy) for k, (dx, dy) in NEIGHBOURS]
    near_peers = [
        {
            "bx": lax.rem(bx + a, NX_BRICKS),
            "by": turn * ROUND + lax.rem(place + b, ROUND),
        }
        for a in range(NX_BRICKS) for b in range(ROUND) if a + b > 0
    ]
    far_peers = [
        {"by": lax.rem(by + c * ROUND, NY_BRICKS)} for c in range(1, NY_BRICKS // ROUND)
    ]
    test_peers = [lax.rem(me + d, TESTS_AXIS) for d in range(1, TESTS_AXIS)]
    for cx in (0, HALO + SIDE):
        for cy in (0, HALO + SIDE):
            ext[cx : cx + HALO, cy : cy + HALO] = jnp.zeros((HALO, HALO, 8, 128), F32)
    everyone = far_peers + neighbours + near_peers + [{"test": peer} for peer in test_peers]
    barrier = pltpu.get_barrier_semaphore()
    for peer in everyone:
        pl.semaphore_signal(barrier, inc=1, device_id=peer, device_id_type=MESH)
    pack(log_conductivity, storage, recharge, packed)
    pl.semaphore_wait(barrier, len(everyone))
    finish_halo = halo_copies(packed, ext, halo_send, halo_recv)
    ext[HALO : HALO + SIDE, HALO : HALO + SIDE] = packed[...]
    pump_cell, pump_tile = pumping(pump_rate, pump_well, owner, column, top)
    wells = own_wells(owner, column, top, observed)
    finish_halo()
    coefficients(ext, e_ref, r_ref, alpha_ref, beta_ref, pump_cell, pump_tile)
    sweeps(e_ref, alpha_ref, beta_ref, u_ref, heads_ref)
    residuals(heads_ref, wells, message, squares)
    near_copies = [
        remote(squares, near.at[i], near_send.at[i], near_recv.at[i], peer)
        for i, peer in enumerate(near_peers)
    ]
    copies = [
        remote(message, messages.at[8 - k], msg_send.at[k], msg_recv.at[k], neighbour(dx, dy))
        for k, (dx, dy) in NEIGHBOURS
    ]
    messages[4] = message[...]
    for copy in near_copies:
        copy.wait()
    here = squares[...]
    for i in range(len(near_peers)):
        here = here + near[i]
    partial[...] = here
    far_copies = [
        remote(partial, far.at[i], far_send.at[i], far_recv.at[i], peer)
        for i, peer in enumerate(far_peers)
    ]
    head_steps(e_ref, heads_ref, steps_ref)
    for copy in copies:
        copy.wait()
    adjoint_source(messages, e_ref, r_ref, beta_ref, lhs)
    sweeps(e_ref, alpha_ref, beta_ref, u_ref, adjoint_ref)
    for copy in far_copies:
        copy.wait()
    total = partial[...]
    for i in range(len(far_peers)):
        total = total + far[i]
    scale = (-0.5 / (4 * TESTS_AXIS)) / (total / WELLS + EPSILON)
    sensitivity(steps_ref, adjoint_ref, scale, sum_ref)
    slabs(sum_ref, parts)
    part_copies = [
        remote(parts.at[peer], slots.at[i], part_send.at[i], part_recv.at[i], {"test": peer})
        for i, peer in enumerate(test_peers)
    ]
    for copy in part_copies:
        copy.wait()
    total = parts[me]
    for i in range(TESTS_AXIS - 1):
        total = total + slots[i]
    for xq in range(2):
        for xx in range(4):
            plane = total[xq]
            if xx:
                plane = pltpu.roll(plane, 128 - 32 * xx, 1)
            out[4 * xq + xx] = plane[:, :32]


def local(
    log_conductivity, storage, recharge, pump_rate, pump_well, observed, owner, screen_column, screen_top
):
    dma = pltpu.SemaphoreType.DMA
    field = (EXT, EXT, 8, 128)
    tile = (8, 128)
    table = [a.reshape(16, 128) for a in (owner, screen_column, screen_top)]
    near, far = NX_BRICKS * ROUND - 1, NY_BRICKS // ROUND - 1
    scratch = [field] * 8 + [
        (SIDE, SIDE) + tile, tile, tile, (9,) + tile,
        (near,) + tile, tile, (far,) + tile, (TESTS_AXIS, 2) + tile, (TESTS_AXIS - 1, 2) + tile,
    ]
    counts = (10, 10, 9, 9, near, near, far, far, TESTS_AXIS - 1, TESTS_AXIS - 1)
    return pl.pallas_call(
        kernel,
        out_shape=jax.ShapeDtypeStruct((SIDE, SIDE, 32), F32),
        in_specs=[pl.BlockSpec(memory_space=VMEM)] * 9,
        out_specs=pl.BlockSpec(memory_space=VMEM),
        scratch_shapes=[
            VMEM((SIDE, SIDE) + tile, F32),
            VMEM((6, SIDE, SIDE) + tile, F32),
            VMEM((EXT - 2, (EXT - 2) * 8, GROUPS * 128), jnp.bfloat16),
        ]
        + [VMEM(s, F32) for s in scratch] + [dma((n,)) for n in counts],
        compiler_params=pltpu.CompilerParams(
            vmem_limit_bytes=48 * 1024 * 1024, collective_id=0, has_side_effects=True
        ),
    )(
        log_conductivity, storage, recharge, *table, observed,
        pump_rate.reshape(1, 4), pump_well.reshape(1, 4),
    )


def solution(mesh):
    placed = (
        P("bx", "by", None), P("bx", "by", None), P("bx", "by", None), P("test"), P("test"),
        P("test", None), P(), P(), P(),
    )
    return jax.shard_map(
        local, mesh=mesh, in_specs=placed, out_specs=P("bx", "by", "test"), check_vma=False
    )
```

```python
import jax
import jax.numpy as jnp
from jax import lax
from jax.experimental import pallas as pl
from jax.experimental.pallas import tpu as pltpu
from jax.sharding import PartitionSpec as P

F32 = jnp.float32
MESH = pl.DeviceIdType.MESH
VMEM = pltpu.VMEM
HIGHEST = lax.Precision.HIGHEST
EPSILON = 1e-06
SCREEN = 8
SIDE = 8
HALO = 4
EXT = SIDE + 2 * HALO
NX_BRICKS, NY_BRICKS = 4, 16
ROUND = 4
TESTS_AXIS = 8
WELLS = 2048
OWN = 32
GROUPS = 7
DIRECTIONS = [(dx, dy) for dx in (-1, 0, 1) for dy in (-1, 0, 1)]
FACES = [(1, 0), (-1, 0), (0, 1), (0, -1)]
NEIGHBOURS = [(k, d) for k, d in enumerate(DIRECTIONS) if d != (0, 0)]


def iota(shape, dim):
    return lax.broadcasted_iota(jnp.int32, shape, dim)


def z_neighbours(values, fill):
    sub, lane = iota(values.shape, 1), iota(values.shape, 2)
    low = pltpu.roll(values, 1, 2)
    low = jnp.where(lane == 0, jnp.where(sub < 4, fill, pltpu.roll(low, 4, 1)), low)
    high = pltpu.roll(values, 127, 2)
    high = jnp.where(lane == 127, jnp.where(sub < 4, pltpu.roll(high, 4, 1), fill), high)
    return low, high


def around(ref, x, lo, hi, fill):
    low, high = z_neighbours(ref[x, lo:hi], fill)
    return (
        (ref[x - 1, lo:hi] + ref[x + 1, lo:hi])
        + (ref[x, lo - 1 : hi - 1] + ref[x, lo + 1 : hi + 1])
        + (low + high)
    )


def rows(lo, hi, body, group):
    def step(i, carry):
        for j in range(group):
            body(lo + i * group + j)
        return carry

    lax.fori_loop(0, (hi - lo) // group, step, 0)


def thirds(values):
    parts, rest = [], values
    for i in range(3):
        parts.append(rest.astype(jnp.bfloat16))
        rest = rest - parts[-1].astype(F32)
    return parts


def halves(ref, x, lo, hi, field):
    first = ref[x, lo:hi, 2 * field : 2 * field + 1, :]
    second = ref[x, lo:hi, 2 * field + 1 : 2 * field + 2, :]
    shape = (hi - lo, 8, 128)
    return jnp.where(
        iota(shape, 1) < 4, jnp.broadcast_to(first, shape), jnp.broadcast_to(second, shape)
    )


def inside(x, lo, hi):
    shape = (hi - lo, 8, 128)
    gx = lax.axis_index("bx") * SIDE + x - HALO + jnp.zeros(shape, jnp.int32)
    gy = lax.axis_index("by") * SIDE + lo - HALO + iota(shape, 0)
    return (gx >= 0) & (gx < NX_BRICKS * SIDE) & (gy >= 0) & (gy < NY_BRICKS * SIDE)


def neighbour(dx, dy):
    bx, by = lax.axis_index("bx"), lax.axis_index("by")
    return {
        "bx": lax.rem(bx + dx + NX_BRICKS, NX_BRICKS),
        "by": lax.rem(by + dy + NY_BRICKS, NY_BRICKS),
    }


def remote(source, target, send_sem, recv_sem, peer):
    copy = pltpu.make_async_remote_copy(
        src_ref=source, dst_ref=target, send_sem=send_sem, recv_sem=recv_sem,
        device_id=peer, device_id_type=MESH,
    )
    copy.start()
    return copy


def halo_copies(packed, ext, send_sems, recv_sems):
    me = lax.axis_index("test")
    core = lax.rem(me, 2)
    partner = {"test": me + 1 - 2 * core}
    deep = HALO - 1
    first, second = [], []
    half = pl.ds(SIDE // 2 * core, SIDE // 2)
    half_there = pl.ds(HALO + SIDE // 2 * core, SIDE // 2)
    corner = pl.ds((SIDE - deep) * core, deep)
    corner_there = pl.ds((HALO + SIDE) * (1 - core) + core, deep)
    for dy, from_y, to_y, skip in ((1, SIDE - deep, 1, 1), (-1, 0, HALO + SIDE, 0)):
        first.append(
            (half, pl.ds(from_y, deep), half_there, pl.ds(to_y, deep), neighbour(0, dy))
        )
        first.append(
            (corner, pl.ds(from_y + skip, deep - 1), corner_there, pl.ds(to_y + skip, deep - 1),
             neighbour(2 * core - 1, dy))
        )
    first = [first[0], first[2], first[1], first[3]]
    for dx, from_x, to_x in ((1, SIDE - HALO, 0), (-1, 0, HALO + SIDE)):
        second.append(
            (pl.ds(from_x, HALO), pl.ds(0, SIDE), pl.ds(to_x, HALO), pl.ds(HALO, SIDE),
             neighbour(dx, 0))
        )
    started = [
        remote(packed.at[x, y], ext.at[to_x, to_y], send_sems.at[k], recv_sems.at[k], peer)
        for k, (x, y, to_x, to_y, peer) in enumerate(first + second)
    ]

    def middle():
        for copy in started[len(first) :]:
            copy.wait()

    def finish():
        passed = []
        for k, (x, y, to_x, to_y, peer) in enumerate(first):
            started[k].wait_recv()
            block = ext.at[to_x, to_y]
            passed.append(remote(block, block, send_sems.at[6 + k], recv_sems.at[6 + k], partner))
        for copy in started[: len(first)]:
            copy.wait_send()
        for copy in passed:
            copy.wait()

    return middle, finish


def roots(ext, e_ref, lo, hi):
    def row(x):
        logs = halves(ext, x, lo, hi, 0)
        e_ref[x, lo:hi] = jnp.where(inside(x, lo, hi), jnp.exp(0.5 * logs), 1.0)

    rows(0, EXT, row, 4)


def terms(ext, e_ref, r_ref, alpha_ref, beta_ref, pump_cell, pump_tile, lo, hi):
    def row(x):
        e = e_ref[x, lo:hi]
        diagonal = halves(ext, x, lo, hi, 1) + e * around(e_ref, x, lo, hi, 1.0)
        r = jnp.where(inside(x, lo, hi), 1.0 / diagonal, 0.0)
        cell = x * EXT + lo + iota(e.shape, 0)
        source = halves(ext, x, lo, hi, 2) + jnp.where(pump_cell[None] == cell, pump_tile[None], 0.0)
        er = e * r
        r_ref[x, lo:hi] = r
        alpha_ref[x, lo:hi] = e * er
        beta_ref[x, lo:hi] = er * source

    rows(1, EXT - 1, row, 2)


def edge_roots(ext, e_ref):
    def edge(xs, y, source_y):
        count = xs.stop - xs.start
        shape = (count, 8, 128)
        first = ext[xs, source_y, 6:7, :]
        second = ext[xs, source_y, 7:8, :]
        logs = jnp.where(
            iota(shape, 1) < 4, jnp.broadcast_to(first, shape), jnp.broadcast_to(second, shape)
        )
        gx = lax.axis_index("bx") * SIDE + xs.start - HALO + iota(shape, 0)
        gy = lax.axis_index("by") * SIDE + y - HALO + jnp.zeros(shape, jnp.int32)
        ok = (gx >= 0) & (gx < NX_BRICKS * SIDE) & (gy >= 0) & (gy < NY_BRICKS * SIDE)
        e_ref[xs, y] = jnp.where(ok, jnp.exp(0.5 * logs), 1.0)

    middle = slice(HALO, HALO + SIDE)
    edge(middle, 0, 1)
    edge(middle, EXT - 1, EXT - 2)
    for x in (HALO - 1, HALO + SIDE):
        edge(slice(x, x + 1), 1, 2)
        edge(slice(x, x + 1), EXT - 2, EXT - 3)


def sweeps(e_ref, alpha_ref, beta_ref, u_ref, out_ref):
    def second(x):
        u_ref[x, 2 : EXT - 2] = beta_ref[x, 2 : EXT - 2] + alpha_ref[x, 2 : EXT - 2] * around(
            beta_ref, x, 2, EXT - 2, 0.0
        )

    rows(2, EXT - 2, second, 4)

    def third(x):
        u = beta_ref[x, 3 : EXT - 3] + alpha_ref[x, 3 : EXT - 3] * around(u_ref, x, 3, EXT - 3, 0.0)
        out_ref[x, 3 : EXT - 3] = u / e_ref[x, 3 : EXT - 3]

    rows(3, EXT - 3, third, 5)


def pumping(pump_rate, pump_well, owner, column, top):
    sub, lane = iota((8, 128), 0), iota((8, 128), 1)
    z = lane + jnp.where(sub < 4, 0, 128)
    cell = jnp.zeros((8, 128), jnp.int32)
    tile = jnp.zeros((8, 128), F32)
    first_x = lax.axis_index("bx") * SIDE - HALO
    first_y = lax.axis_index("by") * SIDE - HALO
    code = (owner[...] * 64 + column[...]) * 256 + top[...]
    code = code.astype(F32)
    index = iota((16, 128), 0) * 128 + iota((16, 128), 1)
    for t in range(4):
        well = jnp.broadcast_to(pump_well[0:1, t : t + 1], (16, 128))
        found = jnp.sum(jnp.where(index == well, code, 0.0), axis=0, keepdims=True)
        found = jnp.broadcast_to(jnp.sum(found, axis=1, keepdims=True), (8, 128)).astype(jnp.int32)
        brick, place, start = found >> 14, (found >> 8) & 63, found & 255
        x = (brick >> 4) * SIDE + (place >> 3) - first_x
        y = (brick & 15) * SIDE + (place & 7) - first_y
        ok = (x >= 0) & (x < EXT) & (y >= 0) & (y < EXT)
        mine = (sub & 3) == t
        cell = jnp.where(mine, jnp.where(ok, x * EXT + y, -1), cell)
        hit = mine & (z >= start) & (z < start + SCREEN)
        tile = jnp.where(hit, -jnp.broadcast_to(pump_rate[0:1, t : t + 1], (8, 128)), tile)
    return cell, tile


def pack(log_conductivity, storage, recharge, packed):
    def row(x):
        logs = log_conductivity[x]
        further = jnp.where(
            iota((SIDE, 256), 0) < 4, pltpu.roll(logs, SIDE - 1, 0), pltpu.roll(logs, 1, 0)
        )
        for field, values in enumerate((logs, storage[x], recharge[x], further)):
            packed[x, :, 2 * field, :] = values[:, :128]
            packed[x, :, 2 * field + 1, :] = values[:, 128:]

    rows(0, SIDE, row, 2)


def own_wells(owner, column, top, observed):
    brick = lax.axis_index("bx") * NY_BRICKS + lax.axis_index("by")
    mine = jnp.where(owner[...] == brick, 1.0, 0.0)
    upto = jnp.where(iota((128, 128), 0) <= iota((128, 128), 1), 1.0, 0.0)
    inner = jnp.dot(mine, upto, precision=HIGHEST, preferred_element_type=F32)
    count = jnp.broadcast_to(jnp.sum(mine, axis=1, keepdims=True), (16, 128))
    before = jnp.where(iota((16, 16), 1) < iota((16, 16), 0), 1.0, 0.0)
    rank = inner + jnp.dot(before, count, precision=HIGHEST, preferred_element_type=F32) - 1.0
    rank = jnp.where(mine > 0.0, rank, -1.0)
    place = iota((OWN, 128), 0).astype(F32)
    sums = [jnp.zeros((OWN, 128), F32) for field in range(6)]
    for k in range(16):
        hit = jnp.broadcast_to(rank[k : k + 1, :], (OWN, 128)) == place
        values = [column[k : k + 1, :].astype(F32), top[k : k + 1, :].astype(F32)]
        values += [observed[t : t + 1, k * 128 : (k + 1) * 128] for t in range(4)]
        for field in range(6):
            sums[field] = sums[field] + jnp.where(
                hit, jnp.broadcast_to(values[field], (OWN, 128)), 0.0
            )
    return [jnp.sum(s, axis=1, keepdims=True) for s in sums]


def residuals(heads_ref, wells, message, squares):
    column, top, observed = wells[0], wells[1], wells[2:]
    column2 = jnp.concatenate([column, column], axis=0)
    top2 = jnp.concatenate([top, top], axis=0)
    half = iota((2 * OWN, 128), 0) // OWN
    z = (iota((2 * OWN, 128), 1) + 128 * half).astype(F32)
    screen = jnp.where((z >= top2) & (z < top2 + SCREEN), 1.0, 0.0)
    heads = heads_ref[HALO : HALO + SIDE, HALO : HALO + SIDE].reshape(512, 128)
    screen = screen.astype(jnp.bfloat16)
    sums = lax.dot_general(
        jnp.concatenate([screen] * 3, axis=1), jnp.concatenate(thirds(heads), axis=1),
        (((1,), (1,)), ((), ())), preferred_element_type=F32,
    )
    at = iota((2 * OWN, 512), 1)
    keep = ((at >> 3).astype(F32) == column2) & (
        ((at >> 2) & 1) == iota((2 * OWN, 512), 0) // OWN
    )
    sums = jnp.where(keep, sums, 0.0)
    pick = jnp.where((iota((512, 128), 0) & 3) == iota((512, 128), 1), 1.0, 0.0)
    pick = pick.astype(jnp.bfloat16)
    sums = sum(jnp.dot(part, pick, preferred_element_type=F32) for part in thirds(sums))
    sums = (sums[:OWN] + sums[OWN:]) * (1.0 / SCREEN)
    lane = iota((OWN, 128), 1)
    for t in range(4):
        sums = jnp.where(lane == t, sums - observed[t], sums)
    sums = jnp.where(lane == 4, column, sums)
    sums = jnp.where(lane == 5, top, sums)
    eye = jnp.where(iota((8, 128), 0) == iota((8, 128), 1), 1.0, 0.0)
    turned = lax.dot_general(
        eye, sums, (((1,), (1,)), ((), ())), precision=HIGHEST, preferred_element_type=F32
    )
    message[...] = jnp.concatenate([turned, jnp.zeros((8, 128 - OWN), F32)], axis=1)
    total = jnp.broadcast_to(jnp.sum(turned * turned, axis=1, keepdims=True), (8, 128))
    squares[...] = jnp.where(iota((8, 128), 0) < 4, total, pltpu.roll(total, 4, 0))


def adjoint_source(messages, e_ref, r_ref, beta_ref, lhs):
    sub, lane = iota((8, 128), 0), iota((8, 128), 1)
    values = [jnp.zeros((8, 128), F32) for g in range(GROUPS)]
    cells = [jnp.zeros((8, 128), F32) for g in range(GROUPS)]
    tops = [jnp.zeros((8, 128), F32) for g in range(GROUPS)]
    for k, (dx, dy) in enumerate(DIRECTIONS):
        tile = messages[k]
        value = jnp.where(sub < 4, tile, pltpu.roll(tile, 4, 0))
        column = jnp.broadcast_to(tile[4:5], (8, 128))
        along = jnp.floor(column * (1.0 / SIDE))
        x = along + (HALO + SIDE * dx)
        y = column - along * SIDE + (HALO + SIDE * dy)
        ok = (x >= 1) & (x < EXT - 1) & (y >= 1) & (y < EXT - 1) & (lane < OWN)
        cell = jnp.where(ok, x * EXT + y, 0.0)
        top = jnp.where(lane < OWN, jnp.broadcast_to(tile[5:6], (8, 128)), 0.0)
        for p, part in enumerate(thirds(value)):
            g, shift = (3 * k + p) // 4, OWN * ((3 * k + p) % 4)
            moved = [part.astype(F32), cell, top]
            if shift:
                moved = [pltpu.roll(v, shift, 1) for v in moved]
            values[g], cells[g], tops[g] = values[g] + moved[0], cells[g] + moved[1], tops[g] + moved[2]
    z = iota((256, 128), 0).astype(F32)
    screens = []
    for g in range(GROUPS):
        top = jnp.broadcast_to(tops[g][0:1], (256, 128))
        screens.append(jnp.where((z >= top) & (z < top + SCREEN), 1.0, 0.0).astype(jnp.bfloat16))
    screen = jnp.concatenate(screens, axis=1)
    wide = EXT - 2
    shape = (wide, 8, 128)
    lo, hi = 1, EXT - 1

    def left(x):
        cell = (x * EXT + 1 + iota(shape, 0)).astype(F32)
        for g in range(GROUPS):
            lhs[x - 1, :, g * 128 : (g + 1) * 128] = (
                jnp.where(cells[g][None] == cell, values[g][None], 0.0)
                .reshape(wide * 8, 128)
                .astype(jnp.bfloat16)
            )

    rows(lo, hi, left, 2)
    group = 7
    for first in range(0, wide, group):
        block = lhs[first : first + group].reshape(group * wide * 8, GROUPS * 128)
        both = lax.dot_general(
            block, screen, (((1,), (1,)), ((), ())), preferred_element_type=F32
        )
        pair = both.reshape(group, wide, 8, 256)
        for i in range(group):
            source = jnp.where(iota(shape, 1) < 4, pair[i, :, :, :128], pair[i, :, :, 128:])
            x = first + i + 1
            beta_ref[x, lo:hi] = e_ref[x, lo:hi] * r_ref[x, lo:hi] * source


def head_steps(e_ref, heads_ref, steps_ref):
    lo, hi = HALO, HALO + SIDE

    def row(x):
        h, e = heads_ref[x, lo:hi], e_ref[x, lo:hi]
        for f, (step_x, step_y) in enumerate(FACES):
            at = (x + step_x, slice(lo + step_y, hi + step_y))
            steps_ref[f, x - HALO] = e * e_ref[at] * (h - heads_ref[at])
        for f, (e_n, h_n) in enumerate(zip(z_neighbours(e, 1.0), z_neighbours(h, 0.0))):
            steps_ref[4 + f, x - HALO] = e * e_n * (h - h_n)

    rows(lo, hi, row, 2)


def sensitivity(steps_ref, adjoint_ref, scale, out_ref):
    lo, hi = HALO, HALO + SIDE

    def row(x):
        a = adjoint_ref[x, lo:hi]
        total = jnp.zeros_like(a)
        for f, (step_x, step_y) in enumerate(FACES):
            total = total + steps_ref[f, x - HALO] * (
                a - adjoint_ref[x + step_x, lo + step_y : hi + step_y]
            )
        for f, a_n in enumerate(z_neighbours(a, 0.0)):
            total = total + steps_ref[4 + f, x - HALO] * (a - a_n)
        total = total * scale[None]
        total = total + pltpu.roll(total, 7, 1)
        out_ref[x - HALO] = total + pltpu.roll(total, 6, 1)

    rows(lo, hi, row, 4)


def slabs(sum_ref, out):
    lane = iota((8, 128), 1)
    for half in range(2):
        planes = sum_ref[:, :, 4 * half, :]
        for q in range(4):
            for xq in range(2):
                packed = jnp.zeros((8, 128), F32)
                for xx in range(4):
                    plane = planes[4 * xq + xx]
                    shift = (32 * (xx - q)) % 128
                    if shift:
                        plane = pltpu.roll(plane, shift, 1)
                    packed = jnp.where((lane >> 5) == xx, plane, packed)
                out[4 * half + q, xq] = packed


def kernel(
    log_hbm, storage_hbm, recharge_hbm, owner_hbm, column_hbm, top_hbm, observed_hbm,
    pump_rate, pump_well, out,
    log_conductivity, storage, recharge, owner, column, top, observed, load_sems,
    packed, steps_ref, lhs, ext, e_ref, r_ref, alpha_ref, heads_ref, beta_ref, u_ref, adjoint_ref, sum_ref,
    message, squares, messages, near, partial, far, parts, slots,
    halo_send, halo_recv, msg_send, msg_recv, near_send, near_recv, far_send, far_recv,
    part_send, part_recv,
):
    pairs = (
        (log_hbm, log_conductivity), (storage_hbm, storage), (recharge_hbm, recharge),
        (owner_hbm, owner), (column_hbm, column), (top_hbm, top), (observed_hbm, observed),
    )
    loads = [
        pltpu.make_async_copy(there, here, load_sems.at[i]) for i, (there, here) in enumerate(pairs)
    ]
    for copy in loads:
        copy.start()
    me, bx, by = lax.axis_index("test"), lax.axis_index("bx"), lax.axis_index("by")
    turn, place = by // ROUND, lax.rem(by, ROUND)
    neighbours = [neighbour(dx, dy) for k, (dx, dy) in NEIGHBOURS]
    near_peers = [
        {
            "bx": lax.rem(bx + a, NX_BRICKS),
            "by": turn * ROUND + lax.rem(place + b, ROUND),
        }
        for a in range(NX_BRICKS) for b in range(ROUND) if a + b > 0
    ]
    far_peers = [
        {"by": lax.rem(by + c * ROUND, NY_BRICKS)} for c in range(1, NY_BRICKS // ROUND)
    ]
    test_peers = [lax.rem(me + d, TESTS_AXIS) for d in range(1, TESTS_AXIS)]
    for cx in (0, HALO + SIDE):
        for cy in (0, HALO + SIDE):
            ext[cx : cx + HALO, cy : cy + HALO] = jnp.zeros((HALO, HALO, 8, 128), F32)
    everyone = far_peers + neighbours + near_peers + [{"test": peer} for peer in test_peers]
    barrier = pltpu.get_barrier_semaphore()
    for peer in everyone:
        pl.semaphore_signal(barrier, inc=1, device_id=peer, device_id_type=MESH)
    for copy in loads[:3]:
        copy.wait()
    pack(log_conductivity, storage, recharge, packed)
    pl.semaphore_wait(barrier, len(everyone))
    middle_halo, finish_halo = halo_copies(packed, ext, halo_send, halo_recv)
    ext[HALO : HALO + SIDE, HALO : HALO + SIDE] = packed[...]
    for copy in loads[3:]:
        copy.wait()
    pump_cell, pump_tile = pumping(pump_rate, pump_well, owner, column, top)
    wells = own_wells(owner, column, top, observed)
    fields = (ext, e_ref, r_ref, alpha_ref, beta_ref, pump_cell, pump_tile)
    middle_halo()
    roots(ext, e_ref, HALO, HALO + SIDE)
    terms(*fields, HALO + 1, HALO + SIDE - 1)
    finish_halo()
    roots(ext, e_ref, 0, HALO)
    roots(ext, e_ref, HALO + SIDE, EXT)
    edge_roots(ext, e_ref)
    terms(*fields, 1, HALO + 1)
    terms(*fields, HALO + SIDE - 1, EXT - 1)
    sweeps(e_ref, alpha_ref, beta_ref, u_ref, heads_ref)
    residuals(heads_ref, wells, message, squares)
    near_copies = [
        remote(squares, near.at[i], near_send.at[i], near_recv.at[i], peer)
        for i, peer in enumerate(near_peers)
    ]
    copies = [
        remote(message, messages.at[8 - k], msg_send.at[k], msg_recv.at[k], neighbour(dx, dy))
        for k, (dx, dy) in NEIGHBOURS
    ]
    messages[4] = message[...]
    for copy in near_copies:
        copy.wait()
    here = squares[...]
    for i in range(len(near_peers)):
        here = here + near[i]
    partial[...] = here
    far_copies = [
        remote(partial, far.at[i], far_send.at[i], far_recv.at[i], peer)
        for i, peer in enumerate(far_peers)
    ]
    head_steps(e_ref, heads_ref, steps_ref)
    for copy in copies:
        copy.wait()
    adjoint_source(messages, e_ref, r_ref, beta_ref, lhs)
    sweeps(e_ref, alpha_ref, beta_ref, u_ref, adjoint_ref)
    for copy in far_copies:
        copy.wait()
    total = partial[...]
    for i in range(len(far_peers)):
        total = total + far[i]
    scale = (-0.5 / (4 * TESTS_AXIS)) / (total / WELLS + EPSILON)
    sensitivity(steps_ref, adjoint_ref, scale, sum_ref)
    slabs(sum_ref, parts)
    part_copies = [
        remote(parts.at[peer], slots.at[i], part_send.at[i], part_recv.at[i], {"test": peer})
        for i, peer in enumerate(test_peers)
    ]
    for copy in part_copies:
        copy.wait()
    total = parts[me]
    for i in range(TESTS_AXIS - 1):
        total = total + slots[i]
    for xq in range(2):
        for xx in range(4):
            plane = total[xq]
            if xx:
                plane = pltpu.roll(plane, 128 - 32 * xx, 1)
            out[4 * xq + xx] = plane[:, :32]


def local(
    log_conductivity, storage, recharge, pump_rate, pump_well, observed, owner, screen_column, screen_top
):
    dma = pltpu.SemaphoreType.DMA
    field = (EXT, EXT, 8, 128)
    tile = (8, 128)
    table = [a.reshape(16, 128) for a in (owner, screen_column, screen_top)]
    near, far = NX_BRICKS * ROUND - 1, NY_BRICKS // ROUND - 1
    scratch = [field] * 8 + [
        (SIDE, SIDE) + tile, tile, tile, (9,) + tile,
        (near,) + tile, tile, (far,) + tile, (TESTS_AXIS, 2) + tile, (TESTS_AXIS - 1, 2) + tile,
    ]
    counts = (10, 10, 9, 9, near, near, far, far, TESTS_AXIS - 1, TESTS_AXIS - 1)
    return pl.pallas_call(
        kernel,
        out_shape=jax.ShapeDtypeStruct((SIDE, SIDE, 32), F32),
        in_specs=[pl.BlockSpec(memory_space=pltpu.HBM)] * 7
        + [pl.BlockSpec(memory_space=VMEM)] * 2,
        out_specs=pl.BlockSpec(memory_space=VMEM),
        scratch_shapes=[VMEM((SIDE, SIDE, 256), F32)] * 3
        + [VMEM((16, 128), jnp.int32)] * 3
        + [VMEM((4, WELLS), F32), dma((7,))]
        + [
            VMEM((SIDE, SIDE) + tile, F32),
            VMEM((6, SIDE, SIDE) + tile, F32),
            VMEM((EXT - 2, (EXT - 2) * 8, GROUPS * 128), jnp.bfloat16),
        ]
        + [VMEM(s, F32) for s in scratch] + [dma((n,)) for n in counts],
        compiler_params=pltpu.CompilerParams(
            vmem_limit_bytes=67_043_328, collective_id=0, has_side_effects=True
        ),
    )(
        log_conductivity, storage, recharge, *table, observed,
        pump_rate.reshape(1, 4), pump_well.reshape(1, 4),
    )


def solution(mesh):
    placed = (
        P("bx", "by", None), P("bx", "by", None), P("bx", "by", None), P("test"), P("test"),
        P("test", None), P(), P(), P(),
    )
    return jax.shard_map(
        local, mesh=mesh, in_specs=placed, out_specs=P("bx", "by", "test"), check_vma=False
    )
```

```python
import jax
import jax.numpy as jnp
from jax import lax
from jax.experimental import pallas as pl
from jax.experimental.pallas import tpu as pltpu
from jax.sharding import PartitionSpec as P

F32 = jnp.float32
MESH = pl.DeviceIdType.MESH
VMEM = pltpu.VMEM
HIGHEST = lax.Precision.HIGHEST
EPSILON = 1e-06
SCREEN = 8
SIDE = 8
HALO = 4
EXT = SIDE + 2 * HALO
NX_BRICKS, NY_BRICKS = 4, 16
ROUND = 4
TESTS_AXIS = 8
WELLS = 2048
OWN = 32
GROUPS = 7
DIRECTIONS = [(dx, dy) for dx in (-1, 0, 1) for dy in (-1, 0, 1)]
FACES = [(1, 0), (-1, 0), (0, 1), (0, -1)]
NEIGHBOURS = [(k, d) for k, d in enumerate(DIRECTIONS) if d != (0, 0)]


def iota(shape, dim):
    return lax.broadcasted_iota(jnp.int32, shape, dim)


def z_neighbours(values, fill):
    sub, lane = iota(values.shape, 1), iota(values.shape, 2)
    low = pltpu.roll(values, 1, 2)
    low = jnp.where(lane == 0, jnp.where(sub < 4, fill, pltpu.roll(low, 4, 1)), low)
    high = pltpu.roll(values, 127, 2)
    high = jnp.where(lane == 127, jnp.where(sub < 4, pltpu.roll(high, 4, 1), fill), high)
    return low, high


def around(ref, x, lo, hi, fill):
    low, high = z_neighbours(ref[x, lo:hi], fill)
    return (
        (ref[x - 1, lo:hi] + ref[x + 1, lo:hi])
        + (ref[x, lo - 1 : hi - 1] + ref[x, lo + 1 : hi + 1])
        + (low + high)
    )


def rows(lo, hi, body, group):
    def step(i, carry):
        for j in range(group):
            body(lo + i * group + j)
        return carry

    lax.fori_loop(0, (hi - lo) // group, step, 0)


def thirds(values):
    parts, rest = [], values
    for i in range(3):
        parts.append(rest.astype(jnp.bfloat16))
        rest = rest - parts[-1].astype(F32)
    return parts


def halves(ref, x, lo, hi, field):
    first = ref[x, lo:hi, 2 * field : 2 * field + 1, :]
    second = ref[x, lo:hi, 2 * field + 1 : 2 * field + 2, :]
    shape = (hi - lo, 8, 128)
    return jnp.where(
        iota(shape, 1) < 4, jnp.broadcast_to(first, shape), jnp.broadcast_to(second, shape)
    )


def inside(x, lo, hi):
    shape = (hi - lo, 8, 128)
    gx = lax.axis_index("bx") * SIDE + x - HALO + jnp.zeros(shape, jnp.int32)
    gy = lax.axis_index("by") * SIDE + lo - HALO + iota(shape, 0)
    return (gx >= 0) & (gx < NX_BRICKS * SIDE) & (gy >= 0) & (gy < NY_BRICKS * SIDE)


def neighbour(dx, dy):
    bx, by = lax.axis_index("bx"), lax.axis_index("by")
    return {
        "bx": lax.rem(bx + dx + NX_BRICKS, NX_BRICKS),
        "by": lax.rem(by + dy + NY_BRICKS, NY_BRICKS),
    }


def remote(source, target, send_sem, recv_sem, peer):
    copy = pltpu.make_async_remote_copy(
        src_ref=source, dst_ref=target, send_sem=send_sem, recv_sem=recv_sem,
        device_id=peer, device_id_type=MESH,
    )
    copy.start()
    return copy


def halo_copies(packed, ext, send_sems, recv_sems):
    me = lax.axis_index("test")
    core = lax.rem(me, 2)
    partner = {"test": me + 1 - 2 * core}
    half = pl.ds(SIDE // 2 * core, SIDE // 2)
    half_there = pl.ds(HALO + SIDE // 2 * core, SIDE // 2)

    def along_x(near, far):
        count = far - near + 1
        here = (near - 1) * (1 - core) + (SIDE - far) * core
        there = (HALO + SIDE + near - 1) * (1 - core) + (HALO - far) * core
        return pl.ds(here, count), pl.ds(there, count)

    def along_y(dy, near, far):
        count = far - near + 1
        if dy > 0:
            return pl.ds(SIDE - far, count), pl.ds(HALO - far, count)
        return pl.ds(near - 1, count), pl.ds(HALO + SIDE + near - 1, count)

    def block(xs, dy, near, far, dx):
        ys = along_y(dy, near, far)
        return xs[0], ys[0], xs[1], ys[1], neighbour(dx, dy)

    face, side = (half, half_there), 2 * core - 1
    near = [block(face, dy, 1, 2, 0) for dy in (1, -1)]
    near += [block(along_x(1, 2), dy, 1, 1, side) for dy in (1, -1)]
    outer = [block(face, dy, 3, 3, 0) for dy in (1, -1)]
    outer += [block(along_x(1, 3), dy, 2, 2, side) for dy in (1, -1)]
    outer += [block(along_x(3, 3), dy, 1, 1, side) for dy in (1, -1)]
    across = [
        (pl.ds(from_x, HALO), pl.ds(0, SIDE), pl.ds(to_x, HALO), pl.ds(HALO, SIDE), neighbour(dx, 0))
        for dx, from_x, to_x in ((1, SIDE - HALO, 0), (-1, 0, HALO + SIDE))
    ]
    plan = near + across + outer
    started = [
        remote(packed.at[x, y], ext.at[to_x, to_y], send_sems.at[k], recv_sems.at[k], peer)
        for k, (x, y, to_x, to_y, peer) in enumerate(plan)
    ]

    def middle():
        for copy in started[4:6]:
            copy.wait()

    def finish(lo, hi):
        passed = []
        for k in range(lo, hi):
            x, y, to_x, to_y, peer = plan[k]
            started[k].wait_recv()
            block = ext.at[to_x, to_y]
            passed.append(remote(block, block, send_sems.at[12 + k], recv_sems.at[12 + k], partner))
        for copy in started[lo:hi]:
            copy.wait_send()
        for copy in passed:
            copy.wait()

    return middle, lambda: finish(0, 4), lambda: finish(6, 12)


def roots(ext, e_ref, lo, hi, first=0, last=EXT, group=4):
    def row(x):
        logs = halves(ext, x, lo, hi, 0)
        e_ref[x, lo:hi] = jnp.where(inside(x, lo, hi), jnp.exp(0.5 * logs), 1.0)

    rows(first, last, row, group)


def terms(ext, e_ref, r_ref, alpha_ref, beta_ref, pump_cell, pump_tile, lo, hi, first=1, last=EXT - 1):
    def row(x):
        e = e_ref[x, lo:hi]
        diagonal = halves(ext, x, lo, hi, 1) + e * around(e_ref, x, lo, hi, 1.0)
        r = jnp.where(inside(x, lo, hi), 1.0 / diagonal, 0.0)
        cell = x * EXT + lo + iota(e.shape, 0)
        source = halves(ext, x, lo, hi, 2) + jnp.where(pump_cell[None] == cell, pump_tile[None], 0.0)
        er = e * r
        r_ref[x, lo:hi] = r
        alpha_ref[x, lo:hi] = e * er
        beta_ref[x, lo:hi] = er * source

    rows(first, last, row, 2)


def edge(ext, e_ref, xs, y, source_y):
    count = xs.stop - xs.start
    shape = (count, 8, 128)
    first = ext[xs, source_y, 6:7, :]
    second = ext[xs, source_y, 7:8, :]
    logs = jnp.where(
        iota(shape, 1) < 4, jnp.broadcast_to(first, shape), jnp.broadcast_to(second, shape)
    )
    gx = lax.axis_index("bx") * SIDE + xs.start - HALO + iota(shape, 0)
    gy = lax.axis_index("by") * SIDE + y - HALO + jnp.zeros(shape, jnp.int32)
    ok = (gx >= 0) & (gx < NX_BRICKS * SIDE) & (gy >= 0) & (gy < NY_BRICKS * SIDE)
    e_ref[xs, y] = jnp.where(ok, jnp.exp(0.5 * logs), 1.0)


MIDDLE = slice(HALO, HALO + SIDE)


def edge_roots(ext, e_ref):
    edge(ext, e_ref, MIDDLE, 0, 1)
    edge(ext, e_ref, MIDDLE, EXT - 1, EXT - 2)
    for x in (HALO - 1, HALO + SIDE):
        edge(ext, e_ref, slice(x, x + 1), 1, 2)
        edge(ext, e_ref, slice(x, x + 1), EXT - 2, EXT - 3)


def near_coefficients(fields):
    ext, e_ref = fields[:2]
    lo, hi = HALO, HALO + SIDE
    for first, last in ((lo - 2, lo), (hi, hi + 2)):
        roots(ext, e_ref, first, last, lo, hi)
        for column in (lo - 1, hi):
            roots(ext, e_ref, column, column + 1, first, last, 2)
    edge(ext, e_ref, MIDDLE, lo - 3, lo - 2)
    edge(ext, e_ref, MIDDLE, hi + 2, hi + 1)
    for x in (lo - 1, hi):
        edge(ext, e_ref, slice(x, x + 1), lo - 2, lo - 1)
        edge(ext, e_ref, slice(x, x + 1), hi + 1, hi)
    terms(*fields, lo - 2, lo + 1, lo, hi)
    terms(*fields, hi - 1, hi + 2, lo, hi)
    for first in (lo - 2, hi):
        terms(*fields, lo - 1, lo + 1, first, first + 2)
        terms(*fields, hi - 1, hi + 1, first, first + 2)


def sweeps(e_ref, alpha_ref, beta_ref, u_ref, out_ref, first):
    def second(x):
        u_ref[x, first : EXT - first] = beta_ref[x, first : EXT - first] + alpha_ref[
            x, first : EXT - first
        ] * around(beta_ref, x, first, EXT - first, 0.0)

    rows(first, EXT - first, second, 2)
    lo, hi = first + 1, EXT - first - 1

    def third(x):
        u = beta_ref[x, lo:hi] + alpha_ref[x, lo:hi] * around(u_ref, x, lo, hi, 0.0)
        out_ref[x, lo:hi] = u / e_ref[x, lo:hi]

    rows(lo, hi, third, 2)


def pumping(pump_rate, pump_well, owner, column, top):
    sub, lane = iota((8, 128), 0), iota((8, 128), 1)
    z = lane + jnp.where(sub < 4, 0, 128)
    cell = jnp.zeros((8, 128), jnp.int32)
    tile = jnp.zeros((8, 128), F32)
    first_x = lax.axis_index("bx") * SIDE - HALO
    first_y = lax.axis_index("by") * SIDE - HALO
    code = (owner[...] * 64 + column[...]) * 256 + top[...]
    code = code.astype(F32)
    index = iota((16, 128), 0) * 128 + iota((16, 128), 1)
    for t in range(4):
        well = jnp.broadcast_to(pump_well[0:1, t : t + 1], (16, 128))
        found = jnp.sum(jnp.where(index == well, code, 0.0), axis=0, keepdims=True)
        found = jnp.broadcast_to(jnp.sum(found, axis=1, keepdims=True), (8, 128)).astype(jnp.int32)
        brick, place, start = found >> 14, (found >> 8) & 63, found & 255
        x = (brick >> 4) * SIDE + (place >> 3) - first_x
        y = (brick & 15) * SIDE + (place & 7) - first_y
        ok = (x >= 0) & (x < EXT) & (y >= 0) & (y < EXT)
        mine = (sub & 3) == t
        cell = jnp.where(mine, jnp.where(ok, x * EXT + y, -1), cell)
        hit = mine & (z >= start) & (z < start + SCREEN)
        tile = jnp.where(hit, -jnp.broadcast_to(pump_rate[0:1, t : t + 1], (8, 128)), tile)
    return cell, tile


def pack(log_conductivity, storage, recharge, packed):
    def row(x):
        logs = log_conductivity[x]
        further = jnp.where(
            iota((SIDE, 256), 0) < 4, pltpu.roll(logs, SIDE - 1, 0), pltpu.roll(logs, 1, 0)
        )
        for field, values in enumerate((logs, storage[x], recharge[x], further)):
            packed[x, :, 2 * field, :] = values[:, :128]
            packed[x, :, 2 * field + 1, :] = values[:, 128:]

    rows(0, SIDE, row, 2)


def own_wells(owner, column, top, observed):
    brick = lax.axis_index("bx") * NY_BRICKS + lax.axis_index("by")
    mine = jnp.where(owner[...] == brick, 1.0, 0.0)
    upto = jnp.where(iota((128, 128), 0) <= iota((128, 128), 1), 1.0, 0.0)
    inner = jnp.dot(mine, upto, precision=HIGHEST, preferred_element_type=F32)
    count = jnp.broadcast_to(jnp.sum(mine, axis=1, keepdims=True), (16, 128))
    before = jnp.where(iota((16, 16), 1) < iota((16, 16), 0), 1.0, 0.0)
    rank = inner + jnp.dot(before, count, precision=HIGHEST, preferred_element_type=F32) - 1.0
    rank = jnp.where(mine > 0.0, rank, -1.0)
    place = iota((OWN, 128), 0).astype(F32)
    sums = [jnp.zeros((OWN, 128), F32) for field in range(6)]
    for k in range(16):
        hit = jnp.broadcast_to(rank[k : k + 1, :], (OWN, 128)) == place
        values = [column[k : k + 1, :].astype(F32), top[k : k + 1, :].astype(F32)]
        values += [observed[t : t + 1, k * 128 : (k + 1) * 128] for t in range(4)]
        for field in range(6):
            sums[field] = sums[field] + jnp.where(
                hit, jnp.broadcast_to(values[field], (OWN, 128)), 0.0
            )
    return [jnp.sum(s, axis=1, keepdims=True) for s in sums]


def residuals(heads_ref, wells, message, squares):
    column, top, observed = wells[0], wells[1], wells[2:]
    column2 = jnp.concatenate([column, column], axis=0)
    top2 = jnp.concatenate([top, top], axis=0)
    half = iota((2 * OWN, 128), 0) // OWN
    z = (iota((2 * OWN, 128), 1) + 128 * half).astype(F32)
    screen = jnp.where((z >= top2) & (z < top2 + SCREEN), 1.0, 0.0)
    heads = heads_ref[HALO : HALO + SIDE, HALO : HALO + SIDE].reshape(512, 128)
    screen = screen.astype(jnp.bfloat16)
    sums = lax.dot_general(
        jnp.concatenate([screen] * 3, axis=1), jnp.concatenate(thirds(heads), axis=1),
        (((1,), (1,)), ((), ())), preferred_element_type=F32,
    )
    at = iota((2 * OWN, 512), 1)
    keep = ((at >> 3).astype(F32) == column2) & (
        ((at >> 2) & 1) == iota((2 * OWN, 512), 0) // OWN
    )
    sums = jnp.where(keep, sums, 0.0)
    pick = jnp.where((iota((512, 128), 0) & 3) == iota((512, 128), 1), 1.0, 0.0)
    pick = pick.astype(jnp.bfloat16)
    sums = sum(jnp.dot(part, pick, preferred_element_type=F32) for part in thirds(sums))
    sums = (sums[:OWN] + sums[OWN:]) * (1.0 / SCREEN)
    lane = iota((OWN, 128), 1)
    for t in range(4):
        sums = jnp.where(lane == t, sums - observed[t], sums)
    sums = jnp.where(lane == 4, column, sums)
    sums = jnp.where(lane == 5, top, sums)
    eye = jnp.where(iota((8, 128), 0) == iota((8, 128), 1), 1.0, 0.0)
    turned = lax.dot_general(
        eye, sums, (((1,), (1,)), ((), ())), precision=HIGHEST, preferred_element_type=F32
    )
    message[...] = jnp.concatenate([turned, jnp.zeros((8, 128 - OWN), F32)], axis=1)
    total = jnp.broadcast_to(jnp.sum(turned * turned, axis=1, keepdims=True), (8, 128))
    squares[...] = jnp.where(iota((8, 128), 0) < 4, total, pltpu.roll(total, 4, 0))


def adjoint_source(messages, e_ref, r_ref, beta_ref, lhs):
    sub, lane = iota((8, 128), 0), iota((8, 128), 1)
    values = [jnp.zeros((8, 128), F32) for g in range(GROUPS)]
    cells = [jnp.zeros((8, 128), F32) for g in range(GROUPS)]
    tops = [jnp.zeros((8, 128), F32) for g in range(GROUPS)]
    for k, (dx, dy) in enumerate(DIRECTIONS):
        tile = messages[k]
        value = jnp.where(sub < 4, tile, pltpu.roll(tile, 4, 0))
        column = jnp.broadcast_to(tile[4:5], (8, 128))
        along = jnp.floor(column * (1.0 / SIDE))
        x = along + (HALO + SIDE * dx)
        y = column - along * SIDE + (HALO + SIDE * dy)
        ok = (x >= 1) & (x < EXT - 1) & (y >= 1) & (y < EXT - 1) & (lane < OWN)
        cell = jnp.where(ok, x * EXT + y, 0.0)
        top = jnp.where(lane < OWN, jnp.broadcast_to(tile[5:6], (8, 128)), 0.0)
        for p, part in enumerate(thirds(value)):
            g, shift = (3 * k + p) // 4, OWN * ((3 * k + p) % 4)
            moved = [part.astype(F32), cell, top]
            if shift:
                moved = [pltpu.roll(v, shift, 1) for v in moved]
            values[g], cells[g], tops[g] = values[g] + moved[0], cells[g] + moved[1], tops[g] + moved[2]
    z = iota((256, 128), 0).astype(F32)
    screens = []
    for g in range(GROUPS):
        top = jnp.broadcast_to(tops[g][0:1], (256, 128))
        screens.append(jnp.where((z >= top) & (z < top + SCREEN), 1.0, 0.0).astype(jnp.bfloat16))
    screen = jnp.concatenate(screens, axis=1)
    wide = EXT - 2
    shape = (wide, 8, 128)
    lo, hi = 1, EXT - 1

    def left(x):
        cell = (x * EXT + 1 + iota(shape, 0)).astype(F32)
        for g in range(GROUPS):
            lhs[x - 1, :, g * 128 : (g + 1) * 128] = (
                jnp.where(cells[g][None] == cell, values[g][None], 0.0)
                .reshape(wide * 8, 128)
                .astype(jnp.bfloat16)
            )

    rows(lo, hi, left, 2)
    group = 7
    for first in range(0, wide, group):
        block = lhs[first : first + group].reshape(group * wide * 8, GROUPS * 128)
        both = lax.dot_general(
            block, screen, (((1,), (1,)), ((), ())), preferred_element_type=F32
        )
        pair = both.reshape(group, wide, 8, 256)
        for i in range(group):
            source = jnp.where(iota(shape, 1) < 4, pair[i, :, :, :128], pair[i, :, :, 128:])
            x = first + i + 1
            beta_ref[x, lo:hi] = e_ref[x, lo:hi] * r_ref[x, lo:hi] * source


def head_steps(e_ref, heads_ref, steps_ref):
    lo, hi = HALO, HALO + SIDE

    def row(x):
        h, e = heads_ref[x, lo:hi], e_ref[x, lo:hi]
        for f, (step_x, step_y) in enumerate(FACES):
            at = (x + step_x, slice(lo + step_y, hi + step_y))
            steps_ref[f, x - HALO] = e * e_ref[at] * (h - heads_ref[at])
        for f, (e_n, h_n) in enumerate(zip(z_neighbours(e, 1.0), z_neighbours(h, 0.0))):
            steps_ref[4 + f, x - HALO] = e * e_n * (h - h_n)

    rows(lo, hi, row, 2)


def sensitivity(steps_ref, adjoint_ref, scale, out_ref):
    lo, hi = HALO, HALO + SIDE

    def row(x):
        a = adjoint_ref[x, lo:hi]
        total = jnp.zeros_like(a)
        for f, (step_x, step_y) in enumerate(FACES):
            total = total + steps_ref[f, x - HALO] * (
                a - adjoint_ref[x + step_x, lo + step_y : hi + step_y]
            )
        for f, a_n in enumerate(z_neighbours(a, 0.0)):
            total = total + steps_ref[4 + f, x - HALO] * (a - a_n)
        total = total * scale[None]
        total = total + pltpu.roll(total, 7, 1)
        out_ref[x - HALO] = total + pltpu.roll(total, 6, 1)

    rows(lo, hi, row, 4)


def slabs(sum_ref, out):
    lane = iota((8, 128), 1)
    for half in range(2):
        planes = sum_ref[:, :, 4 * half, :]
        for q in range(4):
            for xq in range(2):
                packed = jnp.zeros((8, 128), F32)
                for xx in range(4):
                    plane = planes[4 * xq + xx]
                    shift = (32 * (xx - q)) % 128
                    if shift:
                        plane = pltpu.roll(plane, shift, 1)
                    packed = jnp.where((lane >> 5) == xx, plane, packed)
                out[4 * half + q, xq] = packed


def kernel(
    log_hbm, storage_hbm, recharge_hbm, owner_hbm, column_hbm, top_hbm, observed_hbm,
    pump_rate, pump_well, out,
    log_conductivity, storage, recharge, owner, column, top, observed, load_sems,
    packed, steps_ref, lhs, ext, e_ref, r_ref, alpha_ref, heads_ref, beta_ref, u_ref, adjoint_ref, sum_ref,
    message, squares, messages, near, partial, far, parts, slots,
    halo_send, halo_recv, msg_send, msg_recv, near_send, near_recv, far_send, far_recv,
    part_send, part_recv,
):
    pairs = (
        (log_hbm, log_conductivity), (storage_hbm, storage), (recharge_hbm, recharge),
        (owner_hbm, owner), (column_hbm, column), (top_hbm, top), (observed_hbm, observed),
    )
    loads = [
        pltpu.make_async_copy(there, here, load_sems.at[i]) for i, (there, here) in enumerate(pairs)
    ]
    for copy in loads:
        copy.start()
    me, bx, by = lax.axis_index("test"), lax.axis_index("bx"), lax.axis_index("by")
    turn, place = by // ROUND, lax.rem(by, ROUND)
    neighbours = [neighbour(dx, dy) for k, (dx, dy) in NEIGHBOURS]
    near_peers = [
        {
            "bx": lax.rem(bx + a, NX_BRICKS),
            "by": turn * ROUND + lax.rem(place + b, ROUND),
        }
        for a in range(NX_BRICKS) for b in range(ROUND) if a + b > 0
    ]
    far_peers = [
        {"by": lax.rem(by + c * ROUND, NY_BRICKS)} for c in range(1, NY_BRICKS // ROUND)
    ]
    test_peers = [lax.rem(me + d, TESTS_AXIS) for d in range(1, TESTS_AXIS)]
    for cx in (0, HALO + SIDE):
        for cy in (0, HALO + SIDE):
            ext[cx : cx + HALO, cy : cy + HALO] = jnp.zeros((HALO, HALO, 8, 128), F32)
    everyone = far_peers + neighbours + near_peers + [{"test": peer} for peer in test_peers]
    barrier = pltpu.get_barrier_semaphore()
    for peer in everyone:
        pl.semaphore_signal(barrier, inc=1, device_id=peer, device_id_type=MESH)
    for copy in loads[:3]:
        copy.wait()
    pack(log_conductivity, storage, recharge, packed)
    pl.semaphore_wait(barrier, len(everyone))
    middle_halo, near_halo, outer_halo = halo_copies(packed, ext, halo_send, halo_recv)
    ext[HALO : HALO + SIDE, HALO : HALO + SIDE] = packed[...]
    for copy in loads[3:]:
        copy.wait()
    pump_cell, pump_tile = pumping(pump_rate, pump_well, owner, column, top)
    wells = own_wells(owner, column, top, observed)
    fields = (ext, e_ref, r_ref, alpha_ref, beta_ref, pump_cell, pump_tile)
    middle_halo()
    roots(ext, e_ref, HALO, HALO + SIDE)
    terms(*fields, HALO + 1, HALO + SIDE - 1)
    near_halo()
    near_coefficients(fields)
    sweeps(e_ref, alpha_ref, beta_ref, u_ref, heads_ref, 3)
    residuals(heads_ref, wells, message, squares)
    near_copies = [
        remote(squares, near.at[i], near_send.at[i], near_recv.at[i], peer)
        for i, peer in enumerate(near_peers)
    ]
    copies = [
        remote(message, messages.at[8 - k], msg_send.at[k], msg_recv.at[k], neighbour(dx, dy))
        for k, (dx, dy) in NEIGHBOURS
    ]
    messages[4] = message[...]
    outer_halo()
    roots(ext, e_ref, 0, HALO)
    roots(ext, e_ref, HALO + SIDE, EXT)
    edge_roots(ext, e_ref)
    terms(*fields, 1, HALO + 1)
    terms(*fields, HALO + SIDE - 1, EXT - 1)
    sweeps(e_ref, alpha_ref, beta_ref, u_ref, heads_ref, 2)
    for copy in near_copies:
        copy.wait()
    here = squares[...]
    for i in range(len(near_peers)):
        here = here + near[i]
    partial[...] = here
    far_copies = [
        remote(partial, far.at[i], far_send.at[i], far_recv.at[i], peer)
        for i, peer in enumerate(far_peers)
    ]
    head_steps(e_ref, heads_ref, steps_ref)
    for copy in copies:
        copy.wait()
    adjoint_source(messages, e_ref, r_ref, beta_ref, lhs)
    sweeps(e_ref, alpha_ref, beta_ref, u_ref, adjoint_ref, 2)
    for copy in far_copies:
        copy.wait()
    total = partial[...]
    for i in range(len(far_peers)):
        total = total + far[i]
    scale = (-0.5 / (4 * TESTS_AXIS)) / (total / WELLS + EPSILON)
    sensitivity(steps_ref, adjoint_ref, scale, sum_ref)
    slabs(sum_ref, parts)
    part_copies = [
        remote(parts.at[peer], slots.at[i], part_send.at[i], part_recv.at[i], {"test": peer})
        for i, peer in enumerate(test_peers)
    ]
    for copy in part_copies:
        copy.wait()
    total = parts[me]
    for i in range(TESTS_AXIS - 1):
        total = total + slots[i]
    for xq in range(2):
        for xx in range(4):
            plane = total[xq]
            if xx:
                plane = pltpu.roll(plane, 128 - 32 * xx, 1)
            out[4 * xq + xx] = plane[:, :32]


def local(
    log_conductivity, storage, recharge, pump_rate, pump_well, observed, owner, screen_column, screen_top
):
    dma = pltpu.SemaphoreType.DMA
    field = (EXT, EXT, 8, 128)
    tile = (8, 128)
    table = [a.reshape(16, 128) for a in (owner, screen_column, screen_top)]
    near, far = NX_BRICKS * ROUND - 1, NY_BRICKS // ROUND - 1
    scratch = [field] * 8 + [
        (SIDE, SIDE) + tile, tile, tile, (9,) + tile,
        (near,) + tile, tile, (far,) + tile, (TESTS_AXIS, 2) + tile, (TESTS_AXIS - 1, 2) + tile,
    ]
    counts = (24, 24, 9, 9, near, near, far, far, TESTS_AXIS - 1, TESTS_AXIS - 1)
    return pl.pallas_call(
        kernel,
        out_shape=jax.ShapeDtypeStruct((SIDE, SIDE, 32), F32),
        in_specs=[pl.BlockSpec(memory_space=pltpu.HBM)] * 7
        + [pl.BlockSpec(memory_space=VMEM)] * 2,
        out_specs=pl.BlockSpec(memory_space=VMEM),
        scratch_shapes=[VMEM((SIDE, SIDE, 256), F32)] * 3
        + [VMEM((16, 128), jnp.int32)] * 3
        + [VMEM((4, WELLS), F32), dma((7,))]
        + [
            VMEM((SIDE, SIDE) + tile, F32),
            VMEM((6, SIDE, SIDE) + tile, F32),
            VMEM((EXT - 2, (EXT - 2) * 8, GROUPS * 128), jnp.bfloat16),
        ]
        + [VMEM(s, F32) for s in scratch] + [dma((n,)) for n in counts],
        compiler_params=pltpu.CompilerParams(
            vmem_limit_bytes=67_043_328, collective_id=0, has_side_effects=True
        ),
    )(
        log_conductivity, storage, recharge, *table, observed,
        pump_rate.reshape(1, 4), pump_well.reshape(1, 4),
    )


def solution(mesh):
    placed = (
        P("bx", "by", None), P("bx", "by", None), P("bx", "by", None), P("test"), P("test"),
        P("test", None), P(), P(), P(),
    )
    return jax.shard_map(
        local, mesh=mesh, in_specs=placed, out_specs=P("bx", "by", "test"), check_vma=False
    )
```

```python
import jax
import jax.numpy as jnp
from jax import lax
from jax.experimental import pallas as pl
from jax.experimental.pallas import tpu as pltpu
from jax.sharding import PartitionSpec as P

F32 = jnp.float32
MESH = pl.DeviceIdType.MESH
VMEM = pltpu.VMEM
HIGHEST = lax.Precision.HIGHEST
EPSILON = 1e-06
SCREEN = 8
SIDE = 8
HALO = 4
EXT = SIDE + 2 * HALO
NX_BRICKS, NY_BRICKS = 4, 16
ROUND = 4
TESTS_AXIS = 8
WELLS = 2048
OWN = 32
GROUPS = 7
DIRECTIONS = [(dx, dy) for dx in (-1, 0, 1) for dy in (-1, 0, 1)]
FACES = [(1, 0), (-1, 0), (0, 1), (0, -1)]
NEIGHBOURS = [(k, d) for k, d in enumerate(DIRECTIONS) if d != (0, 0)]


def iota(shape, dim):
    return lax.broadcasted_iota(jnp.int32, shape, dim)


def z_neighbours(values, fill):
    sub, lane = iota(values.shape, 1), iota(values.shape, 2)
    low = pltpu.roll(values, 1, 2)
    low = jnp.where(lane == 0, jnp.where(sub < 4, fill, pltpu.roll(low, 4, 1)), low)
    high = pltpu.roll(values, 127, 2)
    high = jnp.where(lane == 127, jnp.where(sub < 4, pltpu.roll(high, 4, 1), fill), high)
    return low, high


def around(ref, x, lo, hi, fill):
    low, high = z_neighbours(ref[x, lo:hi], fill)
    return (
        (ref[x - 1, lo:hi] + ref[x + 1, lo:hi])
        + (ref[x, lo - 1 : hi - 1] + ref[x, lo + 1 : hi + 1])
        + (low + high)
    )


def rows(lo, hi, body, group):
    def step(i, carry):
        for j in range(group):
            body(lo + i * group + j)
        return carry

    lax.fori_loop(0, (hi - lo) // group, step, 0)


def thirds(values):
    parts, rest = [], values
    for i in range(3):
        parts.append(rest.astype(jnp.bfloat16))
        rest = rest - parts[-1].astype(F32)
    return parts


def halves(ref, x, lo, hi, field):
    first = ref[x, lo:hi, 2 * field : 2 * field + 1, :]
    second = ref[x, lo:hi, 2 * field + 1 : 2 * field + 2, :]
    shape = (hi - lo, 8, 128)
    return jnp.where(
        iota(shape, 1) < 4, jnp.broadcast_to(first, shape), jnp.broadcast_to(second, shape)
    )


def inside(x, lo, hi):
    shape = (hi - lo, 8, 128)
    gx = lax.axis_index("bx") * SIDE + x - HALO + jnp.zeros(shape, jnp.int32)
    gy = lax.axis_index("by") * SIDE + lo - HALO + iota(shape, 0)
    return (gx >= 0) & (gx < NX_BRICKS * SIDE) & (gy >= 0) & (gy < NY_BRICKS * SIDE)


def neighbour(dx, dy):
    bx, by = lax.axis_index("bx"), lax.axis_index("by")
    return {
        "bx": lax.rem(bx + dx + NX_BRICKS, NX_BRICKS),
        "by": lax.rem(by + dy + NY_BRICKS, NY_BRICKS),
    }


def remote(source, target, send_sem, recv_sem, peer):
    copy = pltpu.make_async_remote_copy(
        src_ref=source, dst_ref=target, send_sem=send_sem, recv_sem=recv_sem,
        device_id=peer, device_id_type=MESH,
    )
    copy.start()
    return copy


def halo_copies(packed, ext, send_sems, recv_sems):
    me = lax.axis_index("test")
    core = lax.rem(me, 2)
    partner = {"test": me + 1 - 2 * core}
    half = pl.ds(SIDE // 2 * core, SIDE // 2)
    half_there = pl.ds(HALO + SIDE // 2 * core, SIDE // 2)

    def along_x(near, far):
        count = far - near + 1
        here = (near - 1) * (1 - core) + (SIDE - far) * core
        there = (HALO + SIDE + near - 1) * (1 - core) + (HALO - far) * core
        return pl.ds(here, count), pl.ds(there, count)

    def along_y(dy, near, far):
        count = far - near + 1
        if dy > 0:
            return pl.ds(SIDE - far, count), pl.ds(HALO - far, count)
        return pl.ds(near - 1, count), pl.ds(HALO + SIDE + near - 1, count)

    def block(xs, dy, near, far, dx):
        ys = along_y(dy, near, far)
        return xs[0], ys[0], xs[1], ys[1], neighbour(dx, dy)

    face, side = (half, half_there), 2 * core - 1
    near = [block(face, dy, 1, 2, 0) for dy in (1, -1)]
    near += [block(along_x(1, 2), dy, 1, 1, side) for dy in (1, -1)]
    outer = [block(face, dy, 3, 3, 0) for dy in (1, -1)]
    outer += [block(along_x(1, 3), dy, 2, 2, side) for dy in (1, -1)]
    outer += [block(along_x(3, 3), dy, 1, 1, side) for dy in (1, -1)]
    across = [
        (pl.ds(from_x, HALO), pl.ds(0, SIDE), pl.ds(to_x, HALO), pl.ds(HALO, SIDE), neighbour(dx, 0))
        for dx, from_x, to_x in ((1, SIDE - HALO, 0), (-1, 0, HALO + SIDE))
    ]
    plan = near + across + outer
    started = [
        remote(packed.at[x, y], ext.at[to_x, to_y], send_sems.at[k], recv_sems.at[k], peer)
        for k, (x, y, to_x, to_y, peer) in enumerate(plan)
    ]

    def middle():
        for copy in started[4:6]:
            copy.wait()

    def finish(lo, hi):
        passed = []
        for k in range(lo, hi):
            x, y, to_x, to_y, peer = plan[k]
            started[k].wait_recv()
            block = ext.at[to_x, to_y]
            passed.append(remote(block, block, send_sems.at[12 + k], recv_sems.at[12 + k], partner))
        for copy in started[lo:hi]:
            copy.wait_send()
        for copy in passed:
            copy.wait()

    return middle, lambda: finish(0, 4), lambda: finish(6, 12)


def roots(ext, e_ref, lo, hi, first=0, last=EXT, group=4):
    def row(x):
        logs = halves(ext, x, lo, hi, 0)
        e_ref[x, lo:hi] = jnp.where(inside(x, lo, hi), jnp.exp(0.5 * logs), 1.0)

    rows(first, last, row, group)


def terms(ext, e_ref, r_ref, alpha_ref, beta_ref, pump_cell, pump_tile, lo, hi, first=1, last=EXT - 1):
    def row(x):
        e = e_ref[x, lo:hi]
        diagonal = halves(ext, x, lo, hi, 1) + e * around(e_ref, x, lo, hi, 1.0)
        r = jnp.where(inside(x, lo, hi), 1.0 / diagonal, 0.0)
        cell = x * EXT + lo + iota(e.shape, 0)
        source = halves(ext, x, lo, hi, 2) + jnp.where(pump_cell[None] == cell, pump_tile[None], 0.0)
        er = e * r
        r_ref[x, lo:hi] = r
        alpha_ref[x, lo:hi] = e * er
        beta_ref[x, lo:hi] = er * source

    rows(first, last, row, 2)


def edge(ext, e_ref, xs, y, source_y):
    count = xs.stop - xs.start
    shape = (count, 8, 128)
    first = ext[xs, source_y, 6:7, :]
    second = ext[xs, source_y, 7:8, :]
    logs = jnp.where(
        iota(shape, 1) < 4, jnp.broadcast_to(first, shape), jnp.broadcast_to(second, shape)
    )
    gx = lax.axis_index("bx") * SIDE + xs.start - HALO + iota(shape, 0)
    gy = lax.axis_index("by") * SIDE + y - HALO + jnp.zeros(shape, jnp.int32)
    ok = (gx >= 0) & (gx < NX_BRICKS * SIDE) & (gy >= 0) & (gy < NY_BRICKS * SIDE)
    e_ref[xs, y] = jnp.where(ok, jnp.exp(0.5 * logs), 1.0)


MIDDLE = slice(HALO, HALO + SIDE)


def edge_roots(ext, e_ref):
    edge(ext, e_ref, MIDDLE, 0, 1)
    edge(ext, e_ref, MIDDLE, EXT - 1, EXT - 2)
    for x in (HALO - 1, HALO + SIDE):
        edge(ext, e_ref, slice(x, x + 1), 1, 2)
        edge(ext, e_ref, slice(x, x + 1), EXT - 2, EXT - 3)


def near_coefficients(fields):
    ext, e_ref = fields[:2]
    lo, hi = HALO, HALO + SIDE
    for first, last in ((lo - 2, lo), (hi, hi + 2)):
        roots(ext, e_ref, first, last, lo, hi)
        for column in (lo - 1, hi):
            roots(ext, e_ref, column, column + 1, first, last, 2)
    edge(ext, e_ref, MIDDLE, lo - 3, lo - 2)
    edge(ext, e_ref, MIDDLE, hi + 2, hi + 1)
    for x in (lo - 1, hi):
        edge(ext, e_ref, slice(x, x + 1), lo - 2, lo - 1)
        edge(ext, e_ref, slice(x, x + 1), hi + 1, hi)
    terms(*fields, lo - 2, lo + 1, lo, hi)
    terms(*fields, hi - 1, hi + 2, lo, hi)
    for first in (lo - 2, hi):
        terms(*fields, lo - 1, lo + 1, first, first + 2)
        terms(*fields, hi - 1, hi + 1, first, first + 2)


def sweeps(e_ref, alpha_ref, beta_ref, u_ref, out_ref, first):
    def second(x):
        u_ref[x, first : EXT - first] = beta_ref[x, first : EXT - first] + alpha_ref[
            x, first : EXT - first
        ] * around(beta_ref, x, first, EXT - first, 0.0)

    rows(first, EXT - first, second, 4 if (EXT - 2 * first) % 4 == 0 else 5)
    lo, hi = first + 1, EXT - first - 1

    def third(x):
        u = beta_ref[x, lo:hi] + alpha_ref[x, lo:hi] * around(u_ref, x, lo, hi, 0.0)
        out_ref[x, lo:hi] = u / e_ref[x, lo:hi]

    rows(lo, hi, third, 4 if (hi - lo) % 4 == 0 else 5)


def pumping(pump_rate, pump_well, owner, column, top):
    sub, lane = iota((8, 128), 0), iota((8, 128), 1)
    z = lane + jnp.where(sub < 4, 0, 128)
    cell = jnp.zeros((8, 128), jnp.int32)
    tile = jnp.zeros((8, 128), F32)
    first_x = lax.axis_index("bx") * SIDE - HALO
    first_y = lax.axis_index("by") * SIDE - HALO
    code = (owner[...] * 64 + column[...]) * 256 + top[...]
    code = code.astype(F32)
    index = iota((16, 128), 0) * 128 + iota((16, 128), 1)
    for t in range(4):
        well = jnp.broadcast_to(pump_well[0:1, t : t + 1], (16, 128))
        found = jnp.sum(jnp.where(index == well, code, 0.0), axis=0, keepdims=True)
        found = jnp.broadcast_to(jnp.sum(found, axis=1, keepdims=True), (8, 128)).astype(jnp.int32)
        brick, place, start = found >> 14, (found >> 8) & 63, found & 255
        x = (brick >> 4) * SIDE + (place >> 3) - first_x
        y = (brick & 15) * SIDE + (place & 7) - first_y
        ok = (x >= 0) & (x < EXT) & (y >= 0) & (y < EXT)
        mine = (sub & 3) == t
        cell = jnp.where(mine, jnp.where(ok, x * EXT + y, -1), cell)
        hit = mine & (z >= start) & (z < start + SCREEN)
        tile = jnp.where(hit, -jnp.broadcast_to(pump_rate[0:1, t : t + 1], (8, 128)), tile)
    return cell, tile


def pack(log_conductivity, storage, recharge, packed):
    def row(x):
        logs = log_conductivity[x]
        further = jnp.where(
            iota((SIDE, 256), 0) < 4, pltpu.roll(logs, SIDE - 1, 0), pltpu.roll(logs, 1, 0)
        )
        for field, values in enumerate((logs, storage[x], recharge[x], further)):
            packed[x, :, 2 * field, :] = values[:, :128]
            packed[x, :, 2 * field + 1, :] = values[:, 128:]

    rows(0, SIDE, row, 2)


def own_wells(owner, column, top, observed):
    brick = lax.axis_index("bx") * NY_BRICKS + lax.axis_index("by")
    mine = jnp.where(owner[...] == brick, 1.0, 0.0)
    upto = jnp.where(iota((128, 128), 0) <= iota((128, 128), 1), 1.0, 0.0)
    inner = jnp.dot(mine, upto, precision=HIGHEST, preferred_element_type=F32)
    count = jnp.broadcast_to(jnp.sum(mine, axis=1, keepdims=True), (16, 128))
    before = jnp.where(iota((16, 16), 1) < iota((16, 16), 0), 1.0, 0.0)
    rank = inner + jnp.dot(before, count, precision=HIGHEST, preferred_element_type=F32) - 1.0
    rank = jnp.where(mine > 0.0, rank, -1.0)
    place = iota((OWN, 128), 0).astype(F32)
    sums = [jnp.zeros((OWN, 128), F32) for field in range(6)]
    for k in range(16):
        hit = jnp.broadcast_to(rank[k : k + 1, :], (OWN, 128)) == place
        values = [column[k : k + 1, :].astype(F32), top[k : k + 1, :].astype(F32)]
        values += [observed[t : t + 1, k * 128 : (k + 1) * 128] for t in range(4)]
        for field in range(6):
            sums[field] = sums[field] + jnp.where(
                hit, jnp.broadcast_to(values[field], (OWN, 128)), 0.0
            )
    return [jnp.sum(s, axis=1, keepdims=True) for s in sums]


def residuals(heads_ref, wells, message, squares):
    column, top, observed = wells[0], wells[1], wells[2:]
    column2 = jnp.concatenate([column, column], axis=0)
    top2 = jnp.concatenate([top, top], axis=0)
    half = iota((2 * OWN, 128), 0) // OWN
    z = (iota((2 * OWN, 128), 1) + 128 * half).astype(F32)
    screen = jnp.where((z >= top2) & (z < top2 + SCREEN), 1.0, 0.0)
    heads = heads_ref[HALO : HALO + SIDE, HALO : HALO + SIDE].reshape(512, 128)
    screen = screen.astype(jnp.bfloat16)
    sums = lax.dot_general(
        jnp.concatenate([screen] * 3, axis=1), jnp.concatenate(thirds(heads), axis=1),
        (((1,), (1,)), ((), ())), preferred_element_type=F32,
    )
    at = iota((2 * OWN, 512), 1)
    keep = ((at >> 3).astype(F32) == column2) & (
        ((at >> 2) & 1) == iota((2 * OWN, 512), 0) // OWN
    )
    sums = jnp.where(keep, sums, 0.0)
    pick = jnp.where((iota((512, 128), 0) & 3) == iota((512, 128), 1), 1.0, 0.0)
    pick = pick.astype(jnp.bfloat16)
    sums = sum(jnp.dot(part, pick, preferred_element_type=F32) for part in thirds(sums))
    sums = (sums[:OWN] + sums[OWN:]) * (1.0 / SCREEN)
    lane = iota((OWN, 128), 1)
    for t in range(4):
        sums = jnp.where(lane == t, sums - observed[t], sums)
    sums = jnp.where(lane == 4, column, sums)
    sums = jnp.where(lane == 5, top, sums)
    eye = jnp.where(iota((8, 128), 0) == iota((8, 128), 1), 1.0, 0.0)
    turned = lax.dot_general(
        eye, sums, (((1,), (1,)), ((), ())), precision=HIGHEST, preferred_element_type=F32
    )
    message[...] = jnp.concatenate([turned, jnp.zeros((8, 128 - OWN), F32)], axis=1)
    total = jnp.broadcast_to(jnp.sum(turned * turned, axis=1, keepdims=True), (8, 128))
    squares[...] = jnp.where(iota((8, 128), 0) < 4, total, pltpu.roll(total, 4, 0))


def adjoint_source(messages, e_ref, r_ref, beta_ref, lhs):
    sub, lane = iota((8, 128), 0), iota((8, 128), 1)
    values = [jnp.zeros((8, 128), F32) for g in range(GROUPS)]
    cells = [jnp.zeros((8, 128), F32) for g in range(GROUPS)]
    tops = [jnp.zeros((8, 128), F32) for g in range(GROUPS)]
    for k, (dx, dy) in enumerate(DIRECTIONS):
        tile = messages[k]
        value = jnp.where(sub < 4, tile, pltpu.roll(tile, 4, 0))
        column = jnp.broadcast_to(tile[4:5], (8, 128))
        along = jnp.floor(column * (1.0 / SIDE))
        x = along + (HALO + SIDE * dx)
        y = column - along * SIDE + (HALO + SIDE * dy)
        ok = (x >= 1) & (x < EXT - 1) & (y >= 1) & (y < EXT - 1) & (lane < OWN)
        cell = jnp.where(ok, x * EXT + y, 0.0)
        top = jnp.where(lane < OWN, jnp.broadcast_to(tile[5:6], (8, 128)), 0.0)
        for p, part in enumerate(thirds(value)):
            g, shift = (3 * k + p) // 4, OWN * ((3 * k + p) % 4)
            moved = [part.astype(F32), cell, top]
            if shift:
                moved = [pltpu.roll(v, shift, 1) for v in moved]
            values[g], cells[g], tops[g] = values[g] + moved[0], cells[g] + moved[1], tops[g] + moved[2]
    z = iota((256, 128), 0).astype(F32)
    screens = []
    for g in range(GROUPS):
        top = jnp.broadcast_to(tops[g][0:1], (256, 128))
        screens.append(jnp.where((z >= top) & (z < top + SCREEN), 1.0, 0.0).astype(jnp.bfloat16))
    screen = jnp.concatenate(screens, axis=1)
    wide = EXT - 2
    shape = (wide, 8, 128)
    lo, hi = 1, EXT - 1

    def left(x):
        cell = (x * EXT + 1 + iota(shape, 0)).astype(F32)
        for g in range(GROUPS):
            lhs[x - 1, :, g * 128 : (g + 1) * 128] = (
                jnp.where(cells[g][None] == cell, values[g][None], 0.0)
                .reshape(wide * 8, 128)
                .astype(jnp.bfloat16)
            )

    rows(lo, hi, left, 2)
    group = 7
    for first in range(0, wide, group):
        block = lhs[first : first + group].reshape(group * wide * 8, GROUPS * 128)
        both = lax.dot_general(
            block, screen, (((1,), (1,)), ((), ())), preferred_element_type=F32
        )
        pair = both.reshape(group, wide, 8, 256)
        for i in range(group):
            source = jnp.where(iota(shape, 1) < 4, pair[i, :, :, :128], pair[i, :, :, 128:])
            x = first + i + 1
            beta_ref[x, lo:hi] = e_ref[x, lo:hi] * r_ref[x, lo:hi] * source


def head_steps(e_ref, heads_ref, steps_ref):
    lo, hi = HALO, HALO + SIDE

    def row(x):
        h, e = heads_ref[x, lo:hi], e_ref[x, lo:hi]
        for f, (step_x, step_y) in enumerate(FACES):
            at = (x + step_x, slice(lo + step_y, hi + step_y))
            steps_ref[f, x - HALO] = e * e_ref[at] * (h - heads_ref[at])
        for f, (e_n, h_n) in enumerate(zip(z_neighbours(e, 1.0), z_neighbours(h, 0.0))):
            steps_ref[4 + f, x - HALO] = e * e_n * (h - h_n)

    rows(lo, hi, row, 2)


def sensitivity(steps_ref, adjoint_ref, out_ref):
    lo, hi = HALO, HALO + SIDE

    def row(x):
        a = adjoint_ref[x, lo:hi]
        total = jnp.zeros_like(a)
        for f, (step_x, step_y) in enumerate(FACES):
            total = total + steps_ref[f, x - HALO] * (
                a - adjoint_ref[x + step_x, lo + step_y : hi + step_y]
            )
        for f, a_n in enumerate(z_neighbours(a, 0.0)):
            total = total + steps_ref[4 + f, x - HALO] * (a - a_n)
        out_ref[x - HALO] = total

    rows(lo, hi, row, 4)


def sum_tests(sum_ref, scale):
    def row(x):
        total = sum_ref[x] * scale[None]
        total = total + pltpu.roll(total, 7, 1)
        sum_ref[x] = total + pltpu.roll(total, 6, 1)

    rows(0, SIDE, row, 4)


def slabs(sum_ref, out):
    lane = iota((8, 128), 1)
    for half in range(2):
        planes = sum_ref[:, :, 4 * half, :]
        for q in range(4):
            for xq in range(2):
                packed = jnp.zeros((8, 128), F32)
                for xx in range(4):
                    plane = planes[4 * xq + xx]
                    shift = (32 * (xx - q)) % 128
                    if shift:
                        plane = pltpu.roll(plane, shift, 1)
                    packed = jnp.where((lane >> 5) == xx, plane, packed)
                out[4 * half + q, xq] = packed


def kernel(
    log_hbm, storage_hbm, recharge_hbm, owner_hbm, column_hbm, top_hbm, observed_hbm,
    pump_rate, pump_well, out,
    log_conductivity, storage, recharge, owner, column, top, observed, load_sems,
    packed, steps_ref, lhs, ext, e_ref, r_ref, alpha_ref, heads_ref, beta_ref, u_ref, adjoint_ref, sum_ref,
    message, squares, messages, near, partial, far, parts, slots,
    halo_send, halo_recv, msg_send, msg_recv, near_send, near_recv, far_send, far_recv,
    part_send, part_recv,
):
    pairs = (
        (log_hbm, log_conductivity), (storage_hbm, storage), (recharge_hbm, recharge),
        (owner_hbm, owner), (column_hbm, column), (top_hbm, top), (observed_hbm, observed),
    )
    loads = [
        pltpu.make_async_copy(there, here, load_sems.at[i]) for i, (there, here) in enumerate(pairs)
    ]
    for copy in loads:
        copy.start()
    me, bx, by = lax.axis_index("test"), lax.axis_index("bx"), lax.axis_index("by")
    turn, place = by // ROUND, lax.rem(by, ROUND)
    neighbours = [neighbour(dx, dy) for k, (dx, dy) in NEIGHBOURS]
    near_peers = [
        {
            "bx": lax.rem(bx + a, NX_BRICKS),
            "by": turn * ROUND + lax.rem(place + b, ROUND),
        }
        for a in range(NX_BRICKS) for b in range(ROUND) if a + b > 0
    ]
    far_peers = [
        {"by": lax.rem(by + c * ROUND, NY_BRICKS)} for c in range(1, NY_BRICKS // ROUND)
    ]
    test_peers = [lax.rem(me + d, TESTS_AXIS) for d in range(1, TESTS_AXIS)]
    for cx in (0, HALO + SIDE):
        for cy in (0, HALO + SIDE):
            ext[cx : cx + HALO, cy : cy + HALO] = jnp.zeros((HALO, HALO, 8, 128), F32)
    everyone = far_peers + neighbours + near_peers + [{"test": peer} for peer in test_peers]
    barrier = pltpu.get_barrier_semaphore()
    for peer in everyone:
        pl.semaphore_signal(barrier, inc=1, device_id=peer, device_id_type=MESH)
    for copy in loads[:3]:
        copy.wait()
    pack(log_conductivity, storage, recharge, packed)
    pl.semaphore_wait(barrier, len(everyone))
    middle_halo, near_halo, outer_halo = halo_copies(packed, ext, halo_send, halo_recv)
    ext[HALO : HALO + SIDE, HALO : HALO + SIDE] = packed[...]
    for copy in loads[3:]:
        copy.wait()
    pump_cell, pump_tile = pumping(pump_rate, pump_well, owner, column, top)
    wells = own_wells(owner, column, top, observed)
    fields = (ext, e_ref, r_ref, alpha_ref, beta_ref, pump_cell, pump_tile)
    middle_halo()
    roots(ext, e_ref, HALO, HALO + SIDE)
    terms(*fields, HALO + 1, HALO + SIDE - 1)
    near_halo()
    near_coefficients(fields)
    sweeps(e_ref, alpha_ref, beta_ref, u_ref, heads_ref, 3)
    residuals(heads_ref, wells, message, squares)
    near_copies = [
        remote(squares, near.at[i], near_send.at[i], near_recv.at[i], peer)
        for i, peer in enumerate(near_peers)
    ]
    copies = [
        remote(message, messages.at[8 - k], msg_send.at[k], msg_recv.at[k], neighbour(dx, dy))
        for k, (dx, dy) in NEIGHBOURS
    ]
    messages[4] = message[...]
    outer_halo()
    roots(ext, e_ref, 0, HALO)
    roots(ext, e_ref, HALO + SIDE, EXT)
    edge_roots(ext, e_ref)
    terms(*fields, 1, HALO + 1)
    terms(*fields, HALO + SIDE - 1, EXT - 1)
    for copy in near_copies:
        copy.wait()
    here = squares[...]
    for i in range(len(near_peers)):
        here = here + near[i]
    partial[...] = here
    far_copies = [
        remote(partial, far.at[i], far_send.at[i], far_recv.at[i], peer)
        for i, peer in enumerate(far_peers)
    ]
    sweeps(e_ref, alpha_ref, beta_ref, u_ref, heads_ref, 2)
    head_steps(e_ref, heads_ref, steps_ref)
    for copy in copies:
        copy.wait()
    adjoint_source(messages, e_ref, r_ref, beta_ref, lhs)
    sweeps(e_ref, alpha_ref, beta_ref, u_ref, adjoint_ref, 2)
    sensitivity(steps_ref, adjoint_ref, sum_ref)
    for copy in far_copies:
        copy.wait()
    total = partial[...]
    for i in range(len(far_peers)):
        total = total + far[i]
    scale = 1.0 / (total / WELLS + EPSILON)
    sum_tests(sum_ref, scale)
    slabs(sum_ref, parts)
    part_copies = [
        remote(parts.at[peer], slots.at[i], part_send.at[i], part_recv.at[i], {"test": peer})
        for i, peer in enumerate(test_peers)
    ]
    for copy in part_copies:
        copy.wait()
    total = parts[me]
    for i in range(TESTS_AXIS - 1):
        total = total + slots[i]
    for xq in range(2):
        for xx in range(4):
            plane = total[xq]
            if xx:
                plane = pltpu.roll(plane, 128 - 32 * xx, 1)
            out[4 * xq + xx] = plane[:, :32]


def local(
    log_conductivity, storage, recharge, pump_rate, pump_well, observed, owner, screen_column, screen_top
):
    dma = pltpu.SemaphoreType.DMA
    field = (EXT, EXT, 8, 128)
    tile = (8, 128)
    table = [a.reshape(16, 128) for a in (owner, screen_column, screen_top)]
    near, far = NX_BRICKS * ROUND - 1, NY_BRICKS // ROUND - 1
    scratch = [field] * 8 + [
        (SIDE, SIDE) + tile, tile, tile, (9,) + tile,
        (near,) + tile, tile, (far,) + tile, (TESTS_AXIS, 2) + tile, (TESTS_AXIS - 1, 2) + tile,
    ]
    counts = (24, 24, 9, 9, near, near, far, far, TESTS_AXIS - 1, TESTS_AXIS - 1)
    total = pl.pallas_call(
        kernel,
        out_shape=jax.ShapeDtypeStruct((SIDE, SIDE, 32), F32),
        in_specs=[pl.BlockSpec(memory_space=pltpu.HBM)] * 7
        + [pl.BlockSpec(memory_space=VMEM)] * 2,
        out_specs=pl.BlockSpec(memory_space=VMEM),
        scratch_shapes=[VMEM((SIDE, SIDE, 256), F32)] * 3
        + [VMEM((16, 128), jnp.int32)] * 3
        + [VMEM((4, WELLS), F32), dma((7,))]
        + [
            VMEM((SIDE, SIDE) + tile, F32),
            VMEM((6, SIDE, SIDE) + tile, F32),
            VMEM((EXT - 2, (EXT - 2) * 8, GROUPS * 128), jnp.bfloat16),
        ]
        + [VMEM(s, F32) for s in scratch] + [dma((n,)) for n in counts],
        compiler_params=pltpu.CompilerParams(
            vmem_limit_bytes=67_043_328, collective_id=0, has_side_effects=True
        ),
    )(
        log_conductivity, storage, recharge, *table, observed,
        pump_rate.reshape(1, 4), pump_well.reshape(1, 4),
    )
    return total * (-0.5 / (4 * TESTS_AXIS))


def solution(mesh):
    placed = (
        P("bx", "by", None), P("bx", "by", None), P("bx", "by", None), P("test"), P("test"),
        P("test", None), P(), P(), P(),
    )
    return jax.shard_map(
        local, mesh=mesh, in_specs=placed, out_specs=P("bx", "by", "test"), check_vma=False
    )
```

```python
import jax
import jax.numpy as jnp
from jax import lax
from jax.experimental import pallas as pl
from jax.experimental.pallas import tpu as pltpu
from jax.sharding import PartitionSpec as P

F32 = jnp.float32
MESH = pl.DeviceIdType.MESH
VMEM = pltpu.VMEM
HIGHEST = lax.Precision.HIGHEST
EPSILON = 1e-06
SCREEN = 8
SIDE = 8
HALO = 4
EXT = SIDE + 2 * HALO
NX_BRICKS, NY_BRICKS = 4, 16
ROUND = 4
TESTS_AXIS = 8
WELLS = 2048
OWN = 32
GROUPS = 7
DIRECTIONS = [(dx, dy) for dx in (-1, 0, 1) for dy in (-1, 0, 1)]
FACES = [(1, 0), (-1, 0), (0, 1), (0, -1)]
NEIGHBOURS = [(k, d) for k, d in enumerate(DIRECTIONS) if d != (0, 0)]


def iota(shape, dim):
    return lax.broadcasted_iota(jnp.int32, shape, dim)


def z_neighbours(values, fill):
    sub, lane = iota(values.shape, 1), iota(values.shape, 2)
    low = pltpu.roll(values, 1, 2)
    low = jnp.where(lane == 0, jnp.where(sub < 4, fill, pltpu.roll(low, 4, 1)), low)
    high = pltpu.roll(values, 127, 2)
    high = jnp.where(lane == 127, jnp.where(sub < 4, pltpu.roll(high, 4, 1), fill), high)
    return low, high


def around(ref, x, lo, hi, fill):
    low, high = z_neighbours(ref[x, lo:hi], fill)
    return (
        (ref[x - 1, lo:hi] + ref[x + 1, lo:hi])
        + (ref[x, lo - 1 : hi - 1] + ref[x, lo + 1 : hi + 1])
        + (low + high)
    )


def rows(lo, hi, body, group):
    def step(i, carry):
        for j in range(group):
            body(lo + i * group + j)
        return carry

    lax.fori_loop(0, (hi - lo) // group, step, 0)


def thirds(values):
    parts, rest = [], values
    for i in range(3):
        parts.append(rest.astype(jnp.bfloat16))
        rest = rest - parts[-1].astype(F32)
    return parts


def halves(ref, x, lo, hi, field):
    first = ref[x, lo:hi, 2 * field : 2 * field + 1, :]
    second = ref[x, lo:hi, 2 * field + 1 : 2 * field + 2, :]
    shape = (hi - lo, 8, 128)
    return jnp.where(
        iota(shape, 1) < 4, jnp.broadcast_to(first, shape), jnp.broadcast_to(second, shape)
    )


def inside(x, lo, hi):
    shape = (hi - lo, 8, 128)
    gx = lax.axis_index("bx") * SIDE + x - HALO + jnp.zeros(shape, jnp.int32)
    gy = lax.axis_index("by") * SIDE + lo - HALO + iota(shape, 0)
    return (gx >= 0) & (gx < NX_BRICKS * SIDE) & (gy >= 0) & (gy < NY_BRICKS * SIDE)


def neighbour(dx, dy):
    bx, by = lax.axis_index("bx"), lax.axis_index("by")
    return {
        "bx": lax.rem(bx + dx + NX_BRICKS, NX_BRICKS),
        "by": lax.rem(by + dy + NY_BRICKS, NY_BRICKS),
    }


def remote(source, target, send_sem, recv_sem, peer):
    copy = pltpu.make_async_remote_copy(
        src_ref=source, dst_ref=target, send_sem=send_sem, recv_sem=recv_sem,
        device_id=peer, device_id_type=MESH,
    )
    copy.start()
    return copy


def halo_copies(packed, ext, send_sems, recv_sems):
    me = lax.axis_index("test")
    core = lax.rem(me, 2)
    partner = {"test": me + 1 - 2 * core}
    half = pl.ds(SIDE // 2 * core, SIDE // 2)
    half_there = pl.ds(HALO + SIDE // 2 * core, SIDE // 2)

    def along_x(near, far):
        count = far - near + 1
        here = (near - 1) * (1 - core) + (SIDE - far) * core
        there = (HALO + SIDE + near - 1) * (1 - core) + (HALO - far) * core
        return pl.ds(here, count), pl.ds(there, count)

    def along_y(dy, near, far):
        count = far - near + 1
        if dy > 0:
            return pl.ds(SIDE - far, count), pl.ds(HALO - far, count)
        return pl.ds(near - 1, count), pl.ds(HALO + SIDE + near - 1, count)

    def block(xs, dy, near, far, dx):
        ys = along_y(dy, near, far)
        return xs[0], ys[0], xs[1], ys[1], neighbour(dx, dy)

    face, side = (half, half_there), 2 * core - 1
    near = [block(face, dy, 1, 2, 0) for dy in (1, -1)]
    near += [block(along_x(1, 2), dy, 1, 1, side) for dy in (1, -1)]
    outer = [block(face, dy, 3, 3, 0) for dy in (1, -1)]
    outer += [block(along_x(1, 3), dy, 2, 2, side) for dy in (1, -1)]
    outer += [block(along_x(3, 3), dy, 1, 1, side) for dy in (1, -1)]
    across = [
        (pl.ds(from_x, HALO), pl.ds(0, SIDE), pl.ds(to_x, HALO), pl.ds(HALO, SIDE), neighbour(dx, 0))
        for dx, from_x, to_x in ((1, SIDE - HALO, 0), (-1, 0, HALO + SIDE))
    ]
    plan = near + across + outer
    started = [
        remote(packed.at[x, y], ext.at[to_x, to_y], send_sems.at[k], recv_sems.at[k], peer)
        for k, (x, y, to_x, to_y, peer) in enumerate(plan)
    ]

    def middle():
        for copy in started[4:6]:
            copy.wait()

    def finish(lo, hi):
        passed = []
        for k in range(lo, hi):
            x, y, to_x, to_y, peer = plan[k]
            started[k].wait_recv()
            block = ext.at[to_x, to_y]
            passed.append(remote(block, block, send_sems.at[12 + k], recv_sems.at[12 + k], partner))
        for copy in started[lo:hi]:
            copy.wait_send()
        for copy in passed:
            copy.wait()

    return middle, lambda: finish(0, 4), lambda: finish(6, 12)


def roots(ext, e_ref, lo, hi, first=0, last=EXT, group=4):
    def row(x):
        logs = halves(ext, x, lo, hi, 0)
        e_ref[x, lo:hi] = jnp.where(inside(x, lo, hi), jnp.exp(0.5 * logs), 1.0)

    rows(first, last, row, group)


def terms(ext, e_ref, r_ref, alpha_ref, beta_ref, pump_cell, pump_tile, lo, hi, first=1, last=EXT - 1):
    def row(x):
        e = e_ref[x, lo:hi]
        diagonal = halves(ext, x, lo, hi, 1) + e * around(e_ref, x, lo, hi, 1.0)
        r = jnp.where(inside(x, lo, hi), 1.0 / diagonal, 0.0)
        cell = x * EXT + lo + iota(e.shape, 0)
        source = halves(ext, x, lo, hi, 2) + jnp.where(pump_cell[None] == cell, pump_tile[None], 0.0)
        er = e * r
        r_ref[x, lo:hi] = r
        alpha_ref[x, lo:hi] = e * er
        beta_ref[x, lo:hi] = er * source

    count = last - first
    rows(first, last, row, 7 if count % 7 == 0 else min(count, 4))


def edge(ext, e_ref, xs, y, source_y):
    count = xs.stop - xs.start
    shape = (count, 8, 128)
    first = ext[xs, source_y, 6:7, :]
    second = ext[xs, source_y, 7:8, :]
    logs = jnp.where(
        iota(shape, 1) < 4, jnp.broadcast_to(first, shape), jnp.broadcast_to(second, shape)
    )
    gx = lax.axis_index("bx") * SIDE + xs.start - HALO + iota(shape, 0)
    gy = lax.axis_index("by") * SIDE + y - HALO + jnp.zeros(shape, jnp.int32)
    ok = (gx >= 0) & (gx < NX_BRICKS * SIDE) & (gy >= 0) & (gy < NY_BRICKS * SIDE)
    e_ref[xs, y] = jnp.where(ok, jnp.exp(0.5 * logs), 1.0)


MIDDLE = slice(HALO, HALO + SIDE)


def edge_roots(ext, e_ref):
    edge(ext, e_ref, MIDDLE, 0, 1)
    edge(ext, e_ref, MIDDLE, EXT - 1, EXT - 2)
    for x in (HALO - 1, HALO + SIDE):
        edge(ext, e_ref, slice(x, x + 1), 1, 2)
        edge(ext, e_ref, slice(x, x + 1), EXT - 2, EXT - 3)


def near_coefficients(fields):
    ext, e_ref = fields[:2]
    lo, hi = HALO, HALO + SIDE
    for first, last in ((lo - 2, lo), (hi, hi + 2)):
        roots(ext, e_ref, first, last, lo, hi)
        for column in (lo - 1, hi):
            roots(ext, e_ref, column, column + 1, first, last, 2)
    edge(ext, e_ref, MIDDLE, lo - 3, lo - 2)
    edge(ext, e_ref, MIDDLE, hi + 2, hi + 1)
    for x in (lo - 1, hi):
        edge(ext, e_ref, slice(x, x + 1), lo - 2, lo - 1)
        edge(ext, e_ref, slice(x, x + 1), hi + 1, hi)
    terms(*fields, lo - 2, lo + 1, lo, hi)
    terms(*fields, hi - 1, hi + 2, lo, hi)
    for first in (lo - 2, hi):
        terms(*fields, lo - 1, lo + 1, first, first + 2)
        terms(*fields, hi - 1, hi + 1, first, first + 2)


def sweeps(e_ref, alpha_ref, beta_ref, u_ref, out_ref, first):
    def second(x):
        u_ref[x, first : EXT - first] = beta_ref[x, first : EXT - first] + alpha_ref[
            x, first : EXT - first
        ] * around(beta_ref, x, first, EXT - first, 0.0)

    rows(first, EXT - first, second, 4 if (EXT - 2 * first) % 4 == 0 else 5)
    lo, hi = first + 1, EXT - first - 1

    def third(x):
        u = beta_ref[x, lo:hi] + alpha_ref[x, lo:hi] * around(u_ref, x, lo, hi, 0.0)
        out_ref[x, lo:hi] = u / e_ref[x, lo:hi]

    rows(lo, hi, third, 4 if (hi - lo) % 4 == 0 else 5)


def pumping(pump_rate, pump_well, owner, column, top):
    sub, lane = iota((8, 128), 0), iota((8, 128), 1)
    z = lane + jnp.where(sub < 4, 0, 128)
    cell = jnp.zeros((8, 128), jnp.int32)
    tile = jnp.zeros((8, 128), F32)
    first_x = lax.axis_index("bx") * SIDE - HALO
    first_y = lax.axis_index("by") * SIDE - HALO
    code = (owner[...] * 64 + column[...]) * 256 + top[...]
    code = code.astype(F32)
    index = iota((16, 128), 0) * 128 + iota((16, 128), 1)
    for t in range(4):
        well = jnp.broadcast_to(pump_well[0:1, t : t + 1], (16, 128))
        found = jnp.sum(jnp.where(index == well, code, 0.0), axis=0, keepdims=True)
        found = jnp.broadcast_to(jnp.sum(found, axis=1, keepdims=True), (8, 128)).astype(jnp.int32)
        brick, place, start = found >> 14, (found >> 8) & 63, found & 255
        x = (brick >> 4) * SIDE + (place >> 3) - first_x
        y = (brick & 15) * SIDE + (place & 7) - first_y
        ok = (x >= 0) & (x < EXT) & (y >= 0) & (y < EXT)
        mine = (sub & 3) == t
        cell = jnp.where(mine, jnp.where(ok, x * EXT + y, -1), cell)
        hit = mine & (z >= start) & (z < start + SCREEN)
        tile = jnp.where(hit, -jnp.broadcast_to(pump_rate[0:1, t : t + 1], (8, 128)), tile)
    return cell, tile


def pack(log_conductivity, storage, recharge, packed):
    def row(x):
        logs = log_conductivity[x]
        further = jnp.where(
            iota((SIDE, 256), 0) < 4, pltpu.roll(logs, SIDE - 1, 0), pltpu.roll(logs, 1, 0)
        )
        for field, values in enumerate((logs, storage[x], recharge[x], further)):
            packed[x, :, 2 * field, :] = values[:, :128]
            packed[x, :, 2 * field + 1, :] = values[:, 128:]

    rows(0, SIDE, row, 2)


def own_wells(owner, column, top, observed):
    brick = lax.axis_index("bx") * NY_BRICKS + lax.axis_index("by")
    mine = jnp.where(owner[...] == brick, 1.0, 0.0)
    upto = jnp.where(iota((128, 128), 0) <= iota((128, 128), 1), 1.0, 0.0)
    inner = jnp.dot(mine, upto, precision=HIGHEST, preferred_element_type=F32)
    count = jnp.broadcast_to(jnp.sum(mine, axis=1, keepdims=True), (16, 128))
    before = jnp.where(iota((16, 16), 1) < iota((16, 16), 0), 1.0, 0.0)
    rank = inner + jnp.dot(before, count, precision=HIGHEST, preferred_element_type=F32) - 1.0
    rank = jnp.where(mine > 0.0, rank, -1.0)
    place = iota((OWN, 128), 0).astype(F32)
    sums = [jnp.zeros((OWN, 128), F32) for field in range(6)]
    for k in range(16):
        hit = jnp.broadcast_to(rank[k : k + 1, :], (OWN, 128)) == place
        values = [column[k : k + 1, :].astype(F32), top[k : k + 1, :].astype(F32)]
        values += [observed[t : t + 1, k * 128 : (k + 1) * 128] for t in range(4)]
        for field in range(6):
            sums[field] = sums[field] + jnp.where(
                hit, jnp.broadcast_to(values[field], (OWN, 128)), 0.0
            )
    return [jnp.sum(s, axis=1, keepdims=True) for s in sums]


def residuals(heads_ref, wells, message, squares):
    column, top, observed = wells[0], wells[1], wells[2:]
    column2 = jnp.concatenate([column, column], axis=0)
    top2 = jnp.concatenate([top, top], axis=0)
    half = iota((2 * OWN, 128), 0) // OWN
    z = (iota((2 * OWN, 128), 1) + 128 * half).astype(F32)
    screen = jnp.where((z >= top2) & (z < top2 + SCREEN), 1.0, 0.0)
    heads = heads_ref[HALO : HALO + SIDE, HALO : HALO + SIDE].reshape(512, 128)
    screen = screen.astype(jnp.bfloat16)
    sums = lax.dot_general(
        jnp.concatenate([screen] * 3, axis=1), jnp.concatenate(thirds(heads), axis=1),
        (((1,), (1,)), ((), ())), preferred_element_type=F32,
    )
    at = iota((2 * OWN, 512), 1)
    keep = ((at >> 3).astype(F32) == column2) & (
        ((at >> 2) & 1) == iota((2 * OWN, 512), 0) // OWN
    )
    sums = jnp.where(keep, sums, 0.0)
    pick = jnp.where((iota((512, 128), 0) & 3) == iota((512, 128), 1), 1.0, 0.0)
    pick = pick.astype(jnp.bfloat16)
    sums = sum(jnp.dot(part, pick, preferred_element_type=F32) for part in thirds(sums))
    sums = (sums[:OWN] + sums[OWN:]) * (1.0 / SCREEN)
    lane = iota((OWN, 128), 1)
    for t in range(4):
        sums = jnp.where(lane == t, sums - observed[t], sums)
    sums = jnp.where(lane == 4, column, sums)
    sums = jnp.where(lane == 5, top, sums)
    eye = jnp.where(iota((8, 128), 0) == iota((8, 128), 1), 1.0, 0.0)
    turned = lax.dot_general(
        eye, sums, (((1,), (1,)), ((), ())), precision=HIGHEST, preferred_element_type=F32
    )
    message[...] = jnp.concatenate([turned, jnp.zeros((8, 128 - OWN), F32)], axis=1)
    total = jnp.broadcast_to(jnp.sum(turned * turned, axis=1, keepdims=True), (8, 128))
    squares[...] = jnp.where(iota((8, 128), 0) < 4, total, pltpu.roll(total, 4, 0))


def adjoint_source(messages, e_ref, r_ref, beta_ref, lhs):
    sub, lane = iota((8, 128), 0), iota((8, 128), 1)
    values = [jnp.zeros((8, 128), F32) for g in range(GROUPS)]
    cells = [jnp.zeros((8, 128), F32) for g in range(GROUPS)]
    tops = [jnp.zeros((8, 128), F32) for g in range(GROUPS)]
    for k, (dx, dy) in enumerate(DIRECTIONS):
        tile = messages[k]
        value = jnp.where(sub < 4, tile, pltpu.roll(tile, 4, 0))
        column = jnp.broadcast_to(tile[4:5], (8, 128))
        along = jnp.floor(column * (1.0 / SIDE))
        x = along + (HALO + SIDE * dx)
        y = column - along * SIDE + (HALO + SIDE * dy)
        ok = (x >= 1) & (x < EXT - 1) & (y >= 1) & (y < EXT - 1) & (lane < OWN)
        cell = jnp.where(ok, x * EXT + y, 0.0)
        top = jnp.where(lane < OWN, jnp.broadcast_to(tile[5:6], (8, 128)), 0.0)
        for p, part in enumerate(thirds(value)):
            g, shift = (3 * k + p) // 4, OWN * ((3 * k + p) % 4)
            moved = [part.astype(F32), cell, top]
            if shift:
                moved = [pltpu.roll(v, shift, 1) for v in moved]
            values[g], cells[g], tops[g] = values[g] + moved[0], cells[g] + moved[1], tops[g] + moved[2]
    z = iota((256, 128), 0).astype(F32)
    screens = []
    for g in range(GROUPS):
        top = jnp.broadcast_to(tops[g][0:1], (256, 128))
        screens.append(jnp.where((z >= top) & (z < top + SCREEN), 1.0, 0.0).astype(jnp.bfloat16))
    screen = jnp.concatenate(screens, axis=1)
    wide = EXT - 2
    shape = (wide, 8, 128)
    lo, hi = 1, EXT - 1

    def left(x):
        cell = (x * EXT + 1 + iota(shape, 0)).astype(F32)
        for g in range(GROUPS):
            lhs[x - 1, :, g * 128 : (g + 1) * 128] = (
                jnp.where(cells[g][None] == cell, values[g][None], 0.0)
                .reshape(wide * 8, 128)
                .astype(jnp.bfloat16)
            )

    rows(lo, hi, left, 7)
    group = 7
    for first in range(0, wide, group):
        block = lhs[first : first + group].reshape(group * wide * 8, GROUPS * 128)
        both = lax.dot_general(
            block, screen, (((1,), (1,)), ((), ())), preferred_element_type=F32
        )
        pair = both.reshape(group, wide, 8, 256)
        for i in range(group):
            source = jnp.where(iota(shape, 1) < 4, pair[i, :, :, :128], pair[i, :, :, 128:])
            x = first + i + 1
            beta_ref[x, lo:hi] = e_ref[x, lo:hi] * r_ref[x, lo:hi] * source


def head_steps(e_ref, heads_ref, steps_ref):
    lo, hi = HALO, HALO + SIDE

    def row(x):
        h, e = heads_ref[x, lo:hi], e_ref[x, lo:hi]
        for f, (step_x, step_y) in enumerate(FACES):
            at = (x + step_x, slice(lo + step_y, hi + step_y))
            steps_ref[f, x - HALO] = e * e_ref[at] * (h - heads_ref[at])
        for f, (e_n, h_n) in enumerate(zip(z_neighbours(e, 1.0), z_neighbours(h, 0.0))):
            steps_ref[4 + f, x - HALO] = e * e_n * (h - h_n)

    rows(lo, hi, row, 2)


def sensitivity(steps_ref, adjoint_ref, out_ref):
    lo, hi = HALO, HALO + SIDE

    def row(x):
        a = adjoint_ref[x, lo:hi]
        total = jnp.zeros_like(a)
        for f, (step_x, step_y) in enumerate(FACES):
            total = total + steps_ref[f, x - HALO] * (
                a - adjoint_ref[x + step_x, lo + step_y : hi + step_y]
            )
        for f, a_n in enumerate(z_neighbours(a, 0.0)):
            total = total + steps_ref[4 + f, x - HALO] * (a - a_n)
        out_ref[x - HALO] = total

    rows(lo, hi, row, 4)


def sum_tests(sum_ref, scale):
    def row(x):
        total = sum_ref[x] * scale[None]
        total = total + pltpu.roll(total, 7, 1)
        sum_ref[x] = total + pltpu.roll(total, 6, 1)

    rows(0, SIDE, row, 4)


def slabs(sum_ref, out):
    lane = iota((8, 128), 1)
    for half in range(2):
        planes = sum_ref[:, :, 4 * half, :]
        for q in range(4):
            for xq in range(2):
                packed = jnp.zeros((8, 128), F32)
                for xx in range(4):
                    plane = planes[4 * xq + xx]
                    shift = (32 * (xx - q)) % 128
                    if shift:
                        plane = pltpu.roll(plane, shift, 1)
                    packed = jnp.where((lane >> 5) == xx, plane, packed)
                out[4 * half + q, xq] = packed


def kernel(
    log_hbm, storage_hbm, recharge_hbm, owner_hbm, column_hbm, top_hbm, observed_hbm,
    pump_rate, pump_well, out,
    log_conductivity, storage, recharge, owner, column, top, observed, load_sems,
    packed, steps_ref, lhs, ext, e_ref, r_ref, alpha_ref, heads_ref, beta_ref, u_ref, adjoint_ref, sum_ref,
    message, squares, messages, near, partial, far, parts, slots,
    halo_send, halo_recv, msg_send, msg_recv, near_send, near_recv, far_send, far_recv,
    part_send, part_recv,
):
    pairs = (
        (log_hbm, log_conductivity), (storage_hbm, storage), (recharge_hbm, recharge),
        (owner_hbm, owner), (column_hbm, column), (top_hbm, top), (observed_hbm, observed),
    )
    loads = [
        pltpu.make_async_copy(there, here, load_sems.at[i]) for i, (there, here) in enumerate(pairs)
    ]
    for copy in loads:
        copy.start()
    me, bx, by = lax.axis_index("test"), lax.axis_index("bx"), lax.axis_index("by")
    turn, place = by // ROUND, lax.rem(by, ROUND)
    neighbours = [neighbour(dx, dy) for k, (dx, dy) in NEIGHBOURS]
    near_peers = [
        {
            "bx": lax.rem(bx + a, NX_BRICKS),
            "by": turn * ROUND + lax.rem(place + b, ROUND),
        }
        for a in range(NX_BRICKS) for b in range(ROUND) if a + b > 0
    ]
    far_peers = [
        {"by": lax.rem(by + c * ROUND, NY_BRICKS)} for c in range(1, NY_BRICKS // ROUND)
    ]
    test_peers = [lax.rem(me + d, TESTS_AXIS) for d in range(1, TESTS_AXIS)]
    for cx in (0, HALO + SIDE):
        for cy in (0, HALO + SIDE):
            ext[cx : cx + HALO, cy : cy + HALO] = jnp.zeros((HALO, HALO, 8, 128), F32)
    everyone = far_peers + neighbours + near_peers + [{"test": peer} for peer in test_peers]
    barrier = pltpu.get_barrier_semaphore()
    for peer in everyone:
        pl.semaphore_signal(barrier, inc=1, device_id=peer, device_id_type=MESH)
    for copy in loads[:3]:
        copy.wait()
    pack(log_conductivity, storage, recharge, packed)
    pl.semaphore_wait(barrier, len(everyone))
    middle_halo, near_halo, outer_halo = halo_copies(packed, ext, halo_send, halo_recv)
    ext[HALO : HALO + SIDE, HALO : HALO + SIDE] = packed[...]
    for copy in loads[3:]:
        copy.wait()
    pump_cell, pump_tile = pumping(pump_rate, pump_well, owner, column, top)
    wells = own_wells(owner, column, top, observed)
    fields = (ext, e_ref, r_ref, alpha_ref, beta_ref, pump_cell, pump_tile)
    middle_halo()
    roots(ext, e_ref, HALO, HALO + SIDE)
    terms(*fields, HALO + 1, HALO + SIDE - 1)
    near_halo()
    near_coefficients(fields)
    sweeps(e_ref, alpha_ref, beta_ref, u_ref, heads_ref, 3)
    residuals(heads_ref, wells, message, squares)
    near_copies = [
        remote(squares, near.at[i], near_send.at[i], near_recv.at[i], peer)
        for i, peer in enumerate(near_peers)
    ]
    copies = [
        remote(message, messages.at[8 - k], msg_send.at[k], msg_recv.at[k], neighbour(dx, dy))
        for k, (dx, dy) in NEIGHBOURS
    ]
    messages[4] = message[...]
    outer_halo()
    roots(ext, e_ref, 0, HALO)
    roots(ext, e_ref, HALO + SIDE, EXT)
    edge_roots(ext, e_ref)
    terms(*fields, 1, HALO + 1)
    terms(*fields, HALO + SIDE - 1, EXT - 1)
    for copy in near_copies:
        copy.wait()
    here = squares[...]
    for i in range(len(near_peers)):
        here = here + near[i]
    partial[...] = here
    far_copies = [
        remote(partial, far.at[i], far_send.at[i], far_recv.at[i], peer)
        for i, peer in enumerate(far_peers)
    ]
    sweeps(e_ref, alpha_ref, beta_ref, u_ref, heads_ref, 2)
    head_steps(e_ref, heads_ref, steps_ref)
    for copy in copies:
        copy.wait()
    adjoint_source(messages, e_ref, r_ref, beta_ref, lhs)
    sweeps(e_ref, alpha_ref, beta_ref, u_ref, adjoint_ref, 2)
    sensitivity(steps_ref, adjoint_ref, sum_ref)
    for copy in far_copies:
        copy.wait()
    total = partial[...]
    for i in range(len(far_peers)):
        total = total + far[i]
    scale = 1.0 / (total / WELLS + EPSILON)
    sum_tests(sum_ref, scale)
    slabs(sum_ref, parts)
    part_copies = [
        remote(parts.at[peer], slots.at[i], part_send.at[i], part_recv.at[i], {"test": peer})
        for i, peer in enumerate(test_peers)
    ]
    for copy in part_copies:
        copy.wait()
    total = parts[me]
    for i in range(TESTS_AXIS - 1):
        total = total + slots[i]
    for xq in range(2):
        for xx in range(4):
            plane = total[xq]
            if xx:
                plane = pltpu.roll(plane, 128 - 32 * xx, 1)
            out[4 * xq + xx] = plane[:, :32]


def local(
    log_conductivity, storage, recharge, pump_rate, pump_well, observed, owner, screen_column, screen_top
):
    dma = pltpu.SemaphoreType.DMA
    field = (EXT, EXT, 8, 128)
    tile = (8, 128)
    table = [a.reshape(16, 128) for a in (owner, screen_column, screen_top)]
    near, far = NX_BRICKS * ROUND - 1, NY_BRICKS // ROUND - 1
    scratch = [field] * 8 + [
        (SIDE, SIDE) + tile, tile, tile, (9,) + tile,
        (near,) + tile, tile, (far,) + tile, (TESTS_AXIS, 2) + tile, (TESTS_AXIS - 1, 2) + tile,
    ]
    counts = (24, 24, 9, 9, near, near, far, far, TESTS_AXIS - 1, TESTS_AXIS - 1)
    total = pl.pallas_call(
        kernel,
        out_shape=jax.ShapeDtypeStruct((SIDE, SIDE, 32), F32),
        in_specs=[pl.BlockSpec(memory_space=pltpu.HBM)] * 7
        + [pl.BlockSpec(memory_space=VMEM)] * 2,
        out_specs=pl.BlockSpec(memory_space=VMEM),
        scratch_shapes=[VMEM((SIDE, SIDE, 256), F32)] * 3
        + [VMEM((16, 128), jnp.int32)] * 3
        + [VMEM((4, WELLS), F32), dma((7,))]
        + [
            VMEM((SIDE, SIDE) + tile, F32),
            VMEM((6, SIDE, SIDE) + tile, F32),
            VMEM((EXT - 2, (EXT - 2) * 8, GROUPS * 128), jnp.bfloat16),
        ]
        + [VMEM(s, F32) for s in scratch] + [dma((n,)) for n in counts],
        compiler_params=pltpu.CompilerParams(
            vmem_limit_bytes=67_043_328, collective_id=0, has_side_effects=True
        ),
    )(
        log_conductivity, storage, recharge, *table, observed,
        pump_rate.reshape(1, 4), pump_well.reshape(1, 4),
    )
    return total * (-0.5 / (4 * TESTS_AXIS))


def solution(mesh):
    placed = (
        P("bx", "by", None), P("bx", "by", None), P("bx", "by", None), P("test"), P("test"),
        P("test", None), P(), P(), P(),
    )
    return jax.shard_map(
        local, mesh=mesh, in_specs=placed, out_specs=P("bx", "by", "test"), check_vma=False
    )
```
